32 devices in a mesh: dp: 16 (over z, y, x), fsdp: 2 (over core).
Axes of the slice: x: 2, y: 2, z: 4, core: 2. Of those that a mesh axis runs over, the one named last changes fastest.
Arguments:
- block_input: float32 [2, 2048, 768], P(None, ('dp', 'fsdp')), may hold values from -6 to 6
- out_grad: float32 [2, 2048, 768], P(None, ('dp', 'fsdp')), may hold values from -6 to 6
- seg_ids: int32 [2, 2048], P(None, ('dp', 'fsdp')), may hold values from -1 to 7, as said below
- params: float32 [7087872], P(('dp', 'fsdp')), as said below
- first_moment: float32 [7087872], P(('dp', 'fsdp')), may hold values from -6 to 6
- second_moment: float32 [7087872], P(('dp', 'fsdp')), may hold values from 1 to 10
Outputs:
- block_output: float32 [2, 2048, 768], P(None, ('dp', 'fsdp'))
- input_grad: float32 [2, 2048, 768], P(None, ('dp', 'fsdp'))
- param_grad: float32 [7087872], P(('dp', 'fsdp'))
- new_params: float32 [7087872], P(('dp', 'fsdp'))
- new_first: float32 [7087872], P(('dp', 'fsdp'))
- new_second: float32 [7087872], P(('dp', 'fsdp'))
The draws below stay inside these ranges and needn't reach their ends.
Inputs may be any that keep to these rules, and one draw needn't show every extreme that they name: `seg_ids`: in each block of 64 slots, ids count the sequences 0, 1, 2, ... in order from the block's first slot, each sequence contiguous, at most 8 sequences a block; the block ends in padding with id -1, at least one slot of it; blocks differ in how much is padding. `params`: laid out as the steps read it.
All inputs are finite; a program needn't handle non-finite values.
Results may differ from the reference program's by a relative error of at most 0.012.
Values may be sent and summed in bfloat16 or wider, within the bound.
No kernel may reach another device: no remote copies, remote signals or barrier semaphores. Data moves between devices by JAX's collectives and lax.ppermute only.
A program may use at most 256 MiB of HBM per device.

```python
import math
import jax
import jax.numpy as jnp
from jax import lax

D = 768
FF = 3072
HEADS = 12
HEAD_DIM = 64
ROT = 16
ROWS = 64
MICRO = 2
STEP = 3
TOKENS_MB = 2048
PARAMS = 7087872


def draw_seg_ids(key, part):
    block_total = MICRO * (TOKENS_MB // ROWS)
    key_len, key_start = jax.random.split(key)
    block_idx = jnp.arange(block_total)[:, None]
    row_idx = jnp.arange(ROWS)[None, :]
    valid_len = jax.random.randint(key_len, (block_total, 1), ROWS // 4, ROWS)
    valid_len = jnp.where(block_idx == 0, ROWS - 1, valid_len)
    starts = jnp.where(jax.random.randint(key_start, (block_total, ROWS), 0, 16) == 0, 1, 0)
    starts = jnp.where(row_idx == 0, 1, starts)
    starts = jnp.where((block_idx == 0) & (row_idx % 8 == 0), 1, starts)
    seg_rows = jnp.minimum(jnp.cumsum(starts, axis=1) - 1, ROWS // 8 - 1)
    seg_rows = jnp.where(row_idx < valid_len, seg_rows, -1)
    return seg_rows.reshape(MICRO, TOKENS_MB).astype(jnp.int32)


def draw_params(key, part):
    key_list = jax.random.split(key, 12)

    def noise(sub_key, item_shape, scale):
        return jax.random.normal(sub_key, item_shape, jnp.float32) * scale
    w_qkv = noise(key_list[0], (D, 3 * D), D ** (-0.5))
    b_qkv = noise(key_list[4], (3 * D,), 0.5)
    w_out = noise(key_list[1], (D, D), 4.0 * D ** (-0.5))
    w_up = noise(key_list[2], (D, FF), D ** (-0.5))
    w_down = noise(key_list[3], (FF, D), 2.0 * FF ** (-0.5))
    b_out = noise(key_list[5], (D,), 0.3)
    b_up = noise(key_list[6], (FF,), 0.5)
    b_down = noise(key_list[7], (D,), 0.3)
    gain_one = jax.random.uniform(key_list[8], (D,), jnp.float32, 0.5, 1.5)
    shift_one = noise(key_list[9], (D,), 0.3)
    gain_two = jax.random.uniform(key_list[10], (D,), jnp.float32, 0.5, 1.5)
    shift_two = noise(key_list[11], (D,), 0.3)
    pieces_in = [w_qkv, w_out, w_up, w_down, b_qkv, b_out, b_up, b_down, gain_one, shift_one, gain_two, shift_two]
    return jnp.concatenate([piece_item.reshape(-1) for piece_item in pieces_in]).astype(jnp.float32)


def steps_of(rng, shape, shards, low, high):
    loudness, own = 1.0, jax.random.fold_in(rng, 6)
    for axis_at, blocks in shards:
        heights = jnp.exp(jax.random.uniform(jax.random.fold_in(own, axis_at), (blocks,), jnp.float32, low / len(shards), high / len(shards)))
        loudness = loudness * jnp.repeat(heights, shape[axis_at] // blocks).reshape([-1 if axis == axis_at else 1 for axis in range(len(shape))])
    return loudness


def gaussian(stream_key, dims, spread, reach, shards=(), held_as=jnp.bfloat16):
    values = jax.random.normal(stream_key, dims, jnp.float32) * spread
    if len(shards) > 0:
        values = steps_of(stream_key, dims, shards, -0.22, 0.18) * values
    return jnp.clip(values, min=-reach, max=reach).astype(held_as)


def setup_inputs(seed: int = 0) -> dict:
    key_of = jax.random.split(jax.random.key(seed), 7)
    block_input = gaussian(key_of[0], (MICRO, TOKENS_MB, D), 1.0, 6.0, ((1, 32),), jnp.float32)
    out_grad = gaussian(key_of[1], (MICRO, TOKENS_MB, D), 1.0, 6.0, ((1, 32),), jnp.float32)
    seg_ids = draw_seg_ids(jax.random.fold_in(key_of[6], 71), 0)
    params = draw_params(jax.random.fold_in(key_of[6], 71), 0)
    first_moment = gaussian(key_of[4], (PARAMS,), 1.0, 6.0, ((0, 32),), jnp.float32)
    second_moment = jnp.clip(jnp.exp(math.log(10.0) - 2.3025851 * jax.random.uniform(key_of[5], (PARAMS,), jnp.float32) ** steps_of(key_of[5], (PARAMS,), ((0, 32),), -0.2, 0.2)), 1.0, 10.0)
    return dict(block_input=block_input, out_grad=out_grad, seg_ids=seg_ids, params=params, first_moment=first_moment, second_moment=second_moment)


NORM_EPS = 1e-05
BETA_ONE = 0.9
BETA_TWO = 0.95
LEARN_RATE = 0.05
WEIGHT_DECAY = 0.1
ADAM_EPS = 1e-08

def layout_shapes():
    return [(D, 3 * D), (D, D), (D, FF), (FF, D), (3 * D,), (D,), (FF,), (D,), (D,), (D,), (D,), (D,)]

def unpack_flat(flat_vec):
    pieces_out = []
    offset = 0
    for item_shape in layout_shapes():
        length = math.prod(item_shape)
        pieces_out.append(flat_vec[offset:offset + length].reshape(item_shape))
        offset += length
    return pieces_out

def product(form, left, right):
    return jnp.einsum(form, left.astype(jnp.float32), right.astype(jnp.float32))

def block_tables(seg_rows):
    row_count = seg_rows.shape[1]
    row_idx = jnp.arange(row_count)
    same_seq = seg_rows[:, :, None] == seg_rows[:, None, :]
    earlier = row_idx[None, :] < row_idx[:, None]
    diagonal = row_idx[None, :] == row_idx[:, None]
    causal = row_idx[None, :] <= row_idx[:, None]
    allowed = same_seq & causal[None] & ((seg_rows[:, :, None] >= 0) | diagonal[None])
    position = lax.optimization_barrier(jnp.sum(jnp.where(same_seq & earlier[None], 1, 0), axis=2)).astype(jnp.float32)
    inv_freq = 10000.0 ** (-(jnp.arange(ROT // 2, dtype=jnp.float32) * 2.0) / ROT)
    angles = position[:, :, None] * inv_freq[None, None, :]
    return (allowed, jnp.cos(angles)[:, :, None, :], jnp.sin(angles)[:, :, None, :])

def rotate(vecs, cos_t, sin_t):
    half_rot = ROT // 2
    first = vecs[..., :half_rot]
    second = vecs[..., half_rot:ROT]
    return jnp.concatenate([first * cos_t - second * sin_t, second * cos_t + first * sin_t, vecs[..., ROT:]], axis=-1)

def unrotate(vecs, cos_t, sin_t):
    half_rot = ROT // 2
    first = vecs[..., :half_rot]
    second = vecs[..., half_rot:ROT]
    return jnp.concatenate([first * cos_t + second * sin_t, second * cos_t - first * sin_t, vecs[..., ROT:]], axis=-1)

def layer_norm(flat_x, gain, shift):
    row_mean = lax.optimization_barrier(jnp.mean(flat_x, axis=-1, keepdims=True))
    centred = flat_x - row_mean
    row_var = lax.optimization_barrier(jnp.mean(centred * centred, axis=-1, keepdims=True))
    inv_std = lax.rsqrt(row_var + NORM_EPS)
    normed = centred * inv_std
    return (normed, inv_std, (normed * gain.astype(jnp.float32) + shift.astype(jnp.float32)).astype(jnp.bfloat16))

def norm_back(grad_act, normed, inv_std, gain):
    grad_gain = lax.optimization_barrier(jnp.sum(grad_act * normed, axis=0))
    grad_shift = lax.optimization_barrier(jnp.sum(grad_act, axis=0))
    scaled = grad_act * gain.astype(jnp.float32)
    grad_in = inv_std * (scaled - lax.optimization_barrier(jnp.mean(scaled, axis=-1, keepdims=True)) - normed * lax.optimization_barrier(jnp.mean(scaled * normed, axis=-1, keepdims=True)))
    return (grad_gain, grad_shift, grad_in)

def softmax_rows(query_bf, key_bf, allowed, log_total):
    scores = product('gqhd,gkhd->ghqk', query_bf, key_bf) * HEAD_DIM ** (-0.5)
    mask_b = allowed[:, None]
    masked = jnp.where(mask_b, scores, -jnp.inf)
    if log_total is None:
        top_score = lax.optimization_barrier(jnp.max(masked, axis=-1, keepdims=True))
        expo = jnp.where(mask_b, jnp.exp(masked - top_score), 0.0)
        log_total = top_score + jnp.log(lax.optimization_barrier(jnp.sum(expo, axis=-1, keepdims=True)))
    prob_rows = jnp.where(mask_b, jnp.exp(masked - log_total), 0.0)
    return (prob_rows, log_total)

def forward(x_rows, seg_rows, weights):
    w_qkv, w_out, w_up, w_down, b_qkv, b_out, b_up, b_down, gain_one, shift_one, gain_two, shift_two = weights
    group_count, row_count = seg_rows.shape
    allowed, cos_t, sin_t = block_tables(seg_rows)
    flat_x = x_rows.reshape(group_count * row_count, D)
    normed_one, inv_one, act_one = layer_norm(flat_x, gain_one, shift_one)
    normed_two, inv_two, act_two = layer_norm(flat_x, gain_two, shift_two)
    qkv_rows = jnp.dot(act_one, w_qkv, preferred_element_type=jnp.float32) + b_qkv.astype(jnp.float32)
    qkv_rows = qkv_rows.reshape(group_count, row_count, 3, HEADS, HEAD_DIM)
    query_bf = rotate(qkv_rows[:, :, 0], cos_t, sin_t).astype(jnp.bfloat16)
    key_bf = rotate(qkv_rows[:, :, 1], cos_t, sin_t).astype(jnp.bfloat16)
    value_bf = qkv_rows[:, :, 2].astype(jnp.bfloat16)
    prob_rows, log_total = softmax_rows(query_bf, key_bf, allowed, None)
    prob_bf = prob_rows.astype(jnp.bfloat16)
    attn_bf = product('ghqk,gkhd->gqhd', prob_bf, value_bf).astype(jnp.bfloat16).reshape(group_count * row_count, D)
    attn_out = jnp.dot(attn_bf, w_out, preferred_element_type=jnp.float32) + b_out.astype(jnp.float32)
    up_rows = jnp.dot(act_two, w_up, preferred_element_type=jnp.float32) + b_up.astype(jnp.float32)
    hidden_bf = jax.nn.gelu(up_rows, approximate=False).astype(jnp.bfloat16)
    mlp_out = jnp.dot(hidden_bf, w_down, preferred_element_type=jnp.float32) + b_down.astype(jnp.float32)
    result = flat_x + attn_out + mlp_out
    kept_state = (normed_one, inv_one, act_one, normed_two, inv_two, act_two, query_bf, key_bf, value_bf, log_total, attn_bf, up_rows, hidden_bf, allowed, cos_t, sin_t, seg_rows)
    return (result.reshape(group_count, row_count, D), kept_state)

def backward(kept_state, grad_rows, weights):
    w_qkv, w_out, w_up, w_down, b_qkv, b_out, b_up, b_down, gain_one, shift_one, gain_two, shift_two = weights
    normed_one, inv_one, act_one, normed_two, inv_two, act_two, query_bf, key_bf, value_bf, log_total, attn_bf, up_rows, hidden_bf, allowed, cos_t, sin_t, seg_rows = kept_state
    group_count, row_count = seg_rows.shape
    valid = (seg_rows >= 0).astype(jnp.float32).reshape(group_count * row_count, 1)
    grad_y = grad_rows.reshape(group_count * row_count, D) * valid
    grad_y_bf = grad_y.astype(jnp.bfloat16)
    grad_bias = lax.optimization_barrier(jnp.sum(grad_y, axis=0))
    grad_w_down = jnp.dot(hidden_bf.T, grad_y_bf, preferred_element_type=jnp.float32)
    grad_w_out = jnp.dot(attn_bf.T, grad_y_bf, preferred_element_type=jnp.float32)
    grad_hidden = jnp.dot(grad_y_bf, w_down.T, preferred_element_type=jnp.float32)
    cdf_part = 0.5 * (1.0 + jax.scipy.special.erf(up_rows * 0.7071067811865476))
    pdf_part = jnp.exp(-0.5 * up_rows * up_rows) * 0.3989422804014327
    grad_up = grad_hidden * (cdf_part + up_rows * pdf_part)
    grad_b_up = lax.optimization_barrier(jnp.sum(grad_up, axis=0))
    grad_up_bf = grad_up.astype(jnp.bfloat16)
    grad_w_up = jnp.dot(act_two.T, grad_up_bf, preferred_element_type=jnp.float32)
    grad_act_two = jnp.dot(grad_up_bf, w_up.T, preferred_element_type=jnp.float32)
    grad_attn = jnp.dot(grad_y_bf, w_out.T, preferred_element_type=jnp.float32).astype(jnp.bfloat16)
    grad_attn = grad_attn.reshape(group_count, row_count, HEADS, HEAD_DIM)
    prob_rows, unused_total = softmax_rows(query_bf, key_bf, allowed, log_total)
    prob_bf = prob_rows.astype(jnp.bfloat16)
    grad_value = product('ghqk,gqhd->gkhd', prob_bf, grad_attn)
    grad_prob = product('gqhd,gkhd->ghqk', grad_attn, value_bf)
    delta_rows = lax.optimization_barrier(jnp.sum(prob_rows * grad_prob, axis=-1, keepdims=True))
    grad_score_bf = (prob_rows * (grad_prob - delta_rows) * HEAD_DIM ** (-0.5)).astype(jnp.bfloat16)
    grad_query = unrotate(product('ghqk,gkhd->gqhd', grad_score_bf, key_bf), cos_t, sin_t)
    grad_key = unrotate(product('ghqk,gqhd->gkhd', grad_score_bf, query_bf), cos_t, sin_t)
    grad_qkv = jnp.stack([grad_query, grad_key, grad_value], axis=2).reshape(group_count * row_count, 3 * D)
    grad_b_qkv = lax.optimization_barrier(jnp.sum(grad_qkv, axis=0))
    grad_qkv_bf = grad_qkv.astype(jnp.bfloat16)
    grad_w_qkv = jnp.dot(act_one.T, grad_qkv_bf, preferred_element_type=jnp.float32)
    grad_act_one = jnp.dot(grad_qkv_bf, w_qkv.T, preferred_element_type=jnp.float32)
    grad_gain_one, grad_shift_one, back_one = norm_back(grad_act_one, normed_one, inv_one, gain_one)
    grad_gain_two, grad_shift_two, back_two = norm_back(grad_act_two, normed_two, inv_two, gain_two)
    input_grad = (grad_y + back_one + back_two).reshape(group_count, row_count, D)
    grads = (grad_w_qkv, grad_w_out, grad_w_up, grad_w_down, grad_b_qkv, grad_bias, grad_b_up, grad_bias, grad_gain_one, grad_shift_one, grad_gain_two, grad_shift_two)
    return (input_grad, grads)

def adam_update(params, grads, first_moment, second_moment):
    new_first = BETA_ONE * first_moment + (1.0 - BETA_ONE) * grads
    new_second = BETA_TWO * second_moment + (1.0 - BETA_TWO) * grads * grads
    first_hat = new_first / (1.0 - BETA_ONE ** STEP)
    second_hat = new_second / (1.0 - BETA_TWO ** STEP)
    new_params = params - LEARN_RATE * (first_hat / (jnp.sqrt(second_hat) + ADAM_EPS) + WEIGHT_DECAY * params)
    return (new_params, new_first, new_second)

def reference(block_input, out_grad, seg_ids, params, first_moment, second_moment):
    weights = unpack_flat(params.astype(jnp.bfloat16))
    block_total = MICRO * (block_input.shape[1] // ROWS)
    group_size = math.gcd(block_total, max(1, 4096 // ROWS))
    scan_len = block_total // group_size
    x_all = block_input.reshape(scan_len, group_size, ROWS, D)
    grad_all = out_grad.reshape(scan_len, group_size, ROWS, D)
    seg_all = seg_ids.reshape(scan_len, group_size, ROWS)

    def step_fn(carry, item):
        x_rows, grad_rows, seg_rows = item
        result, kept_state = forward(x_rows, seg_rows, weights)
        back_x, grads = backward(kept_state, grad_rows, weights)
        return (tuple((acc + part for acc, part in zip(carry, grads))), (result, back_x))
    init = tuple((jnp.zeros(item_shape, jnp.float32) for item_shape in layout_shapes()))
    totals, (results, back_all) = lax.scan(step_fn, init, (x_all, grad_all, seg_all))
    param_grad = jnp.concatenate([part.reshape(-1) for part in totals])
    new_params, new_first, new_second = adam_update(params, param_grad, first_moment, second_moment)
    block_output = results.reshape(MICRO, block_input.shape[1], D)
    input_grad = back_all.reshape(MICRO, block_input.shape[1], D)
    return (block_output, input_grad, param_grad, new_params, new_first, new_second)
```

```python
import functools
import math

import jax
import jax.numpy as jnp
from jax import lax
from jax.sharding import PartitionSpec as P

D = 768
FF = 3072
HEADS = 12
HEAD_DIM = 64
ROT = 16
STEP = 3


NORM_EPS = 1e-05
BETA_ONE = 0.9
BETA_TWO = 0.95
LEARN_RATE = 0.05
WEIGHT_DECAY = 0.1
ADAM_EPS = 1e-08


def layout_shapes():
    return [
        (D, 3 * D),
        (D, D),
        (D, FF),
        (FF, D),
        (3 * D,),
        (D,),
        (FF,),
        (D,),
        (D,),
        (D,),
        (D,),
        (D,),
    ]


def unpack_flat(flat_vec):
    pieces_out = []
    offset = 0
    for item_shape in layout_shapes():
        length = math.prod(item_shape)
        pieces_out.append(flat_vec[offset : offset + length].reshape(item_shape))
        offset += length
    return pieces_out


def product(form, left, right):
    return jnp.einsum(form, left, right, preferred_element_type=jnp.float32)


def block_tables(seg_rows):
    row_count = seg_rows.shape[1]
    row_idx = jnp.arange(row_count)
    same_seq = seg_rows[:, :, None] == seg_rows[:, None, :]
    earlier = row_idx[None, :] < row_idx[:, None]
    diagonal = row_idx[None, :] == row_idx[:, None]
    causal = row_idx[None, :] <= row_idx[:, None]
    allowed = same_seq & causal[None] & ((seg_rows[:, :, None] >= 0) | diagonal[None])
    position = jnp.sum(jnp.where(same_seq & earlier[None], 1, 0), axis=2).astype(jnp.float32)
    inv_freq = 10000.0 ** (-(jnp.arange(ROT // 2, dtype=jnp.float32) * 2.0) / ROT)
    angles = position[:, :, None] * inv_freq[None, None, :]
    return (allowed, jnp.cos(angles)[:, :, None, :], jnp.sin(angles)[:, :, None, :])


def rotate(vecs, cos_t, sin_t):
    half_rot = ROT // 2
    first = vecs[..., :half_rot]
    second = vecs[..., half_rot:ROT]
    return jnp.concatenate(
        [first * cos_t - second * sin_t, second * cos_t + first * sin_t, vecs[..., ROT:]], axis=-1
    )


def unrotate(vecs, cos_t, sin_t):
    half_rot = ROT // 2
    first = vecs[..., :half_rot]
    second = vecs[..., half_rot:ROT]
    return jnp.concatenate(
        [first * cos_t + second * sin_t, second * cos_t - first * sin_t, vecs[..., ROT:]], axis=-1
    )


def layer_norm(flat_x, gain, shift):
    row_mean = jnp.mean(flat_x, axis=-1, keepdims=True)
    centred = flat_x - row_mean
    row_var = jnp.mean(centred * centred, axis=-1, keepdims=True)
    inv_std = lax.rsqrt(row_var + NORM_EPS)
    normed = centred * inv_std
    return (
        normed,
        inv_std,
        (normed * gain.astype(jnp.float32) + shift.astype(jnp.float32)).astype(jnp.bfloat16),
    )


def norm_back(grad_act, normed, inv_std, gain):
    grad_gain = jnp.sum(grad_act * normed, axis=0)
    grad_shift = jnp.sum(grad_act, axis=0)
    scaled = grad_act * gain.astype(jnp.float32)
    grad_in = inv_std * (
        scaled
        - jnp.mean(scaled, axis=-1, keepdims=True)
        - normed * jnp.mean(scaled * normed, axis=-1, keepdims=True)
    )
    return (grad_gain, grad_shift, grad_in)


def softmax_rows(query_bf, key_bf, allowed, log_total):
    scores = product("gqhd,gkhd->ghqk", query_bf, key_bf) * HEAD_DIM ** (-0.5)
    mask_b = allowed[:, None]
    masked = jnp.where(mask_b, scores, -jnp.inf)
    if log_total is None:
        top_score = jnp.max(masked, axis=-1, keepdims=True)
        expo = jnp.where(mask_b, jnp.exp(masked - top_score), 0.0)
        log_total = top_score + jnp.log(jnp.sum(expo, axis=-1, keepdims=True))
    prob_rows = jnp.where(mask_b, jnp.exp(masked - log_total), 0.0)
    return (prob_rows, log_total)


def forward(x_rows, seg_rows, weights):
    (
        w_qkv,
        w_out,
        w_up,
        w_down,
        b_qkv,
        b_out,
        b_up,
        b_down,
        gain_one,
        shift_one,
        gain_two,
        shift_two,
    ) = weights
    group_count, row_count = seg_rows.shape
    allowed, cos_t, sin_t = block_tables(seg_rows)
    flat_x = x_rows.reshape(group_count * row_count, D)
    normed_one, inv_one, act_one = layer_norm(flat_x, gain_one, shift_one)
    normed_two, inv_two, act_two = layer_norm(flat_x, gain_two, shift_two)
    qkv_rows = jnp.dot(act_one, w_qkv, preferred_element_type=jnp.float32) + b_qkv.astype(
        jnp.float32
    )
    qkv_rows = qkv_rows.reshape(group_count, row_count, 3, HEADS, HEAD_DIM)
    query_bf = rotate(qkv_rows[:, :, 0], cos_t, sin_t).astype(jnp.bfloat16)
    key_bf = rotate(qkv_rows[:, :, 1], cos_t, sin_t).astype(jnp.bfloat16)
    value_bf = qkv_rows[:, :, 2].astype(jnp.bfloat16)
    prob_rows, log_total = softmax_rows(query_bf, key_bf, allowed, None)
    prob_bf = prob_rows.astype(jnp.bfloat16)
    attn_bf = (
        product("ghqk,gkhd->gqhd", prob_bf, value_bf)
        .astype(jnp.bfloat16)
        .reshape(group_count * row_count, D)
    )
    attn_out = jnp.dot(attn_bf, w_out, preferred_element_type=jnp.float32) + b_out.astype(
        jnp.float32
    )
    up_rows = jnp.dot(act_two, w_up, preferred_element_type=jnp.float32) + b_up.astype(jnp.float32)
    hidden_bf = jax.nn.gelu(up_rows, approximate=False).astype(jnp.bfloat16)
    mlp_out = jnp.dot(hidden_bf, w_down, preferred_element_type=jnp.float32) + b_down.astype(
        jnp.float32
    )
    result = flat_x + attn_out + mlp_out
    kept_state = (
        normed_one,
        inv_one,
        act_one,
        normed_two,
        inv_two,
        act_two,
        query_bf,
        key_bf,
        value_bf,
        log_total,
        attn_bf,
        up_rows,
        hidden_bf,
        allowed,
        cos_t,
        sin_t,
        seg_rows,
    )
    return (result.reshape(group_count, row_count, D), kept_state)


def backward(kept_state, grad_rows, weights):
    (
        w_qkv,
        w_out,
        w_up,
        w_down,
        b_qkv,
        b_out,
        b_up,
        b_down,
        gain_one,
        shift_one,
        gain_two,
        shift_two,
    ) = weights
    (
        normed_one,
        inv_one,
        act_one,
        normed_two,
        inv_two,
        act_two,
        query_bf,
        key_bf,
        value_bf,
        log_total,
        attn_bf,
        up_rows,
        hidden_bf,
        allowed,
        cos_t,
        sin_t,
        seg_rows,
    ) = kept_state
    group_count, row_count = seg_rows.shape
    valid = (seg_rows >= 0).astype(jnp.float32).reshape(group_count * row_count, 1)
    grad_y = grad_rows.reshape(group_count * row_count, D) * valid
    grad_y_bf = grad_y.astype(jnp.bfloat16)
    grad_bias = jnp.sum(grad_y, axis=0)
    grad_w_down = jnp.dot(hidden_bf.T, grad_y_bf, preferred_element_type=jnp.float32)
    grad_w_out = jnp.dot(attn_bf.T, grad_y_bf, preferred_element_type=jnp.float32)
    grad_hidden = jnp.dot(grad_y_bf, w_down.T, preferred_element_type=jnp.float32)
    cdf_part = 0.5 * (1.0 + jax.scipy.special.erf(up_rows * 0.7071067811865476))
    pdf_part = jnp.exp(-0.5 * up_rows * up_rows) * 0.3989422804014327
    grad_up = grad_hidden * (cdf_part + up_rows * pdf_part)
    grad_b_up = jnp.sum(grad_up, axis=0)
    grad_up_bf = grad_up.astype(jnp.bfloat16)
    grad_w_up = jnp.dot(act_two.T, grad_up_bf, preferred_element_type=jnp.float32)
    grad_act_two = jnp.dot(grad_up_bf, w_up.T, preferred_element_type=jnp.float32)
    grad_attn = jnp.dot(grad_y_bf, w_out.T, preferred_element_type=jnp.float32).astype(jnp.bfloat16)
    grad_attn = grad_attn.reshape(group_count, row_count, HEADS, HEAD_DIM)
    prob_rows, unused_total = softmax_rows(query_bf, key_bf, allowed, log_total)
    prob_bf = prob_rows.astype(jnp.bfloat16)
    grad_value = product("ghqk,gqhd->gkhd", prob_bf, grad_attn)
    grad_prob = product("gqhd,gkhd->ghqk", grad_attn, value_bf)
    delta_rows = jnp.sum(prob_rows * grad_prob, axis=-1, keepdims=True)
    grad_score_bf = (prob_rows * (grad_prob - delta_rows) * HEAD_DIM ** (-0.5)).astype(jnp.bfloat16)
    grad_query = unrotate(product("ghqk,gkhd->gqhd", grad_score_bf, key_bf), cos_t, sin_t)
    grad_key = unrotate(product("ghqk,gqhd->gkhd", grad_score_bf, query_bf), cos_t, sin_t)
    grad_qkv = jnp.stack([grad_query, grad_key, grad_value], axis=2).reshape(
        group_count * row_count, 3 * D
    )
    grad_b_qkv = jnp.sum(grad_qkv, axis=0)
    grad_qkv_bf = grad_qkv.astype(jnp.bfloat16)
    grad_w_qkv = jnp.dot(act_one.T, grad_qkv_bf, preferred_element_type=jnp.float32)
    grad_act_one = jnp.dot(grad_qkv_bf, w_qkv.T, preferred_element_type=jnp.float32)
    grad_gain_one, grad_shift_one, back_one = norm_back(grad_act_one, normed_one, inv_one, gain_one)
    grad_gain_two, grad_shift_two, back_two = norm_back(grad_act_two, normed_two, inv_two, gain_two)
    input_grad = (grad_y + back_one + back_two).reshape(group_count, row_count, D)
    grads = (
        grad_w_qkv,
        grad_w_out,
        grad_w_up,
        grad_w_down,
        grad_b_qkv,
        grad_bias,
        grad_b_up,
        grad_bias,
        grad_gain_one,
        grad_shift_one,
        grad_gain_two,
        grad_shift_two,
    )
    return (input_grad, grads)


def adam_update(params, grads, first_moment, second_moment):
    new_first = BETA_ONE * first_moment + (1.0 - BETA_ONE) * grads
    new_second = BETA_TWO * second_moment + (1.0 - BETA_TWO) * grads * grads
    first_hat = new_first / (1.0 - BETA_ONE**STEP)
    second_hat = new_second / (1.0 - BETA_TWO**STEP)
    new_params = params - LEARN_RATE * (
        first_hat / (jnp.sqrt(second_hat) + ADAM_EPS) + WEIGHT_DECAY * params
    )
    return (new_params, new_first, new_second)


AXES = ("dp", "fsdp")
MATRIX_ROWS = 9 * D + 3 * D
TAIL = 13 * D


def rows_from_flat(flat, spread, count):
    me = lax.axis_index(AXES)
    tail = flat[flat.shape[0] - TAIL :]
    before = lax.ppermute(tail, AXES, [(i, (i + 1) % count) for i in range(count)])
    joined = jnp.concatenate([before, flat])
    rows = lax.dynamic_slice(joined, (TAIL - spread * me,), (flat.shape[0] - spread,))
    return rows.reshape(-1, D), tail.reshape(-1, D)


def flat_from_rows(rows, tail, spread, count):
    me = lax.axis_index(AXES)
    head = rows.reshape(-1)[:TAIL]
    after = lax.ppermute(head, AXES, [(i, (i - 1) % count) for i in range(count)])
    after = jnp.where(me == count - 1, tail.reshape(-1), after)
    joined = jnp.concatenate([rows.reshape(-1), after])
    return lax.dynamic_slice(joined, (spread * me,), (rows.size + spread,))


def body(count, block_input, out_grad, seg_ids, params, first_moment, second_moment):
    spread = TAIL // count
    row_count = (params.shape[0] - spread) // D
    rows, tail = rows_from_flat(params.astype(jnp.bfloat16), spread, count)
    sent = jnp.concatenate([rows, jnp.pad(tail, ((0, 3), (0, 0)))])
    whole = lax.all_gather(sent, AXES, axis=0, tiled=False)
    matrices = whole[:, :row_count].reshape(-1)
    weights = unpack_flat(jnp.concatenate([matrices, whole[count - 1, row_count : row_count + 13].reshape(-1)]))
    result, kept_state = forward(block_input, seg_ids, weights)
    back_x, grads = backward(kept_state, out_grad, weights)
    big = jnp.concatenate([g.astype(jnp.bfloat16).reshape(-1, D) for g in grads[:4]])
    small = jnp.concatenate([g.astype(jnp.bfloat16).reshape(-1, D) for g in grads[4:]])
    small = jnp.pad(small, ((0, 3), (0, 0)))
    spots = jnp.where(jnp.arange(count)[:, None, None] == count - 1, small[None], jnp.zeros((), jnp.bfloat16))
    out = jnp.concatenate([big.reshape(count, row_count, D), spots], axis=1)
    owned = lax.psum_scatter(out, AXES, scatter_dimension=0, tiled=False).astype(jnp.float32)
    owned_grads = flat_from_rows(owned[:row_count], owned[row_count : row_count + 13], spread, count)
    new_params, new_first, new_second = adam_update(params, owned_grads, first_moment, second_moment)
    return (result, back_x, owned_grads, new_params, new_first, new_second)


def solution(mesh):
    in_specs = (
        P(None, ("dp", "fsdp"), None),
        P(None, ("dp", "fsdp"), None),
        P(None, ("dp", "fsdp")),
        P(("dp", "fsdp")),
        P(("dp", "fsdp")),
        P(("dp", "fsdp")),
    )
    out_specs = (
        P(None, ("dp", "fsdp"), None),
        P(None, ("dp", "fsdp"), None),
        P(("dp", "fsdp")),
        P(("dp", "fsdp")),
        P(("dp", "fsdp")),
        P(("dp", "fsdp")),
    )
    count = mesh.shape["dp"] * mesh.shape["fsdp"]
    return jax.shard_map(functools.partial(body, count), mesh=mesh, in_specs=in_specs, out_specs=out_specs, check_vma=False)
```

```python
import functools
import math

import jax
import jax.numpy as jnp
from jax import lax
from jax.experimental import pallas as pl
from jax.experimental.pallas import tpu as pltpu
from jax.sharding import PartitionSpec as P

D = 768
FF = 3072
HEADS = 12
HEAD_DIM = 64
ROT = 16
STEP = 3


NORM_EPS = 1e-05
BETA_ONE = 0.9
BETA_TWO = 0.95
LEARN_RATE = 0.05
WEIGHT_DECAY = 0.1
ADAM_EPS = 1e-08


def layout_shapes():
    return [
        (D, 3 * D),
        (D, D),
        (D, FF),
        (FF, D),
        (3 * D,),
        (D,),
        (FF,),
        (D,),
        (D,),
        (D,),
        (D,),
        (D,),
    ]


def unpack_flat(flat_vec):
    pieces_out = []
    offset = 0
    for item_shape in layout_shapes():
        length = math.prod(item_shape)
        pieces_out.append(flat_vec[offset : offset + length].reshape(item_shape))
        offset += length
    return pieces_out


def product(form, left, right):
    return jnp.einsum(form, left, right, preferred_element_type=jnp.float32)


def block_tables(seg_rows):
    row_count = seg_rows.shape[1]
    row_idx = jnp.arange(row_count)
    same_seq = seg_rows[:, :, None] == seg_rows[:, None, :]
    earlier = row_idx[None, :] < row_idx[:, None]
    diagonal = row_idx[None, :] == row_idx[:, None]
    causal = row_idx[None, :] <= row_idx[:, None]
    allowed = same_seq & causal[None] & ((seg_rows[:, :, None] >= 0) | diagonal[None])
    position = jnp.sum(jnp.where(same_seq & earlier[None], 1, 0), axis=2).astype(jnp.float32)
    inv_freq = 10000.0 ** (-(jnp.arange(ROT // 2, dtype=jnp.float32) * 2.0) / ROT)
    angles = position[:, :, None] * inv_freq[None, None, :]
    return (allowed, jnp.cos(angles)[:, :, None, :], jnp.sin(angles)[:, :, None, :])


def rotate(vecs, cos_t, sin_t):
    half_rot = ROT // 2
    first = vecs[..., :half_rot]
    second = vecs[..., half_rot:ROT]
    return jnp.concatenate(
        [first * cos_t - second * sin_t, second * cos_t + first * sin_t, vecs[..., ROT:]], axis=-1
    )


def unrotate(vecs, cos_t, sin_t):
    half_rot = ROT // 2
    first = vecs[..., :half_rot]
    second = vecs[..., half_rot:ROT]
    return jnp.concatenate(
        [first * cos_t + second * sin_t, second * cos_t - first * sin_t, vecs[..., ROT:]], axis=-1
    )


def layer_norm(flat_x, gain, shift):
    row_mean = jnp.mean(flat_x, axis=-1, keepdims=True)
    centred = flat_x - row_mean
    row_var = jnp.mean(centred * centred, axis=-1, keepdims=True)
    inv_std = lax.rsqrt(row_var + NORM_EPS)
    normed = centred * inv_std
    return (
        normed,
        inv_std,
        (normed * gain.astype(jnp.float32) + shift.astype(jnp.float32)).astype(jnp.bfloat16),
    )


def norm_back(grad_act, normed, inv_std, gain):
    grad_gain = jnp.sum(grad_act * normed, axis=0)
    grad_shift = jnp.sum(grad_act, axis=0)
    scaled = grad_act * gain.astype(jnp.float32)
    grad_in = inv_std * (
        scaled
        - jnp.mean(scaled, axis=-1, keepdims=True)
        - normed * jnp.mean(scaled * normed, axis=-1, keepdims=True)
    )
    return (grad_gain, grad_shift, grad_in)


def softmax_rows(query_bf, key_bf, allowed, log_total):
    scores = product("gqhd,gkhd->ghqk", query_bf, key_bf) * HEAD_DIM ** (-0.5)
    mask_b = allowed[:, None]
    masked = jnp.where(mask_b, scores, -jnp.inf)
    if log_total is None:
        top_score = jnp.max(masked, axis=-1, keepdims=True)
        expo = jnp.where(mask_b, jnp.exp(masked - top_score), 0.0)
        log_total = top_score + jnp.log(jnp.sum(expo, axis=-1, keepdims=True))
    prob_rows = jnp.where(mask_b, jnp.exp(masked - log_total), 0.0)
    return (prob_rows, log_total)


def forward(x_rows, seg_rows, weights):
    (
        w_qkv,
        w_out,
        w_up,
        w_down,
        b_qkv,
        b_out,
        b_up,
        b_down,
        gain_one,
        shift_one,
        gain_two,
        shift_two,
    ) = weights
    group_count, row_count = seg_rows.shape
    allowed, cos_t, sin_t = block_tables(seg_rows)
    flat_x = x_rows.reshape(group_count * row_count, D)
    normed_one, inv_one, act_one = layer_norm(flat_x, gain_one, shift_one)
    normed_two, inv_two, act_two = layer_norm(flat_x, gain_two, shift_two)
    qkv_rows = jnp.dot(act_one, w_qkv, preferred_element_type=jnp.float32) + b_qkv.astype(
        jnp.float32
    )
    qkv_rows = qkv_rows.reshape(group_count, row_count, 3, HEADS, HEAD_DIM)
    query_bf = rotate(qkv_rows[:, :, 0], cos_t, sin_t).astype(jnp.bfloat16)
    key_bf = rotate(qkv_rows[:, :, 1], cos_t, sin_t).astype(jnp.bfloat16)
    value_bf = qkv_rows[:, :, 2].astype(jnp.bfloat16)
    prob_rows, log_total = softmax_rows(query_bf, key_bf, allowed, None)
    prob_bf = prob_rows.astype(jnp.bfloat16)
    attn_bf = (
        product("ghqk,gkhd->gqhd", prob_bf, value_bf)
        .astype(jnp.bfloat16)
        .reshape(group_count * row_count, D)
    )
    attn_out = jnp.dot(attn_bf, w_out, preferred_element_type=jnp.float32) + b_out.astype(
        jnp.float32
    )
    up_rows = jnp.dot(act_two, w_up, preferred_element_type=jnp.float32) + b_up.astype(jnp.float32)
    hidden_bf = jax.nn.gelu(up_rows, approximate=False).astype(jnp.bfloat16)
    mlp_out = jnp.dot(hidden_bf, w_down, preferred_element_type=jnp.float32) + b_down.astype(
        jnp.float32
    )
    result = flat_x + attn_out + mlp_out
    kept_state = (
        normed_one,
        inv_one,
        act_one,
        normed_two,
        inv_two,
        act_two,
        query_bf,
        key_bf,
        value_bf,
        log_total,
        attn_bf,
        up_rows,
        hidden_bf,
        allowed,
        cos_t,
        sin_t,
        seg_rows,
    )
    return (result.reshape(group_count, row_count, D), kept_state)


def backward(kept_state, grad_rows, weights):
    (
        w_qkv,
        w_out,
        w_up,
        w_down,
        b_qkv,
        b_out,
        b_up,
        b_down,
        gain_one,
        shift_one,
        gain_two,
        shift_two,
    ) = weights
    (
        normed_one,
        inv_one,
        act_one,
        normed_two,
        inv_two,
        act_two,
        query_bf,
        key_bf,
        value_bf,
        log_total,
        attn_bf,
        up_rows,
        hidden_bf,
        allowed,
        cos_t,
        sin_t,
        seg_rows,
    ) = kept_state
    group_count, row_count = seg_rows.shape
    valid = (seg_rows >= 0).astype(jnp.float32).reshape(group_count * row_count, 1)
    grad_y = grad_rows.reshape(group_count * row_count, D) * valid
    grad_y_bf = grad_y.astype(jnp.bfloat16)
    grad_bias = jnp.sum(grad_y, axis=0)
    grad_w_down = jnp.dot(hidden_bf.T, grad_y_bf, preferred_element_type=jnp.float32)
    grad_w_out = jnp.dot(attn_bf.T, grad_y_bf, preferred_element_type=jnp.float32)
    grad_hidden = jnp.dot(grad_y_bf, w_down.T, preferred_element_type=jnp.float32)
    cdf_part = 0.5 * (1.0 + jax.scipy.special.erf(up_rows * 0.7071067811865476))
    pdf_part = jnp.exp(-0.5 * up_rows * up_rows) * 0.3989422804014327
    grad_up = grad_hidden * (cdf_part + up_rows * pdf_part)
    grad_b_up = jnp.sum(grad_up, axis=0)
    grad_up_bf = grad_up.astype(jnp.bfloat16)
    grad_w_up = jnp.dot(act_two.T, grad_up_bf, preferred_element_type=jnp.float32)
    grad_act_two = jnp.dot(grad_up_bf, w_up.T, preferred_element_type=jnp.float32)
    grad_attn = jnp.dot(grad_y_bf, w_out.T, preferred_element_type=jnp.float32).astype(jnp.bfloat16)
    grad_attn = grad_attn.reshape(group_count, row_count, HEADS, HEAD_DIM)
    prob_rows, unused_total = softmax_rows(query_bf, key_bf, allowed, log_total)
    prob_bf = prob_rows.astype(jnp.bfloat16)
    grad_value = product("ghqk,gqhd->gkhd", prob_bf, grad_attn)
    grad_prob = product("gqhd,gkhd->ghqk", grad_attn, value_bf)
    delta_rows = jnp.sum(prob_rows * grad_prob, axis=-1, keepdims=True)
    grad_score_bf = (prob_rows * (grad_prob - delta_rows) * HEAD_DIM ** (-0.5)).astype(jnp.bfloat16)
    grad_query = unrotate(product("ghqk,gkhd->gqhd", grad_score_bf, key_bf), cos_t, sin_t)
    grad_key = unrotate(product("ghqk,gqhd->gkhd", grad_score_bf, query_bf), cos_t, sin_t)
    grad_qkv = jnp.stack([grad_query, grad_key, grad_value], axis=2).reshape(
        group_count * row_count, 3 * D
    )
    grad_b_qkv = jnp.sum(grad_qkv, axis=0)
    grad_qkv_bf = grad_qkv.astype(jnp.bfloat16)
    grad_w_qkv = jnp.dot(act_one.T, grad_qkv_bf, preferred_element_type=jnp.float32)
    grad_act_one = jnp.dot(grad_qkv_bf, w_qkv.T, preferred_element_type=jnp.float32)
    grad_gain_one, grad_shift_one, back_one = norm_back(grad_act_one, normed_one, inv_one, gain_one)
    grad_gain_two, grad_shift_two, back_two = norm_back(grad_act_two, normed_two, inv_two, gain_two)
    input_grad = (grad_y + back_one + back_two).reshape(group_count, row_count, D)
    grads = (
        grad_w_qkv,
        grad_w_out,
        grad_w_up,
        grad_w_down,
        grad_b_qkv,
        grad_bias,
        grad_b_up,
        grad_bias,
        grad_gain_one,
        grad_shift_one,
        grad_gain_two,
        grad_shift_two,
    )
    return (input_grad, grads)


def adam_update(params, grads, first_moment, second_moment):
    new_first = BETA_ONE * first_moment + (1.0 - BETA_ONE) * grads
    new_second = BETA_TWO * second_moment + (1.0 - BETA_TWO) * grads * grads
    first_hat = new_first / (1.0 - BETA_ONE**STEP)
    second_hat = new_second / (1.0 - BETA_TWO**STEP)
    new_params = params - LEARN_RATE * (
        first_hat / (jnp.sqrt(second_hat) + ADAM_EPS) + WEIGHT_DECAY * params
    )
    return (new_params, new_first, new_second)


AXES = ("dp", "fsdp")
MATRIX_ROWS = 9 * D + 3 * D
TAIL = 13 * D


def rows_from_flat(flat, spread, count):
    me = lax.axis_index(AXES)
    tail = flat[flat.shape[0] - TAIL :]
    before = lax.ppermute(tail, AXES, [(i, (i + 1) % count) for i in range(count)])
    joined = jnp.concatenate([before, flat])
    rows = lax.dynamic_slice(joined, (TAIL - spread * me,), (flat.shape[0] - spread,))
    return rows.reshape(-1, D), tail.reshape(-1, D)


def flat_from_rows(rows, tail, spread, count):
    me = lax.axis_index(AXES)
    head = rows.reshape(-1)[:TAIL]
    after = lax.ppermute(head, AXES, [(i, (i - 1) % count) for i in range(count)])
    after = jnp.where(me == count - 1, tail.reshape(-1), after)
    joined = jnp.concatenate([rows.reshape(-1), after])
    return lax.dynamic_slice(joined, (spread * me,), (rows.size + spread,))


def body(count, block_input, out_grad, seg_ids, params, first_moment, second_moment):
    spread = TAIL // count
    row_count = (params.shape[0] - spread) // D
    rows, tail = rows_from_flat(params.astype(jnp.bfloat16), spread, count)
    sent = jnp.concatenate([rows, jnp.pad(tail, ((0, 3), (0, 0)))])
    whole = lax.all_gather(sent, AXES, axis=0, tiled=False)
    matrices = whole[:, :row_count].reshape(-1)
    weights = unpack_flat(jnp.concatenate([matrices, whole[count - 1, row_count : row_count + 13].reshape(-1)]))
    result, kept_state = forward(block_input, seg_ids, weights)
    back_x, grads = backward(kept_state, out_grad, weights)
    big = jnp.concatenate([g.astype(jnp.bfloat16).reshape(-1, D) for g in grads[:4]])
    small = jnp.concatenate([g.astype(jnp.bfloat16).reshape(-1, D) for g in grads[4:]])
    small = jnp.pad(small, ((0, 3), (0, 0)))
    spots = jnp.where(jnp.arange(count)[:, None, None] == count - 1, small[None], jnp.zeros((), jnp.bfloat16))
    out = jnp.concatenate([big.reshape(count, row_count, D), spots], axis=1)
    owned = lax.psum_scatter(out, AXES, scatter_dimension=0, tiled=False).astype(jnp.float32)
    owned_grads = flat_from_rows(owned[:row_count], owned[row_count : row_count + 13], spread, count)
    new_params, new_first, new_second = adam_update(params, owned_grads, first_moment, second_moment)
    return (result, back_x, owned_grads, new_params, new_first, new_second)


BF = jnp.bfloat16
F32 = jnp.float32
PLANES = 4
PART = D // PLANES
SPOT = 96
SLAB = 352
STARTS = (0, 80, 176, 256)


def dot_nn(a, b):
    return lax.dot_general(a, b, (((1,), (0,)), ((), ())), preferred_element_type=F32)


def dot_nt(a, b):
    return lax.dot_general(a, b, (((1,), (1,)), ((), ())), preferred_element_type=F32)


def dot_tn(a, b):
    return lax.dot_general(a, b, (((0,), (0,)), ((), ())), preferred_element_type=F32)


def lanes_of(width):
    return lax.broadcasted_iota(jnp.int32, (1, width), 1)


def group_mask(index, width=D, size=PART):
    lane = lanes_of(width)
    return (lane >= index * size) & (lane < (index + 1) * size)


def turned(value, shift):
    shift = shift % value.shape[-1]
    return value if shift == 0 else pltpu.roll(value, shift, value.ndim - 1)


def spread_groups(parts, first):
    total = None
    for group, part in enumerate(parts):
        moved = jnp.where(group_mask(group), turned(part, PART * (group - first)), 0.0)
        total = moved if total is None else total + moved
    return total


def every(size, stride, first):
    row = lax.broadcasted_iota(jnp.int32, (size, SPOT), 0)
    col = lax.broadcasted_iota(jnp.int32, (size, SPOT), 1)
    return jnp.where(col == stride * row + first, 1.0, 0.0).astype(BF)


def permutations():
    place = jnp.arange(D)
    part, inner = place // PART, place % PART
    hidden_from = SPOT * (inner // 24) + 24 * part + inner % 24
    kind = inner // HEAD_DIM
    head = jnp.where(
        part < 3,
        part + jnp.where(kind == 0, 0, jnp.where(kind == 1, 5, 9)),
        jnp.where(kind == 0, 3, jnp.where(kind == 1, 4, 8)),
    )
    head_from = HEAD_DIM * head + inner % HEAD_DIM
    rows = place[:, None]
    return (
        (rows == head_from[None]).astype(BF),
        (rows == hidden_from[None]).astype(BF),
    )


def pack_kernel(where_ref, rows_ref, tail_ref, heads_ref, hidden_ref, *outs):
    out_refs, spot = outs[:PLANES], outs[PLANES]
    plane, place = where_ref[0], where_ref[1]
    device = 8 * plane + place
    spot[...] = jnp.zeros_like(spot)
    for i in range(3):
        block = 3 * device + i

        @pl.when(block < 24)
        def _():
            for j in range(3):
                picked = dot_nn(every(32, 3, j), rows_ref[SPOT * i : SPOT * i + SPOT, :].astype(BF))
                sorted_ = dot_nn(picked.astype(BF), heads_ref[...])
                parts = [sorted_[8 * g : 8 * g + 8] for g in range(4)]
                for s in range(PLANES):
                    spot[s, 24 * i + 8 * j : 24 * i + 8 * j + 8, :] = spread_groups(parts, s)

        @pl.when((block >= 32) & (block < 64))
        def _():
            source = rows_ref[SPOT * i : SPOT * i + SPOT, :].astype(BF)
            parts = [
                dot_nn(dot_nn(every(24, 4, j), source).astype(BF), hidden_ref[...])
                for j in range(4)
            ]
            for s in range(PLANES):
                value = spread_groups(parts, s)
                if i < 2:
                    spot[s, 24 * i : 24 * i + 24, :] = value
                else:
                    mixed = block == 32

                    @pl.when(mixed)
                    def _():
                        spot[s, 0:24, :] = value

                    @pl.when(jnp.logical_not(mixed))
                    def _():
                        spot[s, 48:72, :] = value

        @pl.when(block >= 64)
        def _():
            for s in range(PLANES):
                spot[s, 24 * i : 24 * i + 24, :] = rows_ref[
                    SPOT * i + 24 * s : SPOT * i + 24 * s + 24, :
                ]

    @pl.when(device == 8)
    def _():
        for s in range(3):
            spot[s, 0:64, :] = rows_ref[64 * s : 64 * s + 64, :]
        spot[3, 0:96, :] = rows_ref[192:288, :]

    @pl.when(device == 9)
    def _():
        for s in range(3):
            spot[s, 0:64, :] = rows_ref[32 + 64 * s : 96 + 64 * s, :]
        spot[3, 0:32, :] = rows_ref[0:32, :]
        spot[3, 32:96, :] = rows_ref[224:288, :]

    @pl.when(device == 10)
    def _():
        for s in range(3):
            spot[s, 24:88, :] = rows_ref[64 * s : 64 * s + 64, :]

    @pl.when(device == 31)
    def _():
        upper = tail_ref[0:8, :].astype(BF)
        by_head = dot_nn(upper, heads_ref[...])
        by_hidden = dot_nn(upper, hidden_ref[...])
        for s in range(PLANES):
            spot[s, 72:73, :] = spread_groups([by_hidden[4 + j : 5 + j] for j in range(4)], s)
            spot[s, 73:74, :] = spread_groups([by_head[j : j + 1] for j in range(3)], s)
            spot[s, 74:75, :] = tail_ref[3:4, :]
            spot[s, 80:88, :] = tail_ref[8:16, :]

    for r in range(PLANES):
        out_refs[r][...] = spot[plane ^ r].astype(BF)


def unpack_kernel(where_ref, *refs):
    in_refs, (heads_ref, hidden_ref, rows_ref, tail_ref, spot) = refs[:PLANES], refs[PLANES:]
    plane, place = where_ref[0], where_ref[1]
    device = 8 * plane + place
    for r in range(PLANES):
        spot[plane ^ r] = in_refs[r][...].astype(F32)
    for i in range(3):
        block = 3 * device + i

        @pl.when(block < 24)
        def _():
            total = None
            for j in range(3):
                base = 24 * i + 8 * j
                parts = [spot[s, base : base + 8, :] for s in range(PLANES)]
                sorted_ = jnp.concatenate([spread_groups(parts, g) for g in range(4)], axis=0)
                picked = dot_nt(sorted_.astype(BF), heads_ref[...]).astype(BF)
                value = dot_tn(every(32, 3, j), picked)
                total = value if total is None else total + value
            rows_ref[SPOT * i : SPOT * i + SPOT, :] = total

        @pl.when((block >= 32) & (block < 64))
        def _():
            start = 24 * i
            if i == 2:
                start = pl.multiple_of(jnp.where(block == 32, 0, 48), 8)
            parts = [spot[s, pl.ds(start, 24), :] for s in range(PLANES)]
            total = None
            for j in range(4):
                picked = dot_nt(spread_groups(parts, j).astype(BF), hidden_ref[...]).astype(BF)
                value = dot_tn(every(24, 4, j), picked)
                total = value if total is None else total + value
            rows_ref[SPOT * i : SPOT * i + SPOT, :] = total

        @pl.when(block >= 64)
        def _():
            for s in range(PLANES):
                rows_ref[SPOT * i + 24 * s : SPOT * i + 24 * s + 24, :] = spot[
                    s, 24 * i : 24 * i + 24, :
                ]

    @pl.when(device == 8)
    def _():
        for s in range(3):
            rows_ref[64 * s : 64 * s + 64, :] = spot[s, 0:64, :]
        rows_ref[192:288, :] = spot[3, 0:96, :]

    @pl.when(device == 9)
    def _():
        for s in range(3):
            rows_ref[32 + 64 * s : 96 + 64 * s, :] = spot[s, 0:64, :]
        rows_ref[0:32, :] = spot[3, 0:32, :]
        rows_ref[224:288, :] = spot[3, 32:96, :]

    @pl.when(device == 10)
    def _():
        for s in range(3):
            rows_ref[64 * s : 64 * s + 64, :] = spot[s, 24:88, :]

    tail_ref[...] = jnp.zeros_like(tail_ref)

    @pl.when(device == 31)
    def _():
        whole = [spot[s, 72:73, :] for s in range(PLANES)]
        for j in range(4):
            row = jnp.broadcast_to(spread_groups(whole, j), (8, D)).astype(BF)
            tail_ref[4 + j : 5 + j, :] = dot_nt(row, hidden_ref[...])[0:1]
        whole = [spot[s, 73:74, :] for s in range(PLANES)]
        for j in range(3):
            row = jnp.broadcast_to(spread_groups(whole, j), (8, D)).astype(BF)
            tail_ref[j : j + 1, :] = dot_nt(row, heads_ref[...])[0:1]
        tail_ref[3:4, :] = sum(spot[s, 74:75, :] for s in range(PLANES))
        tail_ref[8:16, :] = sum(spot[s, 80:88, :] for s in range(PLANES))


def slab_start(plane):
    start = jnp.where(plane == 1, STARTS[1], jnp.where(plane == 2, STARTS[2], STARTS[3]))
    return pl.multiple_of(jnp.where(plane == 0, 0, start), 16)


def slab_kernel(where_ref, a_ref, b_ref, c_ref, d_ref, out_ref):
    for r, ref in enumerate((a_ref, b_ref, c_ref, d_ref)):
        source = where_ref[0] ^ r
        out_ref[pl.ds(slab_start(source), 80), :] = ref[0:80, :]

        @pl.when((source == 1) | (source == 3))
        def _():
            out_ref[pl.ds(slab_start(source) + 80, 16), :] = ref[80:96, :]


def split_kernel(where_ref, a_ref, b_ref, c_ref, d_ref, *outs):
    out_refs, total = outs[:PLANES], outs[PLANES]
    total[...] = (a_ref[...].astype(F32) + b_ref[...].astype(F32)) + (
        c_ref[...].astype(F32) + d_ref[...].astype(F32)
    )
    for r in range(PLANES):
        out_refs[r][...] = total[pl.ds(slab_start(where_ref[0] ^ r), SPOT), :].astype(BF)


def layer_kernel(where_ref, *refs):
    act_refs, slab_refs = refs[:4], refs[4:12]
    grad_refs, back_refs = refs[12:20], refs[20:24]
    (w_up, w_down, w_out, packed, w_qkv, tails, bf_up, bf_down, bf_out, bf_qkv, normed, grad_y,
     qkv, attn, g_qkv, g_attn, up, slab) = refs[24:]
    plane, spot, core = where_ref[0], where_ref[1], where_ref[2]
    lane = lanes_of(D)

    def place_of(index):
        return 2 * (spot ^ (index % 4)) + (core if index < 4 else 1 - core)

    w_out[...] = jnp.zeros_like(w_out)
    for index, ref in enumerate(slab_refs):
        q = place_of(index)
        for i in range(3):
            for j in range(3):
                packed[j, pl.ds(pl.multiple_of(24 * q + 8 * i, 8), 8), :] = ref[0:80, :][
                    24 * i + 8 * j : 24 * i + 8 * j + 8
                ].astype(F32)
        one = ref[80:176, :].astype(F32)
        two = ref[176:256, :].astype(F32)
        three = ref[256:352, :].astype(F32)

        @pl.when(q >= 3)
        def _():
            w_up[pl.ds(pl.multiple_of(72 * q - 192, 8), 72), :] = one[0:72]

        @pl.when(q == 2)
        def _():
            w_up[0:24, :] = one[0:24]

            @pl.when(plane < 3)
            def _():
                w_out[128:192, :] = one[24:88]

        @pl.when((q < 2) & (plane < 3))
        def _():
            w_out[pl.ds(pl.multiple_of(64 * q, 8), 64), :] = one[0:64]

        @pl.when((q < 2) & (plane == 3))
        def _():
            w_out[pl.ds(pl.multiple_of(96 * q, 8), 96), :] = one[0:96]

        @pl.when(q < 5)
        def _():
            w_up[pl.ds(pl.multiple_of(384 + 72 * q, 8), 72), :] = two[0:72]

        @pl.when(q == 5)
        def _():
            w_up[744:768, :] = two[0:24]
            w_down[0:48, :] = two[24:72]

        @pl.when(q > 5)
        def _():
            w_down[pl.ds(pl.multiple_of(72 * q - 384, 8), 72), :] = two[0:72]

        w_down[pl.ds(pl.multiple_of(192 + 72 * q, 8), 72), :] = three[0:72]

        @pl.when(q == 7)
        def _():
            tails[...] = three[72:88]

    for j in range(3):
        for i in range(4):
            moved = turned(packed[j], -PART * i)[:, 0:256]
            moved = jnp.where(lanes_of(256) < PART, moved, 0.0)
            w_qkv[:, i, :, 256 * j : 256 * j + 256] = moved.reshape(24, 8, 256)
    bf_up[...] = w_up[...].astype(BF)
    bf_down[...] = w_down[...].astype(BF)
    bf_out[...] = w_out[...].astype(BF)
    bf_qkv[...] = w_qkv[...].reshape(D, D).astype(BF)

    for r in range(4):
        normed[128 * r : 128 * r + 128, :] = act_refs[r][0:128, :]
        grad_y[128 * r : 128 * r + 128, :] = act_refs[r][128:256, :]
    bias_up = tails[0:1, :]
    flat_bias = tails[1:2, :]
    bias_qkv = jnp.zeros((1, D), F32)
    for j in range(3):
        keep = (lane >= 256 * j) & (lane < 256 * j + PART)
        bias_qkv = jnp.where(keep, turned(flat_bias, 64 * j), bias_qkv)
    bias_y = jnp.where(plane == 0, tails[2:3, :] + tails[8:9, :], 0.0)
    gain_one, shift_one = tails[9:10, :], tails[10:11, :]
    gain_two, shift_two = tails[11:12, :], tails[12:13, :]

    def act_of(gain, shift):
        return (normed[...].astype(F32) * gain + shift).astype(BF)

    act_one = act_of(gain_one, shift_one)
    qkv[...] = dot_nn(act_one, bf_qkv[...]) + bias_qkv
    g_attn[...] = dot_nt(grad_y[...], bf_out[...]).astype(BF)

    rows = lax.broadcasted_iota(jnp.int32, (128, 128), 0)
    cols = lax.broadcasted_iota(jnp.int32, (128, 128), 1)
    same_block = (rows < 64) == (cols < 64)
    eye = rows == cols
    in_head = lanes_of(128) % 64
    freq = jnp.exp((in_head % 8).astype(F32) * (-2.0 * math.log(10000.0) / ROT))
    low_half = lanes_of(128) < 64
    for r in range(4):
        span = slice(128 * r, 128 * r + 128)
        seg_row = jnp.broadcast_to(act_refs[r][256:272, 0:128].astype(F32)[0:1], (128, 128))
        seg_col = jnp.sum(jnp.where(eye, seg_row, 0.0), axis=1, keepdims=True)
        same = (seg_col == seg_row) & same_block
        allowed = same & (cols <= rows) & ((seg_col >= 0.0) | eye)
        position = jnp.sum(jnp.where(same & (cols < rows), 1.0, 0.0), axis=1, keepdims=True)
        angle = position * freq
        cos_t = jnp.where(in_head < ROT, jnp.cos(angle), 1.0)
        sine = jnp.sin(angle)
        sin_a = jnp.where(in_head < 8, sine, 0.0)
        sin_b = jnp.where((in_head >= 8) & (in_head < ROT), sine, 0.0)

        def rotated(x):
            return x * cos_t - turned(x, -8) * sin_a + turned(x, 8) * sin_b

        def unrotated(x):
            return x * cos_t + turned(x, -8) * sin_a - turned(x, 8) * sin_b

        for tile in range(2):
            at = [256 * j + 128 * tile for j in range(3)]
            query = rotated(qkv[span, at[0] : at[0] + 128]).astype(BF)
            key = rotated(qkv[span, at[1] : at[1] + 128]).astype(BF)
            value = qkv[span, at[2] : at[2] + 128].astype(BF)
            g_out = g_attn[span, 128 * tile : 128 * tile + 128]
            parts = []
            for half in range(2 - tile):
                mask = low_half if half == 0 else jnp.logical_not(low_half)
                key_h = jnp.where(mask, key, jnp.zeros_like(key))
                value_h = jnp.where(mask, value, jnp.zeros_like(value))
                scores = dot_nt(query, key_h) * HEAD_DIM ** (-0.5)
                masked = jnp.where(allowed, scores, -1e30)
                top = jnp.max(masked, axis=1, keepdims=True)
                expo = jnp.where(allowed, jnp.exp(masked - top), 0.0)
                prob = expo * (1.0 / jnp.sum(expo, axis=1, keepdims=True))
                prob_bf = prob.astype(BF)
                g_prob = dot_nt(g_out, value_h)
                delta = jnp.sum(prob * g_prob, axis=1, keepdims=True)
                g_score = (prob * (g_prob - delta) * HEAD_DIM ** (-0.5)).astype(BF)
                parts.append(
                    (
                        dot_nn(prob_bf, value),
                        dot_tn(prob_bf, g_out),
                        dot_nn(g_score, key),
                        dot_tn(g_score, query),
                    )
                )
            if tile == 0:
                o, gv, gq, gk = [jnp.where(low_half, a, b) for a, b in zip(*parts)]
            else:
                o, gv, gq, gk = [jnp.where(low_half, a, 0.0) for a in parts[0]]
            attn[span, 128 * tile : 128 * tile + 128] = o.astype(BF)
            g_qkv[span, at[0] : at[0] + 128] = unrotated(gq)
            g_qkv[span, at[1] : at[1] + 128] = unrotated(gk)
            g_qkv[span, at[2] : at[2] + 128] = gv
    y = dot_nn(attn[...], bf_out[...]) + bias_y
    grad_out = dot_tn(attn[...], grad_y[...])
    g_bias_qkv = jnp.sum(g_qkv[...], axis=0, keepdims=True)
    g_qkv_bf = g_qkv[...].astype(BF)
    w_qkv[...] = dot_tn(act_one, g_qkv_bf).reshape(24, 4, 8, D)
    g_act_one = dot_nt(g_qkv_bf, bf_qkv[...])
    w_out[...] = grad_out

    act_two = act_of(gain_two, shift_two)
    up[...] = dot_nn(act_two, bf_up[...]) + bias_up
    cdf = 0.5 * (1.0 + lax.erf(up[...] * 0.7071067811865476))
    hidden = (up[...] * cdf).astype(BF)
    y = y + dot_nn(hidden, bf_down[...])
    for r in range(4):
        back_refs[r][0:128, :] = y[128 * r : 128 * r + 128].astype(BF)
    w_down[...] = dot_tn(hidden, grad_y[...])
    pdf = jnp.exp(-0.5 * up[...] * up[...]) * 0.3989422804014327
    g_up = dot_nt(grad_y[...], bf_down[...]) * (cdf + up[...] * pdf)
    g_bias_up = jnp.sum(g_up, axis=0, keepdims=True)
    g_up_bf = g_up.astype(BF)
    w_up[...] = dot_tn(act_two, g_up_bf)
    g_act_two = dot_nt(g_up_bf, bf_up[...])
    wide = normed[...].astype(F32)
    for r in range(4):
        span = slice(128 * r, 128 * r + 128)
        back_refs[r][128:256, :] = (g_act_one[span] * gain_one + g_act_two[span] * gain_two).astype(BF)

    def row_sum(x):
        return jnp.sum(x, axis=0, keepdims=True)

    g_bias_y = row_sum(grad_y[0:128, :].astype(F32))
    flat_bias = jnp.zeros((1, D), F32)
    for j in range(3):
        keep = (lane >= PART * j) & (lane < PART * (j + 1))
        flat_bias = jnp.where(keep, turned(g_bias_qkv, -64 * j), flat_bias)
    tails[...] = jnp.zeros_like(tails)
    tails[0:1, :] = g_bias_up
    tails[1:2, :] = flat_bias
    tails[2:3, :] = g_bias_y
    tails[8:9, :] = g_bias_y
    tails[9:10, :] = row_sum(g_act_one * wide)
    tails[10:11, :] = row_sum(g_act_one)
    tails[11:12, :] = row_sum(g_act_two * wide)
    tails[12:13, :] = row_sum(g_act_two)

    for j in range(3):
        total = None
        for i in range(4):
            piece = w_qkv[:, i, :, 256 * j : 256 * j + 256].reshape(PART, 256)
            piece = jnp.where(lanes_of(256) < PART, piece, 0.0)
            piece = jnp.concatenate([piece, jnp.zeros((PART, 512), F32)], axis=1)
            piece = turned(piece, PART * i)
            total = piece if total is None else total + piece
        packed[j] = total
    for index, ref in enumerate(grad_refs):
        q = place_of(index)
        for i in range(3):
            for j in range(3):
                slab[24 * i + 8 * j : 24 * i + 8 * j + 8, :] = packed[
                    j, pl.ds(pl.multiple_of(24 * q + 8 * i, 8), 8), :
                ]

        @pl.when(q >= 3)
        def _():
            slab[80:152, :] = w_up[pl.ds(pl.multiple_of(72 * q - 192, 8), 72), :]

        @pl.when(q == 2)
        def _():
            slab[80:104, :] = w_up[0:24, :]
            slab[104:168, :] = w_out[128:192, :]

        @pl.when((q < 2) & (plane < 3))
        def _():
            slab[80:144, :] = w_out[pl.ds(pl.multiple_of(64 * q, 8), 64), :]

        @pl.when((q < 2) & (plane == 3))
        def _():
            slab[80:176, :] = w_out[pl.ds(pl.multiple_of(96 * q, 8), 96), :]

        @pl.when(q < 5)
        def _():
            slab[176:248, :] = w_up[pl.ds(pl.multiple_of(384 + 72 * q, 8), 72), :]

        @pl.when(q == 5)
        def _():
            slab[176:200, :] = w_up[744:768, :]
            slab[200:248, :] = w_down[0:48, :]

        @pl.when(q > 5)
        def _():
            slab[176:248, :] = w_down[pl.ds(pl.multiple_of(72 * q - 384, 8), 72), :]

        slab[256:328, :] = w_down[pl.ds(pl.multiple_of(192 + 72 * q, 8), 72), :]
        slab[328:344, :] = tails[...]
        ref[...] = slab[...].astype(BF)


def local_call(kernel, outs, scratch, *operands):
    vmem = pl.BlockSpec(memory_space=pltpu.VMEM)
    return pl.pallas_call(
        kernel,
        out_shape=outs,
        in_specs=[pl.BlockSpec(memory_space=pltpu.SMEM)] + [vmem] * (len(operands) - 1),
        out_specs=jax.tree.map(lambda _: vmem, outs),
        scratch_shapes=scratch,
    )(*operands)


def sliced_body(planes, places, block_input, out_grad, seg_ids, params, first_moment, second_moment):
    count = planes * places * 2
    spread = TAIL // count
    dp, core = lax.axis_index("dp"), lax.axis_index("fsdp")
    plane, spot = dp // places, dp % places
    where_owner = jnp.stack([plane, 2 * spot + core]).astype(jnp.int32)
    where_spot = jnp.stack([plane, spot, core]).astype(jnp.int32)
    across = [
        [(i, (i // places ^ r) * places + i % places) for i in range(planes * places)]
        for r in range(planes)
    ]
    within = [
        [(i, i // places * places + (i % places ^ r)) for i in range(planes * places)]
        for r in range(places)
    ]

    def to_plane(value, r):
        return lax.ppermute(value, "dp", across[r]) if r else value

    def to_spot(value, r):
        return lax.ppermute(value, "dp", within[r]) if r else value

    def to_core(value):
        return lax.ppermute(value, "fsdp", [(0, 1), (1, 0)])

    micro, row_count, _ = block_input.shape
    tokens = micro * row_count
    flat_x = block_input.reshape(tokens, D)
    mean = jnp.mean(flat_x, axis=-1, keepdims=True)
    centred = flat_x - mean
    inv_std = lax.rsqrt(jnp.mean(centred * centred, axis=-1, keepdims=True) + NORM_EPS)
    normed = centred * inv_std
    valid = (seg_ids >= 0).astype(F32).reshape(tokens, 1)
    grad_y = out_grad.reshape(tokens, D) * valid
    seg_rows = jnp.pad(seg_ids.reshape(1, tokens).astype(BF), ((0, 15), (0, D - tokens)))
    sent_acts = jnp.concatenate([normed.astype(BF), grad_y.astype(BF), seg_rows])
    acts = [to_plane(sent_acts, r) for r in range(planes)]

    heads, hidden = permutations()
    rows, tail = rows_from_flat(params, spread, count)
    tail = jnp.pad(tail, ((0, 3), (0, 0)))
    spot_shape = jax.ShapeDtypeStruct((SPOT, D), BF)
    slab_shape = jax.ShapeDtypeStruct((SLAB, D), BF)
    spots = local_call(
        pack_kernel, [spot_shape] * planes, [pltpu.VMEM((planes, SPOT, D), F32)],
        where_owner, rows, tail, heads, hidden,
    )
    spots = [to_plane(spots[r], r) for r in range(planes)]
    slab = local_call(slab_kernel, slab_shape, [], where_owner, *spots)
    slabs = [to_spot(slab, r) for r in range(places)]
    slabs = slabs + [to_core(s) for s in slabs]

    total = planes * tokens
    outs = local_call(
        layer_kernel,
        [slab_shape] * 8 + [jax.ShapeDtypeStruct((2 * tokens, D), BF)] * planes,
        [
            pltpu.VMEM((D, D), F32),
            pltpu.VMEM((D, D), F32),
            pltpu.VMEM((256, D), F32),
            pltpu.VMEM((3, PART, D), F32),
            pltpu.VMEM((24, 4, 8, D), F32),
            pltpu.VMEM((16, D), F32),
            pltpu.VMEM((D, D), BF),
            pltpu.VMEM((D, D), BF),
            pltpu.VMEM((256, D), BF),
            pltpu.VMEM((D, D), BF),
            pltpu.VMEM((total, D), BF),
            pltpu.VMEM((total, D), BF),
            pltpu.VMEM((total, D), F32),
            pltpu.VMEM((total, 256), BF),
            pltpu.VMEM((total, D), F32),
            pltpu.VMEM((total, 256), BF),
            pltpu.VMEM((total, D), F32),
            pltpu.VMEM((SLAB, D), F32),
        ],
        where_spot, *acts, *slabs,
    )
    grads, backs = outs[:8], outs[8:]
    paired = [
        (grads[r].astype(F32) + to_core(grads[4 + r]).astype(F32)).astype(BF) for r in range(places)
    ]
    arrived = [to_spot(paired[r], r) for r in range(places)]
    backs = [to_plane(backs[r], r) for r in range(planes)]
    spots = local_call(
        split_kernel, [spot_shape] * planes, [pltpu.VMEM((SLAB, D), F32)], where_owner, *arrived
    )
    spots = [to_plane(spots[r], r) for r in range(planes)]
    grad_rows, grad_tail = local_call(
        unpack_kernel,
        [
            jax.ShapeDtypeStruct(rows.shape, F32),
            jax.ShapeDtypeStruct((16, D), F32),
        ],
        [pltpu.VMEM((planes, SPOT, D), F32)],
        where_owner, *spots, heads, hidden,
    )
    back = sum(b.astype(F32) for b in backs)
    result = flat_x + back[:tokens]
    scaled = back[tokens:]
    input_grad = grad_y + inv_std * (
        scaled
        - jnp.mean(scaled, axis=-1, keepdims=True)
        - normed * jnp.mean(scaled * normed, axis=-1, keepdims=True)
    )
    owned = flat_from_rows(grad_rows, grad_tail[:13], spread, count)
    new_params, new_first, new_second = adam_update(params, owned, first_moment, second_moment)
    return (
        result.reshape(block_input.shape),
        input_grad.reshape(block_input.shape),
        owned,
        new_params,
        new_first,
        new_second,
    )


def solution(mesh):
    vector, tokens = P(AXES), P(None, AXES, None)
    dp, cores = mesh.shape["dp"], mesh.shape["fsdp"]
    if dp == PLANES * PLANES and cores == 2:
        step = functools.partial(sliced_body, PLANES, dp // PLANES)
    else:
        step = functools.partial(body, dp * cores)
    return jax.shard_map(
        step,
        mesh=mesh,
        in_specs=(tokens, tokens, P(None, AXES), vector, vector, vector),
        out_specs=(tokens, tokens, vector, vector, vector, vector),
        check_vma=False,
    )
```

```python
import functools
import math

import jax
import jax.numpy as jnp
from jax import lax
from jax.experimental import pallas as pl
from jax.experimental.pallas import tpu as pltpu
from jax.sharding import PartitionSpec as P


D = 768
FF = 3072
HEADS = 12
HEAD_DIM = 64
ROT = 16
STEP = 3


NORM_EPS = 1e-05
BETA_ONE = 0.9
BETA_TWO = 0.95
LEARN_RATE = 0.05
WEIGHT_DECAY = 0.1
ADAM_EPS = 1e-08


def layout_shapes():
    return [
        (D, 3 * D),
        (D, D),
        (D, FF),
        (FF, D),
        (3 * D,),
        (D,),
        (FF,),
        (D,),
        (D,),
        (D,),
        (D,),
        (D,),
    ]


def unpack_flat(flat_vec):
    pieces_out = []
    offset = 0
    for item_shape in layout_shapes():
        length = math.prod(item_shape)
        pieces_out.append(flat_vec[offset : offset + length].reshape(item_shape))
        offset += length
    return pieces_out


def product(form, left, right):
    return jnp.einsum(form, left, right, preferred_element_type=jnp.float32)


def block_tables(seg_rows):
    row_count = seg_rows.shape[1]
    row_idx = jnp.arange(row_count)
    same_seq = seg_rows[:, :, None] == seg_rows[:, None, :]
    earlier = row_idx[None, :] < row_idx[:, None]
    diagonal = row_idx[None, :] == row_idx[:, None]
    causal = row_idx[None, :] <= row_idx[:, None]
    allowed = same_seq & causal[None] & ((seg_rows[:, :, None] >= 0) | diagonal[None])
    position = jnp.sum(jnp.where(same_seq & earlier[None], 1, 0), axis=2).astype(jnp.float32)
    inv_freq = 10000.0 ** (-(jnp.arange(ROT // 2, dtype=jnp.float32) * 2.0) / ROT)
    angles = position[:, :, None] * inv_freq[None, None, :]
    return (allowed, jnp.cos(angles)[:, :, None, :], jnp.sin(angles)[:, :, None, :])


def rotate(vecs, cos_t, sin_t):
    half_rot = ROT // 2
    first = vecs[..., :half_rot]
    second = vecs[..., half_rot:ROT]
    return jnp.concatenate(
        [first * cos_t - second * sin_t, second * cos_t + first * sin_t, vecs[..., ROT:]], axis=-1
    )


def unrotate(vecs, cos_t, sin_t):
    half_rot = ROT // 2
    first = vecs[..., :half_rot]
    second = vecs[..., half_rot:ROT]
    return jnp.concatenate(
        [first * cos_t + second * sin_t, second * cos_t - first * sin_t, vecs[..., ROT:]], axis=-1
    )


def layer_norm(flat_x, gain, shift):
    row_mean = jnp.mean(flat_x, axis=-1, keepdims=True)
    centred = flat_x - row_mean
    row_var = jnp.mean(centred * centred, axis=-1, keepdims=True)
    inv_std = lax.rsqrt(row_var + NORM_EPS)
    normed = centred * inv_std
    return (
        normed,
        inv_std,
        (normed * gain.astype(jnp.float32) + shift.astype(jnp.float32)).astype(jnp.bfloat16),
    )


def norm_back(grad_act, normed, inv_std, gain):
    grad_gain = jnp.sum(grad_act * normed, axis=0)
    grad_shift = jnp.sum(grad_act, axis=0)
    scaled = grad_act * gain.astype(jnp.float32)
    grad_in = inv_std * (
        scaled
        - jnp.mean(scaled, axis=-1, keepdims=True)
        - normed * jnp.mean(scaled * normed, axis=-1, keepdims=True)
    )
    return (grad_gain, grad_shift, grad_in)


def softmax_rows(query_bf, key_bf, allowed, log_total):
    scores = product("gqhd,gkhd->ghqk", query_bf, key_bf) * HEAD_DIM ** (-0.5)
    mask_b = allowed[:, None]
    masked = jnp.where(mask_b, scores, -jnp.inf)
    if log_total is None:
        top_score = jnp.max(masked, axis=-1, keepdims=True)
        expo = jnp.where(mask_b, jnp.exp(masked - top_score), 0.0)
        log_total = top_score + jnp.log(jnp.sum(expo, axis=-1, keepdims=True))
    prob_rows = jnp.where(mask_b, jnp.exp(masked - log_total), 0.0)
    return (prob_rows, log_total)


def forward(x_rows, seg_rows, weights):
    (
        w_qkv,
        w_out,
        w_up,
        w_down,
        b_qkv,
        b_out,
        b_up,
        b_down,
        gain_one,
        shift_one,
        gain_two,
        shift_two,
    ) = weights
    group_count, row_count = seg_rows.shape
    allowed, cos_t, sin_t = block_tables(seg_rows)
    flat_x = x_rows.reshape(group_count * row_count, D)
    normed_one, inv_one, act_one = layer_norm(flat_x, gain_one, shift_one)
    normed_two, inv_two, act_two = layer_norm(flat_x, gain_two, shift_two)
    qkv_rows = jnp.dot(act_one, w_qkv, preferred_element_type=jnp.float32) + b_qkv.astype(
        jnp.float32
    )
    qkv_rows = qkv_rows.reshape(group_count, row_count, 3, HEADS, HEAD_DIM)
    query_bf = rotate(qkv_rows[:, :, 0], cos_t, sin_t).astype(jnp.bfloat16)
    key_bf = rotate(qkv_rows[:, :, 1], cos_t, sin_t).astype(jnp.bfloat16)
    value_bf = qkv_rows[:, :, 2].astype(jnp.bfloat16)
    prob_rows, log_total = softmax_rows(query_bf, key_bf, allowed, None)
    prob_bf = prob_rows.astype(jnp.bfloat16)
    attn_bf = (
        product("ghqk,gkhd->gqhd", prob_bf, value_bf)
        .astype(jnp.bfloat16)
        .reshape(group_count * row_count, D)
    )
    attn_out = jnp.dot(attn_bf, w_out, preferred_element_type=jnp.float32) + b_out.astype(
        jnp.float32
    )
    up_rows = jnp.dot(act_two, w_up, preferred_element_type=jnp.float32) + b_up.astype(jnp.float32)
    hidden_bf = jax.nn.gelu(up_rows, approximate=False).astype(jnp.bfloat16)
    mlp_out = jnp.dot(hidden_bf, w_down, preferred_element_type=jnp.float32) + b_down.astype(
        jnp.float32
    )
    result = flat_x + attn_out + mlp_out
    kept_state = (
        normed_one,
        inv_one,
        act_one,
        normed_two,
        inv_two,
        act_two,
        query_bf,
        key_bf,
        value_bf,
        log_total,
        attn_bf,
        up_rows,
        hidden_bf,
        allowed,
        cos_t,
        sin_t,
        seg_rows,
    )
    return (result.reshape(group_count, row_count, D), kept_state)


def backward(kept_state, grad_rows, weights):
    (w_qkv, w_out, w_up, w_down, _, _, _, _, gain_one, _, gain_two, _) = weights
    (
        normed_one,
        inv_one,
        act_one,
        normed_two,
        inv_two,
        act_two,
        query_bf,
        key_bf,
        value_bf,
        log_total,
        attn_bf,
        up_rows,
        hidden_bf,
        allowed,
        cos_t,
        sin_t,
        seg_rows,
    ) = kept_state
    group_count, row_count = seg_rows.shape
    valid = (seg_rows >= 0).astype(jnp.float32).reshape(group_count * row_count, 1)
    grad_y = grad_rows.reshape(group_count * row_count, D) * valid
    grad_y_bf = grad_y.astype(jnp.bfloat16)
    grad_bias = jnp.sum(grad_y, axis=0)
    grad_w_down = jnp.dot(hidden_bf.T, grad_y_bf, preferred_element_type=jnp.float32)
    grad_w_out = jnp.dot(attn_bf.T, grad_y_bf, preferred_element_type=jnp.float32)
    grad_hidden = jnp.dot(grad_y_bf, w_down.T, preferred_element_type=jnp.float32)
    cdf_part = 0.5 * (1.0 + jax.scipy.special.erf(up_rows * 0.7071067811865476))
    pdf_part = jnp.exp(-0.5 * up_rows * up_rows) * 0.3989422804014327
    grad_up = grad_hidden * (cdf_part + up_rows * pdf_part)
    grad_b_up = jnp.sum(grad_up, axis=0)
    grad_up_bf = grad_up.astype(jnp.bfloat16)
    grad_w_up = jnp.dot(act_two.T, grad_up_bf, preferred_element_type=jnp.float32)
    grad_act_two = jnp.dot(grad_up_bf, w_up.T, preferred_element_type=jnp.float32)
    grad_attn = jnp.dot(grad_y_bf, w_out.T, preferred_element_type=jnp.float32).astype(jnp.bfloat16)
    grad_attn = grad_attn.reshape(group_count, row_count, HEADS, HEAD_DIM)
    prob_rows, _ = softmax_rows(query_bf, key_bf, allowed, log_total)
    prob_bf = prob_rows.astype(jnp.bfloat16)
    grad_value = product("ghqk,gqhd->gkhd", prob_bf, grad_attn)
    grad_prob = product("gqhd,gkhd->ghqk", grad_attn, value_bf)
    delta_rows = jnp.sum(prob_rows * grad_prob, axis=-1, keepdims=True)
    grad_score_bf = (prob_rows * (grad_prob - delta_rows) * HEAD_DIM ** (-0.5)).astype(jnp.bfloat16)
    grad_query = unrotate(product("ghqk,gkhd->gqhd", grad_score_bf, key_bf), cos_t, sin_t)
    grad_key = unrotate(product("ghqk,gqhd->gkhd", grad_score_bf, query_bf), cos_t, sin_t)
    grad_qkv = jnp.stack([grad_query, grad_key, grad_value], axis=2).reshape(
        group_count * row_count, 3 * D
    )
    grad_b_qkv = jnp.sum(grad_qkv, axis=0)
    grad_qkv_bf = grad_qkv.astype(jnp.bfloat16)
    grad_w_qkv = jnp.dot(act_one.T, grad_qkv_bf, preferred_element_type=jnp.float32)
    grad_act_one = jnp.dot(grad_qkv_bf, w_qkv.T, preferred_element_type=jnp.float32)
    grad_gain_one, grad_shift_one, back_one = norm_back(grad_act_one, normed_one, inv_one, gain_one)
    grad_gain_two, grad_shift_two, back_two = norm_back(grad_act_two, normed_two, inv_two, gain_two)
    input_grad = (grad_y + back_one + back_two).reshape(group_count, row_count, D)
    grads = (
        grad_w_qkv,
        grad_w_out,
        grad_w_up,
        grad_w_down,
        grad_b_qkv,
        grad_bias,
        grad_b_up,
        grad_bias,
        grad_gain_one,
        grad_shift_one,
        grad_gain_two,
        grad_shift_two,
    )
    return (input_grad, grads)


def adam_update(params, grads, first_moment, second_moment):
    new_first = BETA_ONE * first_moment + (1.0 - BETA_ONE) * grads
    new_second = BETA_TWO * second_moment + (1.0 - BETA_TWO) * grads * grads
    first_hat = new_first / (1.0 - BETA_ONE**STEP)
    second_hat = new_second / (1.0 - BETA_TWO**STEP)
    new_params = params - LEARN_RATE * (
        first_hat / (jnp.sqrt(second_hat) + ADAM_EPS) + WEIGHT_DECAY * params
    )
    return (new_params, new_first, new_second)


AXES = ("dp", "fsdp")
TAIL = 13 * D


def rows_from_flat(flat, spread, count):
    me = lax.axis_index(AXES)
    tail = flat[flat.shape[0] - TAIL :]
    before = lax.ppermute(tail, AXES, [(i, (i + 1) % count) for i in range(count)])
    joined = jnp.concatenate([before, flat])
    rows = lax.dynamic_slice(joined, (TAIL - spread * me,), (flat.shape[0] - spread,))
    return rows.reshape(-1, D), tail.reshape(-1, D)


def flat_from_rows(rows, tail, spread, count):
    me = lax.axis_index(AXES)
    head = rows.reshape(-1)[:TAIL]
    after = lax.ppermute(head, AXES, [(i, (i - 1) % count) for i in range(count)])
    after = jnp.where(me == count - 1, tail.reshape(-1), after)
    joined = jnp.concatenate([rows.reshape(-1), after])
    return lax.dynamic_slice(joined, (spread * me,), (rows.size + spread,))


def body(count, block_input, out_grad, seg_ids, params, first_moment, second_moment):
    spread = TAIL // count
    row_count = (params.shape[0] - spread) // D
    rows, tail = rows_from_flat(params.astype(jnp.bfloat16), spread, count)
    sent = jnp.concatenate([rows, jnp.pad(tail, ((0, 3), (0, 0)))])
    whole = lax.all_gather(sent, AXES, axis=0, tiled=False)
    matrices = whole[:, :row_count].reshape(-1)
    weights = unpack_flat(jnp.concatenate([matrices, whole[count - 1, row_count : row_count + 13].reshape(-1)]))
    result, kept_state = forward(block_input, seg_ids, weights)
    back_x, grads = backward(kept_state, out_grad, weights)
    big = jnp.concatenate([g.astype(jnp.bfloat16).reshape(-1, D) for g in grads[:4]])
    small = jnp.concatenate([g.astype(jnp.bfloat16).reshape(-1, D) for g in grads[4:]])
    small = jnp.pad(small, ((0, 3), (0, 0)))
    spots = jnp.where(jnp.arange(count)[:, None, None] == count - 1, small[None], jnp.zeros((), jnp.bfloat16))
    out = jnp.concatenate([big.reshape(count, row_count, D), spots], axis=1)
    owned = lax.psum_scatter(out, AXES, scatter_dimension=0, tiled=False).astype(jnp.float32)
    owned_grads = flat_from_rows(owned[:row_count], owned[row_count : row_count + 13], spread, count)
    new_params, new_first, new_second = adam_update(params, owned_grads, first_moment, second_moment)
    return (result, back_x, owned_grads, new_params, new_first, new_second)


BF = jnp.bfloat16
F32 = jnp.float32
PLANES = 4
PART = D // PLANES
SPOT = 96
SLAB = 352
STARTS = (0, 80, 176, 256)


def dot_nn(a, b):
    return lax.dot_general(a, b, (((1,), (0,)), ((), ())), preferred_element_type=F32)


def dot_nt(a, b):
    return lax.dot_general(a, b, (((1,), (1,)), ((), ())), preferred_element_type=F32)


def dot_tn(a, b):
    return lax.dot_general(a, b, (((0,), (0,)), ((), ())), preferred_element_type=F32)


def lanes_of(width):
    return lax.broadcasted_iota(jnp.int32, (1, width), 1)


def group_mask(index, width=D, size=PART):
    lane = lanes_of(width)
    return (lane >= index * size) & (lane < (index + 1) * size)


def turned(value, shift):
    shift = shift % value.shape[-1]
    return value if shift == 0 else pltpu.roll(value, shift, value.ndim - 1)


def spread_groups(parts, first):
    total = None
    for group, part in enumerate(parts):
        moved = jnp.where(group_mask(group), turned(part, PART * (group - first)), 0.0)
        total = moved if total is None else total + moved
    return total


def every(size, stride, first):
    row = lax.broadcasted_iota(jnp.int32, (size, SPOT), 0)
    col = lax.broadcasted_iota(jnp.int32, (size, SPOT), 1)
    return jnp.where(col == stride * row + first, 1.0, 0.0).astype(BF)


def permutations():
    place = jnp.arange(D)
    part, inner = place // PART, place % PART
    hidden_from = SPOT * (inner // 24) + 24 * part + inner % 24
    kind = inner // HEAD_DIM
    head = jnp.where(
        part < 3,
        part + jnp.where(kind == 0, 0, jnp.where(kind == 1, 5, 9)),
        jnp.where(kind == 0, 3, jnp.where(kind == 1, 4, 8)),
    )
    head_from = HEAD_DIM * head + inner % HEAD_DIM
    rows = place[:, None]
    return (
        (rows == head_from[None]).astype(BF),
        (rows == hidden_from[None]).astype(BF),
    )


def pack_kernel(where_ref, rows_ref, tail_ref, heads_ref, hidden_ref, *outs):
    out_refs, spot = outs[:PLANES], outs[PLANES]
    plane, place = where_ref[0], where_ref[1]
    device = 8 * plane + place
    spot[...] = jnp.zeros_like(spot)
    for i in range(3):
        block = 3 * device + i

        @pl.when(block < 24)
        def _():
            for j in range(3):
                picked = dot_nn(every(32, 3, j), rows_ref[SPOT * i : SPOT * i + SPOT, :].astype(BF))
                sorted_ = dot_nn(picked.astype(BF), heads_ref[...])
                parts = [sorted_[8 * g : 8 * g + 8] for g in range(4)]
                for s in range(PLANES):
                    spot[s, 24 * i + 8 * j : 24 * i + 8 * j + 8, :] = spread_groups(parts, s)

        @pl.when((block >= 32) & (block < 64))
        def _():
            source = rows_ref[SPOT * i : SPOT * i + SPOT, :].astype(BF)
            parts = [
                dot_nn(dot_nn(every(24, 4, j), source).astype(BF), hidden_ref[...])
                for j in range(4)
            ]
            for s in range(PLANES):
                value = spread_groups(parts, s)
                if i < 2:
                    spot[s, 24 * i : 24 * i + 24, :] = value
                else:
                    mixed = block == 32

                    @pl.when(mixed)
                    def _():
                        spot[s, 0:24, :] = value

                    @pl.when(jnp.logical_not(mixed))
                    def _():
                        spot[s, 48:72, :] = value

        @pl.when(block >= 64)
        def _():
            for s in range(PLANES):
                spot[s, 24 * i : 24 * i + 24, :] = rows_ref[
                    SPOT * i + 24 * s : SPOT * i + 24 * s + 24, :
                ]

    @pl.when(device == 8)
    def _():
        for s in range(3):
            spot[s, 0:64, :] = rows_ref[64 * s : 64 * s + 64, :]
        spot[3, 0:96, :] = rows_ref[192:288, :]

    @pl.when(device == 9)
    def _():
        for s in range(3):
            spot[s, 0:64, :] = rows_ref[32 + 64 * s : 96 + 64 * s, :]
        spot[3, 0:32, :] = rows_ref[0:32, :]
        spot[3, 32:96, :] = rows_ref[224:288, :]

    @pl.when(device == 10)
    def _():
        for s in range(3):
            spot[s, 24:88, :] = rows_ref[64 * s : 64 * s + 64, :]

    @pl.when(device == 31)
    def _():
        upper = tail_ref[0:8, :].astype(BF)
        by_head = dot_nn(upper, heads_ref[...])
        by_hidden = dot_nn(upper, hidden_ref[...])
        for s in range(PLANES):
            spot[s, 72:73, :] = spread_groups([by_hidden[4 + j : 5 + j] for j in range(4)], s)
            spot[s, 73:74, :] = spread_groups([by_head[j : j + 1] for j in range(3)], s)
            spot[s, 74:75, :] = tail_ref[3:4, :]
            spot[s, 80:88, :] = tail_ref[8:16, :]

    for r in range(PLANES):
        out_refs[r][...] = spot[plane ^ r].astype(BF)


def unpack_kernel(where_ref, *refs):
    in_refs, (heads_ref, hidden_ref, rows_ref, tail_ref, spot) = refs[:PLANES], refs[PLANES:]
    plane, place = where_ref[0], where_ref[1]
    device = 8 * plane + place
    for r in range(PLANES):
        spot[plane ^ r] = in_refs[r][...].astype(F32)
    for i in range(3):
        block = 3 * device + i

        @pl.when(block < 24)
        def _():
            total = None
            for j in range(3):
                base = 24 * i + 8 * j
                parts = [spot[s, base : base + 8, :] for s in range(PLANES)]
                sorted_ = jnp.concatenate([spread_groups(parts, g) for g in range(4)], axis=0)
                picked = dot_nt(sorted_.astype(BF), heads_ref[...]).astype(BF)
                value = dot_tn(every(32, 3, j), picked)
                total = value if total is None else total + value
            rows_ref[SPOT * i : SPOT * i + SPOT, :] = total

        @pl.when((block >= 32) & (block < 64))
        def _():
            start = 24 * i
            if i == 2:
                start = pl.multiple_of(jnp.where(block == 32, 0, 48), 8)
            parts = [spot[s, pl.ds(start, 24), :] for s in range(PLANES)]
            total = None
            for j in range(4):
                picked = dot_nt(spread_groups(parts, j).astype(BF), hidden_ref[...]).astype(BF)
                value = dot_tn(every(24, 4, j), picked)
                total = value if total is None else total + value
            rows_ref[SPOT * i : SPOT * i + SPOT, :] = total

        @pl.when(block >= 64)
        def _():
            for s in range(PLANES):
                rows_ref[SPOT * i + 24 * s : SPOT * i + 24 * s + 24, :] = spot[
                    s, 24 * i : 24 * i + 24, :
                ]

    @pl.when(device == 8)
    def _():
        for s in range(3):
            rows_ref[64 * s : 64 * s + 64, :] = spot[s, 0:64, :]
        rows_ref[192:288, :] = spot[3, 0:96, :]

    @pl.when(device == 9)
    def _():
        for s in range(3):
            rows_ref[32 + 64 * s : 96 + 64 * s, :] = spot[s, 0:64, :]
        rows_ref[0:32, :] = spot[3, 0:32, :]
        rows_ref[224:288, :] = spot[3, 32:96, :]

    @pl.when(device == 10)
    def _():
        for s in range(3):
            rows_ref[64 * s : 64 * s + 64, :] = spot[s, 24:88, :]

    tail_ref[...] = jnp.zeros_like(tail_ref)

    @pl.when(device == 31)
    def _():
        whole = [spot[s, 72:73, :] for s in range(PLANES)]
        for j in range(4):
            row = jnp.broadcast_to(spread_groups(whole, j), (8, D)).astype(BF)
            tail_ref[4 + j : 5 + j, :] = dot_nt(row, hidden_ref[...])[0:1]
        whole = [spot[s, 73:74, :] for s in range(PLANES)]
        for j in range(3):
            row = jnp.broadcast_to(spread_groups(whole, j), (8, D)).astype(BF)
            tail_ref[j : j + 1, :] = dot_nt(row, heads_ref[...])[0:1]
        tail_ref[3:4, :] = sum(spot[s, 74:75, :] for s in range(PLANES))
        tail_ref[8:16, :] = sum(spot[s, 80:88, :] for s in range(PLANES))


def slab_start(plane):
    start = jnp.where(plane == 1, STARTS[1], jnp.where(plane == 2, STARTS[2], STARTS[3]))
    return pl.multiple_of(jnp.where(plane == 0, 0, start), 16)


def slab_kernel(where_ref, a_ref, b_ref, c_ref, d_ref, out_ref):
    for r, ref in enumerate((a_ref, b_ref, c_ref, d_ref)):
        source = where_ref[0] ^ r
        out_ref[pl.ds(slab_start(source), 80), :] = ref[0:80, :]

        @pl.when((source == 1) | (source == 3))
        def _():
            out_ref[pl.ds(slab_start(source) + 80, 16), :] = ref[80:96, :]


def split_kernel(where_ref, a_ref, b_ref, c_ref, d_ref, *outs):
    out_refs, total = outs[:PLANES], outs[PLANES]
    total[...] = (a_ref[...].astype(F32) + b_ref[...].astype(F32)) + (
        c_ref[...].astype(F32) + d_ref[...].astype(F32)
    )
    for r in range(PLANES):
        out_refs[r][...] = total[pl.ds(slab_start(where_ref[0] ^ r), SPOT), :].astype(BF)


def layer_kernel(where_ref, *refs):
    act_refs, slab_refs = refs[:4], refs[4:12]
    grad_refs, back_refs = refs[12:20], refs[20:24]
    (w_up, w_down, w_out, packed, w_qkv, tails, bf_up, bf_down, bf_out, bf_qkv, normed, grad_y,
     qkv, attn, g_qkv, g_attn, up, slab) = refs[24:]
    plane, spot, core = where_ref[0], where_ref[1], where_ref[2]
    lane = lanes_of(D)

    def place_of(index):
        return 2 * (spot ^ (index % 4)) + (core if index < 4 else 1 - core)

    w_out[...] = jnp.zeros_like(w_out)
    for index, ref in enumerate(slab_refs):
        q = place_of(index)
        for i in range(3):
            for j in range(3):
                packed[j, pl.ds(pl.multiple_of(24 * q + 8 * i, 8), 8), :] = ref[0:80, :][
                    24 * i + 8 * j : 24 * i + 8 * j + 8
                ].astype(F32)
        one = ref[80:176, :].astype(F32)
        two = ref[176:256, :].astype(F32)
        three = ref[256:352, :].astype(F32)

        @pl.when(q >= 3)
        def _():
            w_up[pl.ds(pl.multiple_of(72 * q - 192, 8), 72), :] = one[0:72]

        @pl.when(q == 2)
        def _():
            w_up[0:24, :] = one[0:24]

            @pl.when(plane < 3)
            def _():
                w_out[128:192, :] = one[24:88]

        @pl.when((q < 2) & (plane < 3))
        def _():
            w_out[pl.ds(pl.multiple_of(64 * q, 8), 64), :] = one[0:64]

        @pl.when((q < 2) & (plane == 3))
        def _():
            w_out[pl.ds(pl.multiple_of(96 * q, 8), 96), :] = one[0:96]

        @pl.when(q < 5)
        def _():
            w_up[pl.ds(pl.multiple_of(384 + 72 * q, 8), 72), :] = two[0:72]

        @pl.when(q == 5)
        def _():
            w_up[744:768, :] = two[0:24]
            w_down[0:48, :] = two[24:72]

        @pl.when(q > 5)
        def _():
            w_down[pl.ds(pl.multiple_of(72 * q - 384, 8), 72), :] = two[0:72]

        w_down[pl.ds(pl.multiple_of(192 + 72 * q, 8), 72), :] = three[0:72]

        @pl.when(q == 7)
        def _():
            tails[...] = three[72:88]

    for j in range(3):
        for i in range(4):
            moved = turned(packed[j], -PART * i)[:, 0:256]
            moved = jnp.where(lanes_of(256) < PART, moved, 0.0)
            w_qkv[:, i, :, 256 * j : 256 * j + 256] = moved.reshape(24, 8, 256)
    bf_up[...] = w_up[...].astype(BF)
    bf_down[...] = w_down[...].astype(BF)
    bf_out[...] = w_out[...].astype(BF)
    bf_qkv[...] = w_qkv[...].reshape(D, D).astype(BF)

    for r in range(4):
        normed[128 * r : 128 * r + 128, :] = act_refs[r][0:128, :]
        grad_y[128 * r : 128 * r + 128, :] = act_refs[r][128:256, :]
    bias_up = tails[0:1, :]
    flat_bias = tails[1:2, :]
    bias_qkv = jnp.zeros((1, D), F32)
    for j in range(3):
        keep = (lane >= 256 * j) & (lane < 256 * j + PART)
        bias_qkv = jnp.where(keep, turned(flat_bias, 64 * j), bias_qkv)
    bias_y = jnp.where(plane == 0, tails[2:3, :] + tails[8:9, :], 0.0)
    gain_one, shift_one = tails[9:10, :], tails[10:11, :]
    gain_two, shift_two = tails[11:12, :], tails[12:13, :]

    def act_of(gain, shift):
        return (normed[...].astype(F32) * gain + shift).astype(BF)

    act_one = act_of(gain_one, shift_one)
    qkv[...] = dot_nn(act_one, bf_qkv[...]) + bias_qkv
    g_attn[...] = dot_nt(grad_y[...], bf_out[...]).astype(BF)

    rows = lax.broadcasted_iota(jnp.int32, (128, 128), 0)
    cols = lax.broadcasted_iota(jnp.int32, (128, 128), 1)
    same_block = (rows < 64) == (cols < 64)
    eye = rows == cols
    in_head = lanes_of(128) % 64
    freq = jnp.exp((in_head % 8).astype(F32) * (-2.0 * math.log(10000.0) / ROT))
    low_half = lanes_of(128) < 64
    for r in range(4):
        span = slice(128 * r, 128 * r + 128)
        seg_row = jnp.broadcast_to(act_refs[r][256:272, 0:128].astype(F32)[0:1], (128, 128))
        seg_col = jnp.sum(jnp.where(eye, seg_row, 0.0), axis=1, keepdims=True)
        same = (seg_col == seg_row) & same_block
        allowed = same & (cols <= rows) & ((seg_col >= 0.0) | eye)
        position = jnp.sum(jnp.where(same & (cols < rows), 1.0, 0.0), axis=1, keepdims=True)
        angle = position * freq
        cos_t = jnp.where(in_head < ROT, jnp.cos(angle), 1.0)
        sine = jnp.sin(angle)
        sin_a = jnp.where(in_head < 8, sine, 0.0)
        sin_b = jnp.where((in_head >= 8) & (in_head < ROT), sine, 0.0)

        def rotated(x):
            return x * cos_t - turned(x, -8) * sin_a + turned(x, 8) * sin_b

        def unrotated(x):
            return x * cos_t + turned(x, -8) * sin_a - turned(x, 8) * sin_b

        for tile in range(2):
            at = [256 * j + 128 * tile for j in range(3)]
            query = rotated(qkv[span, at[0] : at[0] + 128]).astype(BF)
            key = rotated(qkv[span, at[1] : at[1] + 128]).astype(BF)
            value = qkv[span, at[2] : at[2] + 128].astype(BF)
            g_out = g_attn[span, 128 * tile : 128 * tile + 128]
            parts = []
            for half in range(2 - tile):
                mask = low_half if half == 0 else jnp.logical_not(low_half)
                key_h = jnp.where(mask, key, jnp.zeros_like(key))
                value_h = jnp.where(mask, value, jnp.zeros_like(value))
                scores = dot_nt(query, key_h) * HEAD_DIM ** (-0.5)
                masked = jnp.where(allowed, scores, -1e30)
                top = jnp.max(masked, axis=1, keepdims=True)
                expo = jnp.where(allowed, jnp.exp(masked - top), 0.0)
                prob = expo * (1.0 / jnp.sum(expo, axis=1, keepdims=True))
                prob_bf = prob.astype(BF)
                g_prob = dot_nt(g_out, value_h)
                delta = jnp.sum(prob * g_prob, axis=1, keepdims=True)
                g_score = (prob * (g_prob - delta) * HEAD_DIM ** (-0.5)).astype(BF)
                parts.append(
                    (
                        dot_nn(prob_bf, value),
                        dot_tn(prob_bf, g_out),
                        dot_nn(g_score, key),
                        dot_tn(g_score, query),
                    )
                )
            if tile == 0:
                o, gv, gq, gk = [jnp.where(low_half, a, b) for a, b in zip(*parts)]
            else:
                o, gv, gq, gk = [jnp.where(low_half, a, 0.0) for a in parts[0]]
            attn[span, 128 * tile : 128 * tile + 128] = o.astype(BF)
            g_qkv[span, at[0] : at[0] + 128] = unrotated(gq)
            g_qkv[span, at[1] : at[1] + 128] = unrotated(gk)
            g_qkv[span, at[2] : at[2] + 128] = gv
    y = dot_nn(attn[...], bf_out[...]) + bias_y
    grad_out = dot_tn(attn[...], grad_y[...])
    g_bias_qkv = jnp.sum(g_qkv[...], axis=0, keepdims=True)
    g_qkv_bf = g_qkv[...].astype(BF)
    w_qkv[...] = dot_tn(act_one, g_qkv_bf).reshape(24, 4, 8, D)
    g_act_one = dot_nt(g_qkv_bf, bf_qkv[...])
    w_out[...] = grad_out

    act_two = act_of(gain_two, shift_two)
    up[...] = dot_nn(act_two, bf_up[...]) + bias_up
    cdf = 0.5 * (1.0 + lax.erf(up[...] * 0.7071067811865476))
    hidden = (up[...] * cdf).astype(BF)
    y = y + dot_nn(hidden, bf_down[...])
    for r in range(4):
        back_refs[r][0:128, :] = y[128 * r : 128 * r + 128].astype(BF)
    w_down[...] = dot_tn(hidden, grad_y[...])
    pdf = jnp.exp(-0.5 * up[...] * up[...]) * 0.3989422804014327
    g_up = dot_nt(grad_y[...], bf_down[...]) * (cdf + up[...] * pdf)
    g_bias_up = jnp.sum(g_up, axis=0, keepdims=True)
    g_up_bf = g_up.astype(BF)
    w_up[...] = dot_tn(act_two, g_up_bf)
    g_act_two = dot_nt(g_up_bf, bf_up[...])
    wide = normed[...].astype(F32)
    for r in range(4):
        span = slice(128 * r, 128 * r + 128)
        back_refs[r][128:256, :] = (g_act_one[span] * gain_one + g_act_two[span] * gain_two).astype(BF)

    def row_sum(x):
        return jnp.sum(x, axis=0, keepdims=True)

    g_bias_y = row_sum(grad_y[0:128, :].astype(F32))
    flat_bias = jnp.zeros((1, D), F32)
    for j in range(3):
        keep = (lane >= PART * j) & (lane < PART * (j + 1))
        flat_bias = jnp.where(keep, turned(g_bias_qkv, -64 * j), flat_bias)
    tails[...] = jnp.zeros_like(tails)
    tails[0:1, :] = g_bias_up
    tails[1:2, :] = flat_bias
    tails[2:3, :] = g_bias_y
    tails[8:9, :] = g_bias_y
    tails[9:10, :] = row_sum(g_act_one * wide)
    tails[10:11, :] = row_sum(g_act_one)
    tails[11:12, :] = row_sum(g_act_two * wide)
    tails[12:13, :] = row_sum(g_act_two)

    for j in range(3):
        total = None
        for i in range(4):
            piece = w_qkv[:, i, :, 256 * j : 256 * j + 256].reshape(PART, 256)
            piece = jnp.where(lanes_of(256) < PART, piece, 0.0)
            piece = jnp.concatenate([piece, jnp.zeros((PART, 512), F32)], axis=1)
            piece = turned(piece, PART * i)
            total = piece if total is None else total + piece
        packed[j] = total
    for index, ref in enumerate(grad_refs):
        q = place_of(index)
        for i in range(3):
            for j in range(3):
                slab[24 * i + 8 * j : 24 * i + 8 * j + 8, :] = packed[
                    j, pl.ds(pl.multiple_of(24 * q + 8 * i, 8), 8), :
                ]

        @pl.when(q >= 3)
        def _():
            slab[80:152, :] = w_up[pl.ds(pl.multiple_of(72 * q - 192, 8), 72), :]

        @pl.when(q == 2)
        def _():
            slab[80:104, :] = w_up[0:24, :]
            slab[104:168, :] = w_out[128:192, :]

        @pl.when((q < 2) & (plane < 3))
        def _():
            slab[80:144, :] = w_out[pl.ds(pl.multiple_of(64 * q, 8), 64), :]

        @pl.when((q < 2) & (plane == 3))
        def _():
            slab[80:176, :] = w_out[pl.ds(pl.multiple_of(96 * q, 8), 96), :]

        @pl.when(q < 5)
        def _():
            slab[176:248, :] = w_up[pl.ds(pl.multiple_of(384 + 72 * q, 8), 72), :]

        @pl.when(q == 5)
        def _():
            slab[176:200, :] = w_up[744:768, :]
            slab[200:248, :] = w_down[0:48, :]

        @pl.when(q > 5)
        def _():
            slab[176:248, :] = w_down[pl.ds(pl.multiple_of(72 * q - 384, 8), 72), :]

        slab[256:328, :] = w_down[pl.ds(pl.multiple_of(192 + 72 * q, 8), 72), :]
        slab[328:344, :] = tails[...]
        ref[...] = slab[...].astype(BF)


def local_call(kernel, outs, scratch, *operands):
    vmem = pl.BlockSpec(memory_space=pltpu.VMEM)
    return pl.pallas_call(
        kernel,
        out_shape=outs,
        in_specs=[pl.BlockSpec(memory_space=pltpu.SMEM)] + [vmem] * (len(operands) - 1),
        out_specs=jax.tree.map(lambda _: vmem, outs),
        scratch_shapes=scratch,
    )(*operands)


def sliced_step(planes, places, *args):
    return sliced_body(planes, places, *args)


def sliced_body(planes, places, block_input, out_grad, seg_ids, params, first_moment, second_moment):
    count = planes * places * 2
    spread = TAIL // count
    dp, core = lax.axis_index("dp"), lax.axis_index("fsdp")
    plane, spot = dp // places, dp % places
    where_owner = jnp.stack([plane, 2 * spot + core]).astype(jnp.int32)
    where_spot = jnp.stack([plane, spot, core]).astype(jnp.int32)
    across = [
        [(i, (i // places ^ r) * places + i % places) for i in range(planes * places)]
        for r in range(planes)
    ]
    within = [
        [(i, i // places * places + (i % places ^ r)) for i in range(planes * places)]
        for r in range(places)
    ]

    def to_plane(value, r):
        return lax.ppermute(value, "dp", across[r]) if r else value

    def to_spot(value, r):
        return lax.ppermute(value, "dp", within[r]) if r else value

    def to_core(value):
        return lax.ppermute(value, "fsdp", [(0, 1), (1, 0)])

    micro, row_count, _ = block_input.shape
    tokens = micro * row_count
    flat_x = block_input.reshape(tokens, D)
    mean = jnp.mean(flat_x, axis=-1, keepdims=True)
    centred = flat_x - mean
    inv_std = lax.rsqrt(jnp.mean(centred * centred, axis=-1, keepdims=True) + NORM_EPS)
    normed = centred * inv_std
    valid = (seg_ids >= 0).astype(F32).reshape(tokens, 1)
    grad_y = out_grad.reshape(tokens, D) * valid
    seg_rows = jnp.pad(seg_ids.reshape(1, tokens).astype(BF), ((0, 15), (0, D - tokens)))
    sent_acts = jnp.concatenate([normed.astype(BF), grad_y.astype(BF), seg_rows])
    acts = [to_plane(sent_acts, r) for r in range(3)]
    acts.append(to_plane(acts[2], 1))

    heads, hidden = permutations()
    rows, tail = rows_from_flat(params, spread, count)
    tail = jnp.pad(tail, ((0, 3), (0, 0)))
    spot_shape = jax.ShapeDtypeStruct((SPOT, D), BF)
    slab_shape = jax.ShapeDtypeStruct((SLAB, D), BF)
    spots = local_call(
        pack_kernel, [spot_shape] * planes, [pltpu.VMEM((planes, SPOT, D), F32)],
        where_owner, rows, tail, heads, hidden,
    )
    spots = [to_plane(spots[r], r) for r in range(planes)]
    slab = local_call(slab_kernel, slab_shape, [], where_owner, *spots)
    slabs = [to_spot(slab, r) for r in range(places)]
    slabs = slabs + [to_core(s) for s in slabs]

    total = planes * tokens
    outs = local_call(
        layer_kernel,
        [slab_shape] * 8 + [jax.ShapeDtypeStruct((2 * tokens, D), BF)] * planes,
        [
            pltpu.VMEM((D, D), F32),
            pltpu.VMEM((D, D), F32),
            pltpu.VMEM((256, D), F32),
            pltpu.VMEM((3, PART, D), F32),
            pltpu.VMEM((24, 4, 8, D), F32),
            pltpu.VMEM((16, D), F32),
            pltpu.VMEM((D, D), BF),
            pltpu.VMEM((D, D), BF),
            pltpu.VMEM((256, D), BF),
            pltpu.VMEM((D, D), BF),
            pltpu.VMEM((total, D), BF),
            pltpu.VMEM((total, D), BF),
            pltpu.VMEM((total, D), F32),
            pltpu.VMEM((total, 256), BF),
            pltpu.VMEM((total, D), F32),
            pltpu.VMEM((total, 256), BF),
            pltpu.VMEM((total, D), F32),
            pltpu.VMEM((SLAB, D), F32),
        ],
        where_spot, *acts, *slabs,
    )
    grads, backs = outs[:8], outs[8:]
    paired = [
        (grads[r].astype(F32) + to_core(grads[4 + r]).astype(F32)).astype(BF) for r in range(places)
    ]
    arrived = [to_spot(paired[r], r) for r in range(places)]
    passed = to_plane(backs[3], 1)
    backs = [
        backs[0],
        to_plane(backs[1], 1),
        to_plane((backs[2].astype(F32) + passed.astype(F32)).astype(BF), 2),
    ]
    spots = local_call(
        split_kernel, [spot_shape] * planes, [pltpu.VMEM((SLAB, D), F32)], where_owner, *arrived
    )
    spots = [to_plane(spots[r], r) for r in range(planes)]
    grad_rows, grad_tail = local_call(
        unpack_kernel,
        [
            jax.ShapeDtypeStruct(rows.shape, F32),
            jax.ShapeDtypeStruct((16, D), F32),
        ],
        [pltpu.VMEM((planes, SPOT, D), F32)],
        where_owner, *spots, heads, hidden,
    )
    back = sum(b.astype(F32) for b in backs)
    result = flat_x + back[:tokens]
    scaled = back[tokens:]
    input_grad = grad_y + inv_std * (
        scaled
        - jnp.mean(scaled, axis=-1, keepdims=True)
        - normed * jnp.mean(scaled * normed, axis=-1, keepdims=True)
    )
    owned = flat_from_rows(grad_rows, grad_tail[:13], spread, count)
    new_params, new_first, new_second = adam_update(params, owned, first_moment, second_moment)
    return (
        result.reshape(block_input.shape),
        input_grad.reshape(block_input.shape),
        owned,
        new_params,
        new_first,
        new_second,
    )


def solution(mesh):
    vector, tokens = P(AXES), P(None, AXES, None)
    dp, cores = mesh.shape["dp"], mesh.shape["fsdp"]
    if dp == PLANES * PLANES and cores == 2:
        step = functools.partial(sliced_step, PLANES, dp // PLANES)
    else:
        step = functools.partial(body, dp * cores)
    return jax.shard_map(
        step,
        mesh=mesh,
        in_specs=(tokens, tokens, P(None, AXES), vector, vector, vector),
        out_specs=(tokens, tokens, vector, vector, vector, vector),
        check_vma=False,
    )
```

```python
import functools
import math

import jax
import jax.numpy as jnp
from jax import lax
from jax.experimental import pallas as pl
from jax.experimental.pallas import tpu as pltpu
from jax.sharding import PartitionSpec as P


D = 768
FF = 3072
HEADS = 12
HEAD_DIM = 64
ROT = 16
STEP = 3


NORM_EPS = 1e-05
BETA_ONE = 0.9
BETA_TWO = 0.95
LEARN_RATE = 0.05
WEIGHT_DECAY = 0.1
ADAM_EPS = 1e-08


def layout_shapes():
    return [
        (D, 3 * D),
        (D, D),
        (D, FF),
        (FF, D),
        (3 * D,),
        (D,),
        (FF,),
        (D,),
        (D,),
        (D,),
        (D,),
        (D,),
    ]


def unpack_flat(flat_vec):
    pieces_out = []
    offset = 0
    for item_shape in layout_shapes():
        length = math.prod(item_shape)
        pieces_out.append(flat_vec[offset : offset + length].reshape(item_shape))
        offset += length
    return pieces_out


def product(form, left, right):
    return jnp.einsum(form, left, right, preferred_element_type=jnp.float32)


def block_tables(seg_rows):
    row_count = seg_rows.shape[1]
    row_idx = jnp.arange(row_count)
    same_seq = seg_rows[:, :, None] == seg_rows[:, None, :]
    earlier = row_idx[None, :] < row_idx[:, None]
    diagonal = row_idx[None, :] == row_idx[:, None]
    causal = row_idx[None, :] <= row_idx[:, None]
    allowed = same_seq & causal[None] & ((seg_rows[:, :, None] >= 0) | diagonal[None])
    position = jnp.sum(jnp.where(same_seq & earlier[None], 1, 0), axis=2).astype(jnp.float32)
    inv_freq = 10000.0 ** (-(jnp.arange(ROT // 2, dtype=jnp.float32) * 2.0) / ROT)
    angles = position[:, :, None] * inv_freq[None, None, :]
    return (allowed, jnp.cos(angles)[:, :, None, :], jnp.sin(angles)[:, :, None, :])


def rotate(vecs, cos_t, sin_t):
    half_rot = ROT // 2
    first = vecs[..., :half_rot]
    second = vecs[..., half_rot:ROT]
    return jnp.concatenate(
        [first * cos_t - second * sin_t, second * cos_t + first * sin_t, vecs[..., ROT:]], axis=-1
    )


def unrotate(vecs, cos_t, sin_t):
    half_rot = ROT // 2
    first = vecs[..., :half_rot]
    second = vecs[..., half_rot:ROT]
    return jnp.concatenate(
        [first * cos_t + second * sin_t, second * cos_t - first * sin_t, vecs[..., ROT:]], axis=-1
    )


def layer_norm(flat_x, gain, shift):
    row_mean = jnp.mean(flat_x, axis=-1, keepdims=True)
    centred = flat_x - row_mean
    row_var = jnp.mean(centred * centred, axis=-1, keepdims=True)
    inv_std = lax.rsqrt(row_var + NORM_EPS)
    normed = centred * inv_std
    return (
        normed,
        inv_std,
        (normed * gain.astype(jnp.float32) + shift.astype(jnp.float32)).astype(jnp.bfloat16),
    )


def norm_back(grad_act, normed, inv_std, gain):
    grad_gain = jnp.sum(grad_act * normed, axis=0)
    grad_shift = jnp.sum(grad_act, axis=0)
    scaled = grad_act * gain.astype(jnp.float32)
    grad_in = inv_std * (
        scaled
        - jnp.mean(scaled, axis=-1, keepdims=True)
        - normed * jnp.mean(scaled * normed, axis=-1, keepdims=True)
    )
    return (grad_gain, grad_shift, grad_in)


def softmax_rows(query_bf, key_bf, allowed, log_total):
    scores = product("gqhd,gkhd->ghqk", query_bf, key_bf) * HEAD_DIM ** (-0.5)
    mask_b = allowed[:, None]
    masked = jnp.where(mask_b, scores, -jnp.inf)
    if log_total is None:
        top_score = jnp.max(masked, axis=-1, keepdims=True)
        expo = jnp.where(mask_b, jnp.exp(masked - top_score), 0.0)
        log_total = top_score + jnp.log(jnp.sum(expo, axis=-1, keepdims=True))
    prob_rows = jnp.where(mask_b, jnp.exp(masked - log_total), 0.0)
    return (prob_rows, log_total)


def forward(x_rows, seg_rows, weights):
    (
        w_qkv,
        w_out,
        w_up,
        w_down,
        b_qkv,
        b_out,
        b_up,
        b_down,
        gain_one,
        shift_one,
        gain_two,
        shift_two,
    ) = weights
    group_count, row_count = seg_rows.shape
    allowed, cos_t, sin_t = block_tables(seg_rows)
    flat_x = x_rows.reshape(group_count * row_count, D)
    normed_one, inv_one, act_one = layer_norm(flat_x, gain_one, shift_one)
    normed_two, inv_two, act_two = layer_norm(flat_x, gain_two, shift_two)
    qkv_rows = jnp.dot(act_one, w_qkv, preferred_element_type=jnp.float32) + b_qkv.astype(
        jnp.float32
    )
    qkv_rows = qkv_rows.reshape(group_count, row_count, 3, HEADS, HEAD_DIM)
    query_bf = rotate(qkv_rows[:, :, 0], cos_t, sin_t).astype(jnp.bfloat16)
    key_bf = rotate(qkv_rows[:, :, 1], cos_t, sin_t).astype(jnp.bfloat16)
    value_bf = qkv_rows[:, :, 2].astype(jnp.bfloat16)
    prob_rows, log_total = softmax_rows(query_bf, key_bf, allowed, None)
    prob_bf = prob_rows.astype(jnp.bfloat16)
    attn_bf = (
        product("ghqk,gkhd->gqhd", prob_bf, value_bf)
        .astype(jnp.bfloat16)
        .reshape(group_count * row_count, D)
    )
    attn_out = jnp.dot(attn_bf, w_out, preferred_element_type=jnp.float32) + b_out.astype(
        jnp.float32
    )
    up_rows = jnp.dot(act_two, w_up, preferred_element_type=jnp.float32) + b_up.astype(jnp.float32)
    hidden_bf = jax.nn.gelu(up_rows, approximate=False).astype(jnp.bfloat16)
    mlp_out = jnp.dot(hidden_bf, w_down, preferred_element_type=jnp.float32) + b_down.astype(
        jnp.float32
    )
    result = flat_x + attn_out + mlp_out
    kept_state = (
        normed_one,
        inv_one,
        act_one,
        normed_two,
        inv_two,
        act_two,
        query_bf,
        key_bf,
        value_bf,
        log_total,
        attn_bf,
        up_rows,
        hidden_bf,
        allowed,
        cos_t,
        sin_t,
        seg_rows,
    )
    return (result.reshape(group_count, row_count, D), kept_state)


def backward(kept_state, grad_rows, weights):
    (w_qkv, w_out, w_up, w_down, _, _, _, _, gain_one, _, gain_two, _) = weights
    (
        normed_one,
        inv_one,
        act_one,
        normed_two,
        inv_two,
        act_two,
        query_bf,
        key_bf,
        value_bf,
        log_total,
        attn_bf,
        up_rows,
        hidden_bf,
        allowed,
        cos_t,
        sin_t,
        seg_rows,
    ) = kept_state
    group_count, row_count = seg_rows.shape
    valid = (seg_rows >= 0).astype(jnp.float32).reshape(group_count * row_count, 1)
    grad_y = grad_rows.reshape(group_count * row_count, D) * valid
    grad_y_bf = grad_y.astype(jnp.bfloat16)
    grad_bias = jnp.sum(grad_y, axis=0)
    grad_w_down = jnp.dot(hidden_bf.T, grad_y_bf, preferred_element_type=jnp.float32)
    grad_w_out = jnp.dot(attn_bf.T, grad_y_bf, preferred_element_type=jnp.float32)
    grad_hidden = jnp.dot(grad_y_bf, w_down.T, preferred_element_type=jnp.float32)
    cdf_part = 0.5 * (1.0 + jax.scipy.special.erf(up_rows * 0.7071067811865476))
    pdf_part = jnp.exp(-0.5 * up_rows * up_rows) * 0.3989422804014327
    grad_up = grad_hidden * (cdf_part + up_rows * pdf_part)
    grad_b_up = jnp.sum(grad_up, axis=0)
    grad_up_bf = grad_up.astype(jnp.bfloat16)
    grad_w_up = jnp.dot(act_two.T, grad_up_bf, preferred_element_type=jnp.float32)
    grad_act_two = jnp.dot(grad_up_bf, w_up.T, preferred_element_type=jnp.float32)
    grad_attn = jnp.dot(grad_y_bf, w_out.T, preferred_element_type=jnp.float32).astype(jnp.bfloat16)
    grad_attn = grad_attn.reshape(group_count, row_count, HEADS, HEAD_DIM)
    prob_rows, _ = softmax_rows(query_bf, key_bf, allowed, log_total)
    prob_bf = prob_rows.astype(jnp.bfloat16)
    grad_value = product("ghqk,gqhd->gkhd", prob_bf, grad_attn)
    grad_prob = product("gqhd,gkhd->ghqk", grad_attn, value_bf)
    delta_rows = jnp.sum(prob_rows * grad_prob, axis=-1, keepdims=True)
    grad_score_bf = (prob_rows * (grad_prob - delta_rows) * HEAD_DIM ** (-0.5)).astype(jnp.bfloat16)
    grad_query = unrotate(product("ghqk,gkhd->gqhd", grad_score_bf, key_bf), cos_t, sin_t)
    grad_key = unrotate(product("ghqk,gqhd->gkhd", grad_score_bf, query_bf), cos_t, sin_t)
    grad_qkv = jnp.stack([grad_query, grad_key, grad_value], axis=2).reshape(
        group_count * row_count, 3 * D
    )
    grad_b_qkv = jnp.sum(grad_qkv, axis=0)
    grad_qkv_bf = grad_qkv.astype(jnp.bfloat16)
    grad_w_qkv = jnp.dot(act_one.T, grad_qkv_bf, preferred_element_type=jnp.float32)
    grad_act_one = jnp.dot(grad_qkv_bf, w_qkv.T, preferred_element_type=jnp.float32)
    grad_gain_one, grad_shift_one, back_one = norm_back(grad_act_one, normed_one, inv_one, gain_one)
    grad_gain_two, grad_shift_two, back_two = norm_back(grad_act_two, normed_two, inv_two, gain_two)
    input_grad = (grad_y + back_one + back_two).reshape(group_count, row_count, D)
    grads = (
        grad_w_qkv,
        grad_w_out,
        grad_w_up,
        grad_w_down,
        grad_b_qkv,
        grad_bias,
        grad_b_up,
        grad_bias,
        grad_gain_one,
        grad_shift_one,
        grad_gain_two,
        grad_shift_two,
    )
    return (input_grad, grads)


def adam_update(params, grads, first_moment, second_moment):
    new_first = BETA_ONE * first_moment + (1.0 - BETA_ONE) * grads
    new_second = BETA_TWO * second_moment + (1.0 - BETA_TWO) * grads * grads
    first_hat = new_first / (1.0 - BETA_ONE**STEP)
    second_hat = new_second / (1.0 - BETA_TWO**STEP)
    new_params = params - LEARN_RATE * (
        first_hat / (jnp.sqrt(second_hat) + ADAM_EPS) + WEIGHT_DECAY * params
    )
    return (new_params, new_first, new_second)


AXES = ("dp", "fsdp")
TAIL = 13 * D


def rows_from_flat(flat, spread, count):
    me = lax.axis_index(AXES)
    tail = flat[flat.shape[0] - TAIL :]
    before = lax.ppermute(tail, AXES, [(i, (i + 1) % count) for i in range(count)])
    joined = jnp.concatenate([before, flat])
    rows = lax.dynamic_slice(joined, (TAIL - spread * me,), (flat.shape[0] - spread,))
    return rows.reshape(-1, D), tail.reshape(-1, D)


def flat_from_rows(rows, tail, spread, count):
    me = lax.axis_index(AXES)
    head = rows.reshape(-1)[:TAIL]
    after = lax.ppermute(head, AXES, [(i, (i - 1) % count) for i in range(count)])
    after = jnp.where(me == count - 1, tail.reshape(-1), after)
    joined = jnp.concatenate([rows.reshape(-1), after])
    return lax.dynamic_slice(joined, (spread * me,), (rows.size + spread,))


def body(count, block_input, out_grad, seg_ids, params, first_moment, second_moment):
    spread = TAIL // count
    row_count = (params.shape[0] - spread) // D
    rows, tail = rows_from_flat(params.astype(jnp.bfloat16), spread, count)
    sent = jnp.concatenate([rows, jnp.pad(tail, ((0, 3), (0, 0)))])
    whole = lax.all_gather(sent, AXES, axis=0, tiled=False)
    matrices = whole[:, :row_count].reshape(-1)
    weights = unpack_flat(jnp.concatenate([matrices, whole[count - 1, row_count : row_count + 13].reshape(-1)]))
    result, kept_state = forward(block_input, seg_ids, weights)
    back_x, grads = backward(kept_state, out_grad, weights)
    big = jnp.concatenate([g.astype(jnp.bfloat16).reshape(-1, D) for g in grads[:4]])
    small = jnp.concatenate([g.astype(jnp.bfloat16).reshape(-1, D) for g in grads[4:]])
    small = jnp.pad(small, ((0, 3), (0, 0)))
    spots = jnp.where(jnp.arange(count)[:, None, None] == count - 1, small[None], jnp.zeros((), jnp.bfloat16))
    out = jnp.concatenate([big.reshape(count, row_count, D), spots], axis=1)
    owned = lax.psum_scatter(out, AXES, scatter_dimension=0, tiled=False).astype(jnp.float32)
    owned_grads = flat_from_rows(owned[:row_count], owned[row_count : row_count + 13], spread, count)
    new_params, new_first, new_second = adam_update(params, owned_grads, first_moment, second_moment)
    return (result, back_x, owned_grads, new_params, new_first, new_second)


BF = jnp.bfloat16
F32 = jnp.float32
PLANES = 4
PART = D // PLANES
SPOT = 96
SLAB = 352
STARTS = (0, 80, 176, 256)


def dot_nn(a, b):
    return lax.dot_general(a, b, (((1,), (0,)), ((), ())), preferred_element_type=F32)


def dot_nt(a, b):
    return lax.dot_general(a, b, (((1,), (1,)), ((), ())), preferred_element_type=F32)


def dot_tn(a, b):
    return lax.dot_general(a, b, (((0,), (0,)), ((), ())), preferred_element_type=F32)


def lanes_of(width):
    return lax.broadcasted_iota(jnp.int32, (1, width), 1)


def group_mask(index, width=D, size=PART):
    lane = lanes_of(width)
    return (lane >= index * size) & (lane < (index + 1) * size)


def turned(value, shift):
    shift = shift % value.shape[-1]
    return value if shift == 0 else pltpu.roll(value, shift, value.ndim - 1)


def spread_groups(parts, first):
    total = None
    for group, part in enumerate(parts):
        moved = turned(part, PART * (group - first))
        total = moved if total is None else jnp.where(group_mask(group), moved, total)
    if len(parts) < PLANES:
        total = jnp.where(lanes_of(D) < PART * len(parts), total, 0.0)
    return total


def count_of(value, *limits):
    return sum(jnp.where(value >= limit, 1, 0) for limit in limits)


def pick_matrix(kinds, size):
    row = lax.broadcasted_iota(jnp.int32, (SPOT, SPOT), 0)
    col = lax.broadcasted_iota(jnp.int32, (SPOT, SPOT), 1)
    kind = count_of(row, *range(size, SPOT, size))
    return jnp.where(col == kinds * (row - size * kind) + kind, 1.0, 0.0).astype(BF)


def order_columns(perm_ref, by_head):
    place = lax.broadcasted_iota(jnp.int32, (8, D), 1)
    part = count_of(place, PART, 2 * PART, 3 * PART)
    inner = place - PART * part
    if by_head:
        kind = count_of(inner, HEAD_DIM, 2 * HEAD_DIM)
        early = part + jnp.where(kind == 0, 0, jnp.where(kind == 1, 5, 9))
        late = jnp.where(kind == 0, 3, jnp.where(kind == 1, 4, 8))
        source = HEAD_DIM * (jnp.where(part < 3, early, late) - kind) + inner
    else:
        run = count_of(inner, *range(24, PART, 24))
        source = (SPOT - 24) * run + 24 * part + inner
    row = lax.broadcasted_iota(jnp.int32, (D, D), 0)
    perm_ref[...] = jnp.where(row == source[0:1], 1.0, 0.0).astype(BF)


def pack_kernel(where_ref, rows_ref, tail_ref, *refs):
    out_refs, (spot, perm, mixed) = refs[:PLANES], refs[PLANES:]
    plane, place = where_ref[0], where_ref[1]
    device = 8 * plane + place
    with_heads = device < 8
    with_hidden = (device >= 10) & (device < 22)
    spot[...] = jnp.zeros_like(spot)
    pl.when(with_heads)(lambda: order_columns(perm, True))
    pl.when(with_hidden)(lambda: order_columns(perm, False))

    @pl.when(with_heads | with_hidden)
    def _():
        mixed[...] = dot_nn(rows_ref[...].astype(BF), perm[...]).astype(BF)

    @pl.when(with_heads)
    def _():
        sort = pick_matrix(3, 32)
        for i in range(3):
            picked = dot_nn(sort, mixed[SPOT * i : SPOT * i + SPOT, :])
            for j in range(3):
                parts = [picked[32 * j + 8 * g : 32 * j + 8 * g + 8] for g in range(4)]
                for s in range(PLANES):
                    spot[s, 24 * i + 8 * j : 24 * i + 8 * j + 8, :] = spread_groups(parts, s)

    for i in range(3):
        block = 3 * device + i

        @pl.when((block >= 32) & (block < 64))
        def _():
            picked = dot_nn(pick_matrix(4, 24), mixed[SPOT * i : SPOT * i + SPOT, :])
            parts = [picked[24 * j : 24 * j + 24] for j in range(4)]
            start = 24 * i
            if i == 2:
                start = pl.multiple_of(jnp.where(block == 32, 0, 48), 8)
            for s in range(PLANES):
                spot[s, pl.ds(start, 24), :] = spread_groups(parts, s)

        @pl.when(block >= 64)
        def _():
            for s in range(PLANES):
                spot[s, 24 * i : 24 * i + 24, :] = rows_ref[
                    SPOT * i + 24 * s : SPOT * i + 24 * s + 24, :
                ]

    @pl.when(device == 8)
    def _():
        for s in range(3):
            spot[s, 0:64, :] = rows_ref[64 * s : 64 * s + 64, :]
        spot[3, 0:96, :] = rows_ref[192:288, :]

    @pl.when(device == 9)
    def _():
        for s in range(3):
            spot[s, 0:64, :] = rows_ref[32 + 64 * s : 96 + 64 * s, :]
        spot[3, 0:32, :] = rows_ref[0:32, :]
        spot[3, 32:96, :] = rows_ref[224:288, :]

    @pl.when(device == 10)
    def _():
        for s in range(3):
            spot[s, 24:88, :] = rows_ref[64 * s : 64 * s + 64, :]

    @pl.when(device == 31)
    def _():
        upper = tail_ref[0:8, :].astype(BF)
        order_columns(perm, True)
        by_head = dot_nn(upper, perm[...])
        order_columns(perm, False)
        by_hidden = dot_nn(upper, perm[...])
        for s in range(PLANES):
            spot[s, 72:73, :] = spread_groups([by_hidden[4 + j : 5 + j] for j in range(4)], s)
            spot[s, 73:74, :] = spread_groups([by_head[j : j + 1] for j in range(3)], s)
            spot[s, 74:75, :] = tail_ref[3:4, :]
            spot[s, 80:88, :] = tail_ref[8:16, :]

    for r in range(PLANES):
        out_refs[r][...] = spot[plane ^ r].astype(BF)


def unpack_kernel(where_ref, *refs):
    in_refs, (rows_ref, tail_ref, spot, perm, mixed) = refs[:PLANES], refs[PLANES:]
    plane, place = where_ref[0], where_ref[1]
    device = 8 * plane + place
    with_heads = device < 8
    with_hidden = (device >= 10) & (device < 22)
    for r in range(PLANES):
        spot[plane ^ r] = in_refs[r][...].astype(F32)
    pl.when(with_heads)(lambda: order_columns(perm, True))

    @pl.when(with_heads)
    def _():
        sort = pick_matrix(3, 32)
        for i in range(3):
            sorted_ = []
            for j in range(3):
                base = 24 * i + 8 * j
                parts = [spot[s, base : base + 8, :] for s in range(PLANES)]
                sorted_.extend(spread_groups(parts, g) for g in range(4))
            block_rows = jnp.concatenate(sorted_, axis=0).astype(BF)
            mixed[SPOT * i : SPOT * i + SPOT, :] = dot_tn(sort, block_rows).astype(BF)

    @pl.when(with_hidden)
    def _():
        order_columns(perm, False)
        mixed[...] = jnp.zeros_like(mixed)

    for i in range(3):
        block = 3 * device + i

        @pl.when((block >= 32) & (block < 64))
        def _():
            start = 24 * i
            if i == 2:
                start = pl.multiple_of(jnp.where(block == 32, 0, 48), 8)
            parts = [spot[s, pl.ds(start, 24), :] for s in range(PLANES)]
            block_rows = jnp.concatenate([spread_groups(parts, j) for j in range(4)], axis=0)
            mixed[SPOT * i : SPOT * i + SPOT, :] = dot_tn(
                pick_matrix(4, 24), block_rows.astype(BF)
            ).astype(BF)

    @pl.when(with_heads | with_hidden)
    def _():
        rows_ref[...] = dot_nt(mixed[...], perm[...])

    for i in range(3):

        @pl.when(3 * device + i >= 64)
        def _():
            for s in range(PLANES):
                rows_ref[SPOT * i + 24 * s : SPOT * i + 24 * s + 24, :] = spot[
                    s, 24 * i : 24 * i + 24, :
                ]

    @pl.when(device == 8)
    def _():
        for s in range(3):
            rows_ref[64 * s : 64 * s + 64, :] = spot[s, 0:64, :]
        rows_ref[192:288, :] = spot[3, 0:96, :]

    @pl.when(device == 9)
    def _():
        for s in range(3):
            rows_ref[32 + 64 * s : 96 + 64 * s, :] = spot[s, 0:64, :]
        rows_ref[0:32, :] = spot[3, 0:32, :]
        rows_ref[224:288, :] = spot[3, 32:96, :]

    @pl.when(device == 10)
    def _():
        for s in range(3):
            rows_ref[64 * s : 64 * s + 64, :] = spot[s, 24:88, :]

    tail_ref[...] = jnp.zeros_like(tail_ref)

    @pl.when(device == 31)
    def _():
        order_columns(perm, False)
        whole = [spot[s, 72:73, :] for s in range(PLANES)]
        for j in range(4):
            row = jnp.broadcast_to(spread_groups(whole, j), (8, D)).astype(BF)
            tail_ref[4 + j : 5 + j, :] = dot_nt(row, perm[...])[0:1]
        order_columns(perm, True)
        whole = [spot[s, 73:74, :] for s in range(PLANES)]
        for j in range(3):
            row = jnp.broadcast_to(spread_groups(whole, j), (8, D)).astype(BF)
            tail_ref[j : j + 1, :] = dot_nt(row, perm[...])[0:1]
        tail_ref[3:4, :] = sum(spot[s, 74:75, :] for s in range(PLANES))
        tail_ref[8:16, :] = sum(spot[s, 80:88, :] for s in range(PLANES))


def slab_start(plane):
    start = jnp.where(plane == 1, STARTS[1], jnp.where(plane == 2, STARTS[2], STARTS[3]))
    return pl.multiple_of(jnp.where(plane == 0, 0, start), 16)


def slab_kernel(where_ref, a_ref, b_ref, c_ref, d_ref, out_ref):
    for r, ref in enumerate((a_ref, b_ref, c_ref, d_ref)):
        source = where_ref[0] ^ r
        out_ref[pl.ds(slab_start(source), 80), :] = ref[0:80, :]

        @pl.when((source == 1) | (source == 3))
        def _():
            out_ref[pl.ds(slab_start(source) + 80, 16), :] = ref[80:96, :]


def split_kernel(where_ref, a_ref, b_ref, c_ref, d_ref, *outs):
    out_refs, total = outs[:PLANES], outs[PLANES]
    total[...] = (a_ref[...].astype(F32) + b_ref[...].astype(F32)) + (
        c_ref[...].astype(F32) + d_ref[...].astype(F32)
    )
    for r in range(PLANES):
        out_refs[r][...] = total[pl.ds(slab_start(where_ref[0] ^ r), SPOT), :].astype(BF)


def layer_kernel(where_ref, *refs):
    act_refs, cot_refs, slab_refs = refs[:4], refs[4:8], refs[8:16]
    grad_refs, back_refs = refs[16:24], refs[24:28]
    (w_up, w_down, w_out, packed, w_qkv, tails, bf_up, bf_down, bf_out, bf_qkv, normed, grad_y,
     qkv, attn, g_qkv, g_attn, up, slab) = refs[28:]
    plane, spot, core = where_ref[0], where_ref[1], where_ref[2]
    lane = lanes_of(D)

    def place_of(index):
        return 2 * (spot ^ (index % 4)) + (core if index < 4 else 1 - core)

    w_out[...] = jnp.zeros_like(w_out)
    for index, ref in enumerate(slab_refs):
        q = place_of(index)
        for i in range(3):
            for j in range(3):
                packed[j, pl.ds(pl.multiple_of(24 * q + 8 * i, 8), 8), :] = ref[0:80, :][
                    24 * i + 8 * j : 24 * i + 8 * j + 8
                ].astype(F32)
        one = ref[80:176, :].astype(F32)
        two = ref[176:256, :].astype(F32)
        three = ref[256:352, :].astype(F32)

        @pl.when(q >= 3)
        def _():
            w_up[pl.ds(pl.multiple_of(72 * q - 192, 8), 72), :] = one[0:72]

        @pl.when(q == 2)
        def _():
            w_up[0:24, :] = one[0:24]

            @pl.when(plane < 3)
            def _():
                w_out[128:192, :] = one[24:88]

        @pl.when((q < 2) & (plane < 3))
        def _():
            w_out[pl.ds(pl.multiple_of(64 * q, 8), 64), :] = one[0:64]

        @pl.when((q < 2) & (plane == 3))
        def _():
            w_out[pl.ds(pl.multiple_of(96 * q, 8), 96), :] = one[0:96]

        @pl.when(q < 5)
        def _():
            w_up[pl.ds(pl.multiple_of(384 + 72 * q, 8), 72), :] = two[0:72]

        @pl.when(q == 5)
        def _():
            w_up[744:768, :] = two[0:24]
            w_down[0:48, :] = two[24:72]

        @pl.when(q > 5)
        def _():
            w_down[pl.ds(pl.multiple_of(72 * q - 384, 8), 72), :] = two[0:72]

        w_down[pl.ds(pl.multiple_of(192 + 72 * q, 8), 72), :] = three[0:72]

        @pl.when(q == 7)
        def _():
            tails[...] = three[72:88]

    for j in range(3):
        for i in range(4):
            moved = turned(packed[j], -PART * i)[:, 0:256]
            moved = jnp.where(lanes_of(256) < PART, moved, 0.0)
            w_qkv[:, i, :, 256 * j : 256 * j + 256] = moved.reshape(24, 8, 256)
    bf_up[...] = w_up[...].astype(BF)
    bf_down[...] = w_down[...].astype(BF)
    bf_out[...] = w_out[...].astype(BF)
    bf_qkv[...] = w_qkv[...].reshape(D, D).astype(BF)

    for r in range(4):
        normed[128 * r : 128 * r + 128, :] = act_refs[r][0:128, :]
        grad_y[128 * r : 128 * r + 128, :] = cot_refs[r][...]
    bias_up = tails[0:1, :]
    flat_bias = tails[1:2, :]
    bias_qkv = jnp.zeros((1, D), F32)
    for j in range(3):
        keep = (lane >= 256 * j) & (lane < 256 * j + PART)
        bias_qkv = jnp.where(keep, turned(flat_bias, 64 * j), bias_qkv)
    bias_y = jnp.where(plane == 0, tails[2:3, :] + tails[8:9, :], 0.0)
    gain_one, shift_one = tails[9:10, :], tails[10:11, :]
    gain_two, shift_two = tails[11:12, :], tails[12:13, :]

    def act_of(gain, shift):
        return (normed[...].astype(F32) * gain + shift).astype(BF)

    act_one = act_of(gain_one, shift_one)
    qkv[...] = dot_nn(act_one, bf_qkv[...]) + bias_qkv
    g_attn[...] = dot_nt(grad_y[...], bf_out[...]).astype(BF)

    rows = lax.broadcasted_iota(jnp.int32, (128, 128), 0)
    cols = lax.broadcasted_iota(jnp.int32, (128, 128), 1)
    same_block = (rows < 64) == (cols < 64)
    eye = rows == cols
    in_head = lanes_of(128) % 64
    freq = jnp.exp((in_head % 8).astype(F32) * (-2.0 * math.log(10000.0) / ROT))
    low_half = lanes_of(128) < 64
    for r in range(4):
        span = slice(128 * r, 128 * r + 128)
        seg_row = jnp.broadcast_to(act_refs[r][128:144, 0:128].astype(F32)[0:1], (128, 128))
        seg_col = jnp.sum(jnp.where(eye, seg_row, 0.0), axis=1, keepdims=True)
        same = (seg_col == seg_row) & same_block
        allowed = same & (cols <= rows) & ((seg_col >= 0.0) | eye)
        position = jnp.sum(jnp.where(same & (cols < rows), 1.0, 0.0), axis=1, keepdims=True)
        angle = position * freq
        cos_t = jnp.where(in_head < ROT, jnp.cos(angle), 1.0)
        sine = jnp.sin(angle)
        sin_a = jnp.where(in_head < 8, sine, 0.0)
        sin_b = jnp.where((in_head >= 8) & (in_head < ROT), sine, 0.0)

        def rotated(x):
            return x * cos_t - turned(x, -8) * sin_a + turned(x, 8) * sin_b

        def unrotated(x):
            return x * cos_t + turned(x, -8) * sin_a - turned(x, 8) * sin_b

        for tile in range(2):
            at = [256 * j + 128 * tile for j in range(3)]
            query = rotated(qkv[span, at[0] : at[0] + 128]).astype(BF)
            key = rotated(qkv[span, at[1] : at[1] + 128]).astype(BF)
            value = qkv[span, at[2] : at[2] + 128].astype(BF)
            g_out = g_attn[span, 128 * tile : 128 * tile + 128]
            parts = []
            for half in range(2 - tile):
                mask = low_half if half == 0 else jnp.logical_not(low_half)
                key_h = jnp.where(mask, key, jnp.zeros_like(key))
                value_h = jnp.where(mask, value, jnp.zeros_like(value))
                scores = dot_nt(query, key_h) * HEAD_DIM ** (-0.5)
                masked = jnp.where(allowed, scores, -1e30)
                top = jnp.max(masked, axis=1, keepdims=True)
                expo = jnp.where(allowed, jnp.exp(masked - top), 0.0)
                prob = expo * (1.0 / jnp.sum(expo, axis=1, keepdims=True))
                prob_bf = prob.astype(BF)
                g_prob = dot_nt(g_out, value_h)
                delta = jnp.sum(prob * g_prob, axis=1, keepdims=True)
                g_score = (prob * (g_prob - delta) * HEAD_DIM ** (-0.5)).astype(BF)
                parts.append(
                    (
                        dot_nn(prob_bf, value),
                        dot_tn(prob_bf, g_out),
                        dot_nn(g_score, key),
                        dot_tn(g_score, query),
                    )
                )
            if tile == 0:
                o, gv, gq, gk = [jnp.where(low_half, a, b) for a, b in zip(*parts)]
            else:
                o, gv, gq, gk = [jnp.where(low_half, a, 0.0) for a in parts[0]]
            attn[span, 128 * tile : 128 * tile + 128] = o.astype(BF)
            g_qkv[span, at[0] : at[0] + 128] = unrotated(gq)
            g_qkv[span, at[1] : at[1] + 128] = unrotated(gk)
            g_qkv[span, at[2] : at[2] + 128] = gv
    y = dot_nn(attn[...], bf_out[...]) + bias_y
    grad_out = dot_tn(attn[...], grad_y[...])
    g_bias_qkv = jnp.sum(g_qkv[...], axis=0, keepdims=True)
    g_qkv_bf = g_qkv[...].astype(BF)
    w_qkv[...] = dot_tn(act_one, g_qkv_bf).reshape(24, 4, 8, D)
    g_act_one = dot_nt(g_qkv_bf, bf_qkv[...])
    w_out[...] = grad_out

    act_two = act_of(gain_two, shift_two)
    up[...] = dot_nn(act_two, bf_up[...]) + bias_up
    cdf = 0.5 * (1.0 + lax.erf(up[...] * 0.7071067811865476))
    hidden = (up[...] * cdf).astype(BF)
    y = y + dot_nn(hidden, bf_down[...])
    for r in range(4):
        back_refs[r][0:128, :] = y[128 * r : 128 * r + 128].astype(BF)
    w_down[...] = dot_tn(hidden, grad_y[...])
    pdf = jnp.exp(-0.5 * up[...] * up[...]) * 0.3989422804014327
    g_up = dot_nt(grad_y[...], bf_down[...]) * (cdf + up[...] * pdf)
    g_bias_up = jnp.sum(g_up, axis=0, keepdims=True)
    g_up_bf = g_up.astype(BF)
    w_up[...] = dot_tn(act_two, g_up_bf)
    g_act_two = dot_nt(g_up_bf, bf_up[...])
    wide = normed[...].astype(F32)
    for r in range(4):
        span = slice(128 * r, 128 * r + 128)
        back_refs[r][128:256, :] = (g_act_one[span] * gain_one + g_act_two[span] * gain_two).astype(BF)

    def row_sum(x):
        return jnp.sum(x, axis=0, keepdims=True)

    g_bias_y = row_sum(grad_y[0:128, :].astype(F32))
    flat_bias = jnp.zeros((1, D), F32)
    for j in range(3):
        keep = (lane >= PART * j) & (lane < PART * (j + 1))
        flat_bias = jnp.where(keep, turned(g_bias_qkv, -64 * j), flat_bias)
    tails[...] = jnp.zeros_like(tails)
    tails[0:1, :] = g_bias_up
    tails[1:2, :] = flat_bias
    tails[2:3, :] = g_bias_y
    tails[8:9, :] = g_bias_y
    tails[9:10, :] = row_sum(g_act_one * wide)
    tails[10:11, :] = row_sum(g_act_one)
    tails[11:12, :] = row_sum(g_act_two * wide)
    tails[12:13, :] = row_sum(g_act_two)

    for j in range(3):
        total = None
        for i in range(4):
            piece = w_qkv[:, i, :, 256 * j : 256 * j + 256].reshape(PART, 256)
            piece = jnp.where(lanes_of(256) < PART, piece, 0.0)
            piece = jnp.concatenate([piece, jnp.zeros((PART, 512), F32)], axis=1)
            piece = turned(piece, PART * i)
            total = piece if total is None else total + piece
        packed[j] = total
    for index, ref in enumerate(grad_refs):
        q = place_of(index)
        for i in range(3):
            for j in range(3):
                slab[24 * i + 8 * j : 24 * i + 8 * j + 8, :] = packed[
                    j, pl.ds(pl.multiple_of(24 * q + 8 * i, 8), 8), :
                ]

        @pl.when(q >= 3)
        def _():
            slab[80:152, :] = w_up[pl.ds(pl.multiple_of(72 * q - 192, 8), 72), :]

        @pl.when(q == 2)
        def _():
            slab[80:104, :] = w_up[0:24, :]
            slab[104:168, :] = w_out[128:192, :]

        @pl.when((q < 2) & (plane < 3))
        def _():
            slab[80:144, :] = w_out[pl.ds(pl.multiple_of(64 * q, 8), 64), :]

        @pl.when((q < 2) & (plane == 3))
        def _():
            slab[80:176, :] = w_out[pl.ds(pl.multiple_of(96 * q, 8), 96), :]

        @pl.when(q < 5)
        def _():
            slab[176:248, :] = w_up[pl.ds(pl.multiple_of(384 + 72 * q, 8), 72), :]

        @pl.when(q == 5)
        def _():
            slab[176:200, :] = w_up[744:768, :]
            slab[200:248, :] = w_down[0:48, :]

        @pl.when(q > 5)
        def _():
            slab[176:248, :] = w_down[pl.ds(pl.multiple_of(72 * q - 384, 8), 72), :]

        slab[256:328, :] = w_down[pl.ds(pl.multiple_of(192 + 72 * q, 8), 72), :]
        slab[328:344, :] = tails[...]
        ref[...] = slab[...].astype(BF)


def local_call(kernel, outs, scratch, *operands):
    vmem = pl.BlockSpec(memory_space=pltpu.VMEM)
    return pl.pallas_call(
        kernel,
        out_shape=outs,
        in_specs=[pl.BlockSpec(memory_space=pltpu.SMEM)] + [vmem] * (len(operands) - 1),
        out_specs=jax.tree.map(lambda _: vmem, outs),
        scratch_shapes=scratch,
    )(*operands)


def sliced_step(planes, places, *args):
    return sliced_body(planes, places, *args)


def sliced_body(planes, places, block_input, out_grad, seg_ids, params, first_moment, second_moment):
    count = planes * places * 2
    spread = TAIL // count
    dp, core = lax.axis_index("dp"), lax.axis_index("fsdp")
    plane, spot = dp // places, dp % places
    where_owner = jnp.stack([plane, 2 * spot + core]).astype(jnp.int32)
    where_spot = jnp.stack([plane, spot, core]).astype(jnp.int32)
    across = [
        [(i, (i // places ^ r) * places + i % places) for i in range(planes * places)]
        for r in range(planes)
    ]
    within = [
        [(i, i // places * places + (i % places ^ r)) for i in range(planes * places)]
        for r in range(places)
    ]

    def to_plane(value, r):
        return lax.ppermute(value, "dp", across[r]) if r else value

    def to_spot(value, r):
        return lax.ppermute(value, "dp", within[r]) if r else value

    def to_core(value):
        return lax.ppermute(value, "fsdp", [(0, 1), (1, 0)])

    micro, row_count, _ = block_input.shape
    tokens = micro * row_count
    flat_x = block_input.reshape(tokens, D)
    mean = jnp.mean(flat_x, axis=-1, keepdims=True)
    centred = flat_x - mean
    inv_std = lax.rsqrt(jnp.mean(centred * centred, axis=-1, keepdims=True) + NORM_EPS)
    normed = centred * inv_std
    valid = (seg_ids >= 0).astype(F32).reshape(tokens, 1)
    grad_y = out_grad.reshape(tokens, D) * valid
    seg_rows = jnp.pad(seg_ids.reshape(1, tokens).astype(BF), ((0, 15), (0, D - tokens)))
    sent_acts = jnp.concatenate([normed.astype(BF), seg_rows])
    acts = [to_plane(sent_acts, r) for r in range(3)]
    acts.append(to_plane(acts[2], 1))
    cots = [to_plane(grad_y.astype(BF), r) for r in range(3)]
    cots.append(to_plane(cots[2], 1))

    rows, tail = rows_from_flat(params, spread, count)
    tail = jnp.pad(tail, ((0, 3), (0, 0)))
    spot_shape = jax.ShapeDtypeStruct((SPOT, D), BF)
    slab_shape = jax.ShapeDtypeStruct((SLAB, D), BF)
    sort_scratch = [
        pltpu.VMEM((planes, SPOT, D), F32),
        pltpu.VMEM((D, D), BF),
        pltpu.VMEM(rows.shape, BF),
    ]
    spots = local_call(
        pack_kernel, [spot_shape] * planes, sort_scratch,
        where_owner, rows, tail,
    )
    spots = [to_plane(spots[r], r) for r in range(planes)]
    slab = local_call(slab_kernel, slab_shape, [], where_owner, *spots)
    slabs = [to_spot(slab, r) for r in range(places)]
    slabs = slabs + [to_core(s) for s in slabs]

    total = planes * tokens
    outs = local_call(
        layer_kernel,
        [slab_shape] * 8 + [jax.ShapeDtypeStruct((2 * tokens, D), BF)] * planes,
        [
            pltpu.VMEM((D, D), F32),
            pltpu.VMEM((D, D), F32),
            pltpu.VMEM((256, D), F32),
            pltpu.VMEM((3, PART, D), F32),
            pltpu.VMEM((24, 4, 8, D), F32),
            pltpu.VMEM((16, D), F32),
            pltpu.VMEM((D, D), BF),
            pltpu.VMEM((D, D), BF),
            pltpu.VMEM((256, D), BF),
            pltpu.VMEM((D, D), BF),
            pltpu.VMEM((total, D), BF),
            pltpu.VMEM((total, D), BF),
            pltpu.VMEM((total, D), F32),
            pltpu.VMEM((total, 256), BF),
            pltpu.VMEM((total, D), F32),
            pltpu.VMEM((total, 256), BF),
            pltpu.VMEM((total, D), F32),
            pltpu.VMEM((SLAB, D), F32),
        ],
        where_spot, *acts, *cots, *slabs,
    )
    grads, backs = outs[:8], outs[8:]
    paired = [
        (grads[r].astype(F32) + to_core(grads[4 + r]).astype(F32)).astype(BF) for r in range(places)
    ]
    arrived = [to_spot(paired[r], r) for r in range(places)]
    passed = to_plane(backs[3], 1)
    backs = [
        backs[0],
        to_plane(backs[1], 1),
        to_plane((backs[2].astype(F32) + passed.astype(F32)).astype(BF), 2),
    ]
    spots = local_call(
        split_kernel, [spot_shape] * planes, [pltpu.VMEM((SLAB, D), F32)], where_owner, *arrived
    )
    spots = [to_plane(spots[r], r) for r in range(planes)]
    grad_rows, grad_tail = local_call(
        unpack_kernel,
        [
            jax.ShapeDtypeStruct(rows.shape, F32),
            jax.ShapeDtypeStruct((16, D), F32),
        ],
        sort_scratch,
        where_owner, *spots,
    )
    back = sum(b.astype(F32) for b in backs)
    result = flat_x + back[:tokens]
    scaled = back[tokens:]
    input_grad = grad_y + inv_std * (
        scaled
        - jnp.mean(scaled, axis=-1, keepdims=True)
        - normed * jnp.mean(scaled * normed, axis=-1, keepdims=True)
    )
    owned = flat_from_rows(grad_rows, grad_tail[:13], spread, count)
    new_params, new_first, new_second = adam_update(params, owned, first_moment, second_moment)
    return (
        result.reshape(block_input.shape),
        input_grad.reshape(block_input.shape),
        owned,
        new_params,
        new_first,
        new_second,
    )


def solution(mesh):
    vector, tokens = P(AXES), P(None, AXES, None)
    dp, cores = mesh.shape["dp"], mesh.shape["fsdp"]
    if dp == PLANES * PLANES and cores == 2:
        step = functools.partial(sliced_step, PLANES, dp // PLANES)
    else:
        step = functools.partial(body, dp * cores)
    return jax.shard_map(
        step,
        mesh=mesh,
        in_specs=(tokens, tokens, P(None, AXES), vector, vector, vector),
        out_specs=(tokens, tokens, vector, vector, vector, vector),
        check_vma=False,
    )
```

```python
import functools
import math

import jax
import jax.numpy as jnp
from jax import lax
from jax.experimental import pallas as pl
from jax.experimental.pallas import tpu as pltpu
from jax.sharding import PartitionSpec as P


D = 768
FF = 3072
HEADS = 12
HEAD_DIM = 64
ROT = 16
STEP = 3


NORM_EPS = 1e-05
BETA_ONE = 0.9
BETA_TWO = 0.95
LEARN_RATE = 0.05
WEIGHT_DECAY = 0.1
ADAM_EPS = 1e-08


def layout_shapes():
    return [
        (D, 3 * D),
        (D, D),
        (D, FF),
        (FF, D),
        (3 * D,),
        (D,),
        (FF,),
        (D,),
        (D,),
        (D,),
        (D,),
        (D,),
    ]


def unpack_flat(flat_vec):
    pieces_out = []
    offset = 0
    for item_shape in layout_shapes():
        length = math.prod(item_shape)
        pieces_out.append(flat_vec[offset : offset + length].reshape(item_shape))
        offset += length
    return pieces_out


def product(form, left, right):
    return jnp.einsum(form, left, right, preferred_element_type=jnp.float32)


def block_tables(seg_rows):
    row_count = seg_rows.shape[1]
    row_idx = jnp.arange(row_count)
    same_seq = seg_rows[:, :, None] == seg_rows[:, None, :]
    earlier = row_idx[None, :] < row_idx[:, None]
    diagonal = row_idx[None, :] == row_idx[:, None]
    causal = row_idx[None, :] <= row_idx[:, None]
    allowed = same_seq & causal[None] & ((seg_rows[:, :, None] >= 0) | diagonal[None])
    position = jnp.sum(jnp.where(same_seq & earlier[None], 1, 0), axis=2).astype(jnp.float32)
    inv_freq = 10000.0 ** (-(jnp.arange(ROT // 2, dtype=jnp.float32) * 2.0) / ROT)
    angles = position[:, :, None] * inv_freq[None, None, :]
    return (allowed, jnp.cos(angles)[:, :, None, :], jnp.sin(angles)[:, :, None, :])


def rotate(vecs, cos_t, sin_t):
    half_rot = ROT // 2
    first = vecs[..., :half_rot]
    second = vecs[..., half_rot:ROT]
    return jnp.concatenate(
        [first * cos_t - second * sin_t, second * cos_t + first * sin_t, vecs[..., ROT:]], axis=-1
    )


def unrotate(vecs, cos_t, sin_t):
    half_rot = ROT // 2
    first = vecs[..., :half_rot]
    second = vecs[..., half_rot:ROT]
    return jnp.concatenate(
        [first * cos_t + second * sin_t, second * cos_t - first * sin_t, vecs[..., ROT:]], axis=-1
    )


def layer_norm(flat_x, gain, shift):
    row_mean = jnp.mean(flat_x, axis=-1, keepdims=True)
    centred = flat_x - row_mean
    row_var = jnp.mean(centred * centred, axis=-1, keepdims=True)
    inv_std = lax.rsqrt(row_var + NORM_EPS)
    normed = centred * inv_std
    return (
        normed,
        inv_std,
        (normed * gain.astype(jnp.float32) + shift.astype(jnp.float32)).astype(jnp.bfloat16),
    )


def norm_back(grad_act, normed, inv_std, gain):
    grad_gain = jnp.sum(grad_act * normed, axis=0)
    grad_shift = jnp.sum(grad_act, axis=0)
    scaled = grad_act * gain.astype(jnp.float32)
    grad_in = inv_std * (
        scaled
        - jnp.mean(scaled, axis=-1, keepdims=True)
        - normed * jnp.mean(scaled * normed, axis=-1, keepdims=True)
    )
    return (grad_gain, grad_shift, grad_in)


def softmax_rows(query_bf, key_bf, allowed, log_total):
    scores = product("gqhd,gkhd->ghqk", query_bf, key_bf) * HEAD_DIM ** (-0.5)
    mask_b = allowed[:, None]
    masked = jnp.where(mask_b, scores, -jnp.inf)
    if log_total is None:
        top_score = jnp.max(masked, axis=-1, keepdims=True)
        expo = jnp.where(mask_b, jnp.exp(masked - top_score), 0.0)
        log_total = top_score + jnp.log(jnp.sum(expo, axis=-1, keepdims=True))
    prob_rows = jnp.where(mask_b, jnp.exp(masked - log_total), 0.0)
    return (prob_rows, log_total)


def forward(x_rows, seg_rows, weights):
    (
        w_qkv,
        w_out,
        w_up,
        w_down,
        b_qkv,
        b_out,
        b_up,
        b_down,
        gain_one,
        shift_one,
        gain_two,
        shift_two,
    ) = weights
    group_count, row_count = seg_rows.shape
    allowed, cos_t, sin_t = block_tables(seg_rows)
    flat_x = x_rows.reshape(group_count * row_count, D)
    normed_one, inv_one, act_one = layer_norm(flat_x, gain_one, shift_one)
    normed_two, inv_two, act_two = layer_norm(flat_x, gain_two, shift_two)
    qkv_rows = jnp.dot(act_one, w_qkv, preferred_element_type=jnp.float32) + b_qkv.astype(
        jnp.float32
    )
    qkv_rows = qkv_rows.reshape(group_count, row_count, 3, HEADS, HEAD_DIM)
    query_bf = rotate(qkv_rows[:, :, 0], cos_t, sin_t).astype(jnp.bfloat16)
    key_bf = rotate(qkv_rows[:, :, 1], cos_t, sin_t).astype(jnp.bfloat16)
    value_bf = qkv_rows[:, :, 2].astype(jnp.bfloat16)
    prob_rows, log_total = softmax_rows(query_bf, key_bf, allowed, None)
    prob_bf = prob_rows.astype(jnp.bfloat16)
    attn_bf = (
        product("ghqk,gkhd->gqhd", prob_bf, value_bf)
        .astype(jnp.bfloat16)
        .reshape(group_count * row_count, D)
    )
    attn_out = jnp.dot(attn_bf, w_out, preferred_element_type=jnp.float32) + b_out.astype(
        jnp.float32
    )
    up_rows = jnp.dot(act_two, w_up, preferred_element_type=jnp.float32) + b_up.astype(jnp.float32)
    hidden_bf = jax.nn.gelu(up_rows, approximate=False).astype(jnp.bfloat16)
    mlp_out = jnp.dot(hidden_bf, w_down, preferred_element_type=jnp.float32) + b_down.astype(
        jnp.float32
    )
    result = flat_x + attn_out + mlp_out
    kept_state = (
        normed_one,
        inv_one,
        act_one,
        normed_two,
        inv_two,
        act_two,
        query_bf,
        key_bf,
        value_bf,
        log_total,
        attn_bf,
        up_rows,
        hidden_bf,
        allowed,
        cos_t,
        sin_t,
        seg_rows,
    )
    return (result.reshape(group_count, row_count, D), kept_state)


def backward(kept_state, grad_rows, weights):
    (w_qkv, w_out, w_up, w_down, _, _, _, _, gain_one, _, gain_two, _) = weights
    (
        normed_one,
        inv_one,
        act_one,
        normed_two,
        inv_two,
        act_two,
        query_bf,
        key_bf,
        value_bf,
        log_total,
        attn_bf,
        up_rows,
        hidden_bf,
        allowed,
        cos_t,
        sin_t,
        seg_rows,
    ) = kept_state
    group_count, row_count = seg_rows.shape
    valid = (seg_rows >= 0).astype(jnp.float32).reshape(group_count * row_count, 1)
    grad_y = grad_rows.reshape(group_count * row_count, D) * valid
    grad_y_bf = grad_y.astype(jnp.bfloat16)
    grad_bias = jnp.sum(grad_y, axis=0)
    grad_w_down = jnp.dot(hidden_bf.T, grad_y_bf, preferred_element_type=jnp.float32)
    grad_w_out = jnp.dot(attn_bf.T, grad_y_bf, preferred_element_type=jnp.float32)
    grad_hidden = jnp.dot(grad_y_bf, w_down.T, preferred_element_type=jnp.float32)
    cdf_part = 0.5 * (1.0 + jax.scipy.special.erf(up_rows * 0.7071067811865476))
    pdf_part = jnp.exp(-0.5 * up_rows * up_rows) * 0.3989422804014327
    grad_up = grad_hidden * (cdf_part + up_rows * pdf_part)
    grad_b_up = jnp.sum(grad_up, axis=0)
    grad_up_bf = grad_up.astype(jnp.bfloat16)
    grad_w_up = jnp.dot(act_two.T, grad_up_bf, preferred_element_type=jnp.float32)
    grad_act_two = jnp.dot(grad_up_bf, w_up.T, preferred_element_type=jnp.float32)
    grad_attn = jnp.dot(grad_y_bf, w_out.T, preferred_element_type=jnp.float32).astype(jnp.bfloat16)
    grad_attn = grad_attn.reshape(group_count, row_count, HEADS, HEAD_DIM)
    prob_rows, _ = softmax_rows(query_bf, key_bf, allowed, log_total)
    prob_bf = prob_rows.astype(jnp.bfloat16)
    grad_value = product("ghqk,gqhd->gkhd", prob_bf, grad_attn)
    grad_prob = product("gqhd,gkhd->ghqk", grad_attn, value_bf)
    delta_rows = jnp.sum(prob_rows * grad_prob, axis=-1, keepdims=True)
    grad_score_bf = (prob_rows * (grad_prob - delta_rows) * HEAD_DIM ** (-0.5)).astype(jnp.bfloat16)
    grad_query = unrotate(product("ghqk,gkhd->gqhd", grad_score_bf, key_bf), cos_t, sin_t)
    grad_key = unrotate(product("ghqk,gqhd->gkhd", grad_score_bf, query_bf), cos_t, sin_t)
    grad_qkv = jnp.stack([grad_query, grad_key, grad_value], axis=2).reshape(
        group_count * row_count, 3 * D
    )
    grad_b_qkv = jnp.sum(grad_qkv, axis=0)
    grad_qkv_bf = grad_qkv.astype(jnp.bfloat16)
    grad_w_qkv = jnp.dot(act_one.T, grad_qkv_bf, preferred_element_type=jnp.float32)
    grad_act_one = jnp.dot(grad_qkv_bf, w_qkv.T, preferred_element_type=jnp.float32)
    grad_gain_one, grad_shift_one, back_one = norm_back(grad_act_one, normed_one, inv_one, gain_one)
    grad_gain_two, grad_shift_two, back_two = norm_back(grad_act_two, normed_two, inv_two, gain_two)
    input_grad = (grad_y + back_one + back_two).reshape(group_count, row_count, D)
    grads = (
        grad_w_qkv,
        grad_w_out,
        grad_w_up,
        grad_w_down,
        grad_b_qkv,
        grad_bias,
        grad_b_up,
        grad_bias,
        grad_gain_one,
        grad_shift_one,
        grad_gain_two,
        grad_shift_two,
    )
    return (input_grad, grads)


def adam_update(params, grads, first_moment, second_moment):
    new_first = BETA_ONE * first_moment + (1.0 - BETA_ONE) * grads
    new_second = BETA_TWO * second_moment + (1.0 - BETA_TWO) * grads * grads
    first_hat = new_first / (1.0 - BETA_ONE**STEP)
    second_hat = new_second / (1.0 - BETA_TWO**STEP)
    new_params = params - LEARN_RATE * (
        first_hat / (jnp.sqrt(second_hat) + ADAM_EPS) + WEIGHT_DECAY * params
    )
    return (new_params, new_first, new_second)


AXES = ("dp", "fsdp")
TAIL = 13 * D


def rows_from_flat(flat, spread, count):
    me = lax.axis_index(AXES)
    tail = flat[flat.shape[0] - TAIL :]
    before = lax.ppermute(tail, AXES, [(i, (i + 1) % count) for i in range(count)])
    joined = jnp.concatenate([before, flat])
    rows = lax.dynamic_slice(joined, (TAIL - spread * me,), (flat.shape[0] - spread,))
    return rows.reshape(-1, D), tail.reshape(-1, D)


def flat_from_rows(rows, tail, spread, count):
    me = lax.axis_index(AXES)
    head = rows.reshape(-1)[:TAIL]
    after = lax.ppermute(head, AXES, [(i, (i - 1) % count) for i in range(count)])
    after = jnp.where(me == count - 1, tail.reshape(-1), after)
    joined = jnp.concatenate([rows.reshape(-1), after])
    return lax.dynamic_slice(joined, (spread * me,), (rows.size + spread,))


def body(count, block_input, out_grad, seg_ids, params, first_moment, second_moment):
    spread = TAIL // count
    row_count = (params.shape[0] - spread) // D
    rows, tail = rows_from_flat(params.astype(jnp.bfloat16), spread, count)
    sent = jnp.concatenate([rows, jnp.pad(tail, ((0, 3), (0, 0)))])
    whole = lax.all_gather(sent, AXES, axis=0, tiled=False)
    matrices = whole[:, :row_count].reshape(-1)
    weights = unpack_flat(jnp.concatenate([matrices, whole[count - 1, row_count : row_count + 13].reshape(-1)]))
    result, kept_state = forward(block_input, seg_ids, weights)
    back_x, grads = backward(kept_state, out_grad, weights)
    big = jnp.concatenate([g.astype(jnp.bfloat16).reshape(-1, D) for g in grads[:4]])
    small = jnp.concatenate([g.astype(jnp.bfloat16).reshape(-1, D) for g in grads[4:]])
    small = jnp.pad(small, ((0, 3), (0, 0)))
    spots = jnp.where(jnp.arange(count)[:, None, None] == count - 1, small[None], jnp.zeros((), jnp.bfloat16))
    out = jnp.concatenate([big.reshape(count, row_count, D), spots], axis=1)
    owned = lax.psum_scatter(out, AXES, scatter_dimension=0, tiled=False).astype(jnp.float32)
    owned_grads = flat_from_rows(owned[:row_count], owned[row_count : row_count + 13], spread, count)
    new_params, new_first, new_second = adam_update(params, owned_grads, first_moment, second_moment)
    return (result, back_x, owned_grads, new_params, new_first, new_second)


BF = jnp.bfloat16
F32 = jnp.float32
PLANES = 4
PART = D // PLANES
SPOT = 96
SLAB = 352
STARTS = (0, 80, 176, 256)


def dot_nn(a, b):
    return lax.dot_general(a, b, (((1,), (0,)), ((), ())), preferred_element_type=F32)


def dot_nt(a, b):
    return lax.dot_general(a, b, (((1,), (1,)), ((), ())), preferred_element_type=F32)


def dot_tn(a, b):
    return lax.dot_general(a, b, (((0,), (0,)), ((), ())), preferred_element_type=F32)


def lanes_of(width):
    return lax.broadcasted_iota(jnp.int32, (1, width), 1)


def group_mask(index, width=D, size=PART):
    lane = lanes_of(width)
    return (lane >= index * size) & (lane < (index + 1) * size)


def turned(value, shift):
    shift = shift % value.shape[-1]
    return value if shift == 0 else pltpu.roll(value, shift, value.ndim - 1)


def spread_groups(parts, first):
    total = None
    for group, part in enumerate(parts):
        moved = turned(part, PART * (group - first))
        total = moved if total is None else jnp.where(group_mask(group), moved, total)
    if len(parts) < PLANES:
        total = jnp.where(lanes_of(D) < PART * len(parts), total, 0.0)
    return total


def count_of(value, *limits):
    return sum(jnp.where(value >= limit, 1, 0) for limit in limits)


def pick_matrix(kinds, size):
    row = lax.broadcasted_iota(jnp.int32, (SPOT, SPOT), 0)
    col = lax.broadcasted_iota(jnp.int32, (SPOT, SPOT), 1)
    kind = count_of(row, *range(size, SPOT, size))
    return jnp.where(col == kinds * (row - size * kind) + kind, 1.0, 0.0).astype(BF)


def order_columns(perm_ref, by_head):
    place = lax.broadcasted_iota(jnp.int32, (8, D), 1)
    part = count_of(place, PART, 2 * PART, 3 * PART)
    inner = place - PART * part
    if by_head:
        kind = count_of(inner, HEAD_DIM, 2 * HEAD_DIM)
        early = part + jnp.where(kind == 0, 0, jnp.where(kind == 1, 5, 9))
        late = jnp.where(kind == 0, 3, jnp.where(kind == 1, 4, 8))
        source = HEAD_DIM * (jnp.where(part < 3, early, late) - kind) + inner
    else:
        run = count_of(inner, *range(24, PART, 24))
        source = (SPOT - 24) * run + 24 * part + inner
    row = lax.broadcasted_iota(jnp.int32, (D, D), 0)
    perm_ref[...] = jnp.where(row == source[0:1], 1.0, 0.0).astype(BF)


def pack_kernel(where_ref, rows_ref, tail_ref, *refs):
    out_refs, (spot, perm, mixed) = refs[:PLANES], refs[PLANES:]
    plane, place = where_ref[0], where_ref[1]
    device = 8 * plane + place
    with_heads = device < 8
    with_hidden = (device >= 10) & (device < 22)
    spot[...] = jnp.zeros_like(spot)
    pl.when(with_heads)(lambda: order_columns(perm, True))
    pl.when(with_hidden)(lambda: order_columns(perm, False))

    @pl.when(with_heads | with_hidden)
    def _():
        mixed[...] = dot_nn(rows_ref[...].astype(BF), perm[...]).astype(BF)

    @pl.when(with_heads)
    def _():
        sort = pick_matrix(3, 32)
        for i in range(3):
            picked = dot_nn(sort, mixed[SPOT * i : SPOT * i + SPOT, :])
            for j in range(3):
                parts = [picked[32 * j + 8 * g : 32 * j + 8 * g + 8] for g in range(4)]
                for s in range(PLANES):
                    spot[s, 24 * i + 8 * j : 24 * i + 8 * j + 8, :] = spread_groups(parts, s)

    for i in range(3):
        block = 3 * device + i

        @pl.when((block >= 32) & (block < 64))
        def _():
            picked = dot_nn(pick_matrix(4, 24), mixed[SPOT * i : SPOT * i + SPOT, :])
            parts = [picked[24 * j : 24 * j + 24] for j in range(4)]
            start = 24 * i
            if i == 2:
                start = pl.multiple_of(jnp.where(block == 32, 0, 48), 8)
            for s in range(PLANES):
                spot[s, pl.ds(start, 24), :] = spread_groups(parts, s)

        @pl.when(block >= 64)
        def _():
            for s in range(PLANES):
                spot[s, 24 * i : 24 * i + 24, :] = rows_ref[
                    SPOT * i + 24 * s : SPOT * i + 24 * s + 24, :
                ]

    @pl.when(device == 8)
    def _():
        for s in range(3):
            spot[s, 0:64, :] = rows_ref[64 * s : 64 * s + 64, :]
        spot[3, 0:96, :] = rows_ref[192:288, :]

    @pl.when(device == 9)
    def _():
        for s in range(3):
            spot[s, 0:64, :] = rows_ref[32 + 64 * s : 96 + 64 * s, :]
        spot[3, 0:32, :] = rows_ref[0:32, :]
        spot[3, 32:96, :] = rows_ref[224:288, :]

    @pl.when(device == 10)
    def _():
        for s in range(3):
            spot[s, 24:88, :] = rows_ref[64 * s : 64 * s + 64, :]

    @pl.when(device == 31)
    def _():
        upper = tail_ref[0:8, :].astype(BF)
        order_columns(perm, True)
        by_head = dot_nn(upper, perm[...])
        order_columns(perm, False)
        by_hidden = dot_nn(upper, perm[...])
        for s in range(PLANES):
            spot[s, 72:73, :] = spread_groups([by_hidden[4 + j : 5 + j] for j in range(4)], s)
            spot[s, 73:74, :] = spread_groups([by_head[j : j + 1] for j in range(3)], s)
            spot[s, 74:75, :] = tail_ref[3:4, :]
            spot[s, 80:88, :] = tail_ref[8:16, :]

    for r in range(PLANES):
        out_refs[r][...] = spot[plane ^ r].astype(BF)


def unpack_kernel(where_ref, *refs):
    in_refs, (rows_ref, tail_ref, spot, perm, mixed) = refs[:PLANES], refs[PLANES:]
    plane, place = where_ref[0], where_ref[1]
    device = 8 * plane + place
    with_heads = device < 8
    with_hidden = (device >= 10) & (device < 22)
    for r in range(PLANES):
        spot[plane ^ r] = in_refs[r][...].astype(F32)
    pl.when(with_heads)(lambda: order_columns(perm, True))

    @pl.when(with_heads)
    def _():
        sort = pick_matrix(3, 32)
        for i in range(3):
            sorted_ = []
            for j in range(3):
                base = 24 * i + 8 * j
                parts = [spot[s, base : base + 8, :] for s in range(PLANES)]
                sorted_.extend(spread_groups(parts, g) for g in range(4))
            block_rows = jnp.concatenate(sorted_, axis=0).astype(BF)
            mixed[SPOT * i : SPOT * i + SPOT, :] = dot_tn(sort, block_rows).astype(BF)

    @pl.when(with_hidden)
    def _():
        order_columns(perm, False)
        mixed[...] = jnp.zeros_like(mixed)

    for i in range(3):
        block = 3 * device + i

        @pl.when((block >= 32) & (block < 64))
        def _():
            start = 24 * i
            if i == 2:
                start = pl.multiple_of(jnp.where(block == 32, 0, 48), 8)
            parts = [spot[s, pl.ds(start, 24), :] for s in range(PLANES)]
            block_rows = jnp.concatenate([spread_groups(parts, j) for j in range(4)], axis=0)
            mixed[SPOT * i : SPOT * i + SPOT, :] = dot_tn(
                pick_matrix(4, 24), block_rows.astype(BF)
            ).astype(BF)

    @pl.when(with_heads | with_hidden)
    def _():
        rows_ref[...] = dot_nt(mixed[...], perm[...])

    for i in range(3):

        @pl.when(3 * device + i >= 64)
        def _():
            for s in range(PLANES):
                rows_ref[SPOT * i + 24 * s : SPOT * i + 24 * s + 24, :] = spot[
                    s, 24 * i : 24 * i + 24, :
                ]

    @pl.when(device == 8)
    def _():
        for s in range(3):
            rows_ref[64 * s : 64 * s + 64, :] = spot[s, 0:64, :]
        rows_ref[192:288, :] = spot[3, 0:96, :]

    @pl.when(device == 9)
    def _():
        for s in range(3):
            rows_ref[32 + 64 * s : 96 + 64 * s, :] = spot[s, 0:64, :]
        rows_ref[0:32, :] = spot[3, 0:32, :]
        rows_ref[224:288, :] = spot[3, 32:96, :]

    @pl.when(device == 10)
    def _():
        for s in range(3):
            rows_ref[64 * s : 64 * s + 64, :] = spot[s, 24:88, :]

    tail_ref[...] = jnp.zeros_like(tail_ref)

    @pl.when(device == 31)
    def _():
        order_columns(perm, False)
        whole = [spot[s, 72:73, :] for s in range(PLANES)]
        for j in range(4):
            row = jnp.broadcast_to(spread_groups(whole, j), (8, D)).astype(BF)
            tail_ref[4 + j : 5 + j, :] = dot_nt(row, perm[...])[0:1]
        order_columns(perm, True)
        whole = [spot[s, 73:74, :] for s in range(PLANES)]
        for j in range(3):
            row = jnp.broadcast_to(spread_groups(whole, j), (8, D)).astype(BF)
            tail_ref[j : j + 1, :] = dot_nt(row, perm[...])[0:1]
        tail_ref[3:4, :] = sum(spot[s, 74:75, :] for s in range(PLANES))
        tail_ref[8:16, :] = sum(spot[s, 80:88, :] for s in range(PLANES))


def slab_start(plane):
    start = jnp.where(plane == 1, STARTS[1], jnp.where(plane == 2, STARTS[2], STARTS[3]))
    return pl.multiple_of(jnp.where(plane == 0, 0, start), 16)


def slab_kernel(where_ref, a_ref, b_ref, c_ref, d_ref, out_ref):
    for r, ref in enumerate((a_ref, b_ref, c_ref, d_ref)):
        source = where_ref[0] ^ r
        out_ref[pl.ds(slab_start(source), 80), :] = ref[0:80, :]

        @pl.when((source == 1) | (source == 3))
        def _():
            out_ref[pl.ds(slab_start(source) + 80, 16), :] = ref[80:96, :]


def split_kernel(where_ref, a_ref, b_ref, c_ref, d_ref, *outs):
    out_refs, total = outs[:PLANES], outs[PLANES]
    total[...] = (a_ref[...].astype(F32) + b_ref[...].astype(F32)) + (
        c_ref[...].astype(F32) + d_ref[...].astype(F32)
    )
    for r in range(PLANES):
        out_refs[r][...] = total[pl.ds(slab_start(where_ref[0] ^ r), SPOT), :].astype(BF)


def layer_kernel(where_ref, *refs):
    act_refs, cot_refs, slab_refs = refs[:4], refs[4:8], refs[8:16]
    grad_refs, back_refs = refs[16:24], refs[24:28]
    (w_up, w_down, w_out, packed, w_qkv, tails, bf_up, bf_down, bf_out, bf_qkv, normed, grad_y,
     qkv, attn, g_qkv, g_attn, up, slab) = refs[28:]
    plane, spot, core = where_ref[0], where_ref[1], where_ref[2]
    lane = lanes_of(D)

    def place_of(index):
        return 2 * (spot ^ (index % 4)) + (core if index < 4 else 1 - core)

    w_out[...] = jnp.zeros_like(w_out)
    for index, ref in enumerate(slab_refs):
        q = place_of(index)
        for i in range(3):
            for j in range(3):
                packed[j, pl.ds(pl.multiple_of(24 * q + 8 * i, 8), 8), :] = ref[0:80, :][
                    24 * i + 8 * j : 24 * i + 8 * j + 8
                ].astype(F32)
        one = ref[80:176, :].astype(F32)
        two = ref[176:256, :].astype(F32)
        three = ref[256:352, :].astype(F32)

        @pl.when(q >= 3)
        def _():
            w_up[pl.ds(pl.multiple_of(72 * q - 192, 8), 72), :] = one[0:72]

        @pl.when(q == 2)
        def _():
            w_up[0:24, :] = one[0:24]

            @pl.when(plane < 3)
            def _():
                w_out[128:192, :] = one[24:88]

        @pl.when((q < 2) & (plane < 3))
        def _():
            w_out[pl.ds(pl.multiple_of(64 * q, 8), 64), :] = one[0:64]

        @pl.when((q < 2) & (plane == 3))
        def _():
            w_out[pl.ds(pl.multiple_of(96 * q, 8), 96), :] = one[0:96]

        @pl.when(q < 5)
        def _():
            w_up[pl.ds(pl.multiple_of(384 + 72 * q, 8), 72), :] = two[0:72]

        @pl.when(q == 5)
        def _():
            w_up[744:768, :] = two[0:24]
            w_down[0:48, :] = two[24:72]

        @pl.when(q > 5)
        def _():
            w_down[pl.ds(pl.multiple_of(72 * q - 384, 8), 72), :] = two[0:72]

        w_down[pl.ds(pl.multiple_of(192 + 72 * q, 8), 72), :] = three[0:72]

        @pl.when(q == 7)
        def _():
            tails[...] = three[72:88]

    for j in range(3):
        for i in range(4):
            moved = turned(packed[j], -PART * i)[:, 0:256]
            moved = jnp.where(lanes_of(256) < PART, moved, 0.0)
            w_qkv[:, i, :, 256 * j : 256 * j + 256] = moved.reshape(24, 8, 256)
    bf_up[...] = w_up[...].astype(BF)
    bf_down[...] = w_down[...].astype(BF)
    bf_out[...] = w_out[...].astype(BF)
    bf_qkv[...] = w_qkv[...].reshape(D, D).astype(BF)

    for r in range(4):
        normed[128 * r : 128 * r + 128, :] = act_refs[r][0:128, :]
        grad_y[128 * r : 128 * r + 128, :] = cot_refs[r][...]
    bias_up = tails[0:1, :]
    flat_bias = tails[1:2, :]
    bias_qkv = jnp.zeros((1, D), F32)
    for j in range(3):
        keep = (lane >= 256 * j) & (lane < 256 * j + PART)
        bias_qkv = jnp.where(keep, turned(flat_bias, 64 * j), bias_qkv)
    bias_y = jnp.where(plane == 0, tails[2:3, :] + tails[8:9, :], 0.0)
    gain_one, shift_one = tails[9:10, :], tails[10:11, :]
    gain_two, shift_two = tails[11:12, :], tails[12:13, :]

    def act_of(gain, shift):
        return (normed[...].astype(F32) * gain + shift).astype(BF)

    act_one = act_of(gain_one, shift_one)
    qkv[...] = dot_nn(act_one, bf_qkv[...]) + bias_qkv
    g_attn[...] = dot_nt(grad_y[...], bf_out[...]).astype(BF)

    rows = lax.broadcasted_iota(jnp.int32, (128, 128), 0)
    cols = lax.broadcasted_iota(jnp.int32, (128, 128), 1)
    same_block = (rows < 64) == (cols < 64)
    eye = rows == cols
    in_head = lanes_of(128) % 64
    freq = jnp.exp((in_head % 8).astype(F32) * (-2.0 * math.log(10000.0) / ROT))
    low_half = lanes_of(128) < 64
    for r in range(4):
        span = slice(128 * r, 128 * r + 128)
        seg_row = jnp.broadcast_to(act_refs[r][128:144, 0:128].astype(F32)[0:1], (128, 128))
        seg_col = jnp.sum(jnp.where(eye, seg_row, 0.0), axis=1, keepdims=True)
        same = (seg_col == seg_row) & same_block
        allowed = same & (cols <= rows) & ((seg_col >= 0.0) | eye)
        position = jnp.sum(jnp.where(same & (cols < rows), 1.0, 0.0), axis=1, keepdims=True)
        angle = position * freq
        cos_t = jnp.where(in_head < ROT, jnp.cos(angle), 1.0)
        sine = jnp.sin(angle)
        sin_a = jnp.where(in_head < 8, sine, 0.0)
        sin_b = jnp.where((in_head >= 8) & (in_head < ROT), sine, 0.0)

        def rotated(x):
            return x * cos_t - turned(x, -8) * sin_a + turned(x, 8) * sin_b

        def unrotated(x):
            return x * cos_t + turned(x, -8) * sin_a - turned(x, 8) * sin_b

        for tile in range(2):
            at = [256 * j + 128 * tile for j in range(3)]
            query = rotated(qkv[span, at[0] : at[0] + 128]).astype(BF)
            key = rotated(qkv[span, at[1] : at[1] + 128]).astype(BF)
            value = qkv[span, at[2] : at[2] + 128].astype(BF)
            g_out = g_attn[span, 128 * tile : 128 * tile + 128]
            parts = []
            for half in range(2 - tile):
                mask = low_half if half == 0 else jnp.logical_not(low_half)
                key_h = jnp.where(mask, key, jnp.zeros_like(key))
                value_h = jnp.where(mask, value, jnp.zeros_like(value))
                scores = dot_nt(query, key_h) * HEAD_DIM ** (-0.5)
                masked = jnp.where(allowed, scores, -1e30)
                top = jnp.max(masked, axis=1, keepdims=True)
                expo = jnp.where(allowed, jnp.exp(masked - top), 0.0)
                prob = expo * (1.0 / jnp.sum(expo, axis=1, keepdims=True))
                prob_bf = prob.astype(BF)
                g_prob = dot_nt(g_out, value_h)
                delta = jnp.sum(prob * g_prob, axis=1, keepdims=True)
                g_score = (prob * (g_prob - delta) * HEAD_DIM ** (-0.5)).astype(BF)
                parts.append(
                    (
                        dot_nn(prob_bf, value),
                        dot_tn(prob_bf, g_out),
                        dot_nn(g_score, key),
                        dot_tn(g_score, query),
                    )
                )
            if tile == 0:
                o, gv, gq, gk = [jnp.where(low_half, a, b) for a, b in zip(*parts)]
            else:
                o, gv, gq, gk = [jnp.where(low_half, a, 0.0) for a in parts[0]]
            attn[span, 128 * tile : 128 * tile + 128] = o.astype(BF)
            g_qkv[span, at[0] : at[0] + 128] = unrotated(gq)
            g_qkv[span, at[1] : at[1] + 128] = unrotated(gk)
            g_qkv[span, at[2] : at[2] + 128] = gv
    y = dot_nn(attn[...], bf_out[...]) + bias_y
    grad_out = dot_tn(attn[...], grad_y[...])
    g_bias_qkv = jnp.sum(g_qkv[...], axis=0, keepdims=True)
    g_qkv_bf = g_qkv[...].astype(BF)
    w_qkv[...] = dot_tn(act_one, g_qkv_bf).reshape(24, 4, 8, D)
    g_act_one = dot_nt(g_qkv_bf, bf_qkv[...])
    w_out[...] = grad_out

    act_two = act_of(gain_two, shift_two)
    up[...] = dot_nn(act_two, bf_up[...]) + bias_up
    cdf = 0.5 * (1.0 + lax.erf(up[...] * 0.7071067811865476))
    hidden = (up[...] * cdf).astype(BF)
    y = y + dot_nn(hidden, bf_down[...])
    for r in range(4):
        back_refs[r][0:128, :] = y[128 * r : 128 * r + 128].astype(BF)
    w_down[...] = dot_tn(hidden, grad_y[...])
    pdf = jnp.exp(-0.5 * up[...] * up[...]) * 0.3989422804014327
    g_up = dot_nt(grad_y[...], bf_down[...]) * (cdf + up[...] * pdf)
    g_bias_up = jnp.sum(g_up, axis=0, keepdims=True)
    g_up_bf = g_up.astype(BF)
    w_up[...] = dot_tn(act_two, g_up_bf)
    g_act_two = dot_nt(g_up_bf, bf_up[...])
    wide = normed[...].astype(F32)
    for r in range(4):
        span = slice(128 * r, 128 * r + 128)
        back_refs[r][128:256, :] = (g_act_one[span] * gain_one + g_act_two[span] * gain_two).astype(BF)

    def row_sum(x):
        return jnp.sum(x, axis=0, keepdims=True)

    g_bias_y = row_sum(grad_y[0:128, :].astype(F32))
    flat_bias = jnp.zeros((1, D), F32)
    for j in range(3):
        keep = (lane >= PART * j) & (lane < PART * (j + 1))
        flat_bias = jnp.where(keep, turned(g_bias_qkv, -64 * j), flat_bias)
    tails[...] = jnp.zeros_like(tails)
    tails[0:1, :] = g_bias_up
    tails[1:2, :] = flat_bias
    tails[2:3, :] = g_bias_y
    tails[8:9, :] = g_bias_y
    tails[9:10, :] = row_sum(g_act_one * wide)
    tails[10:11, :] = row_sum(g_act_one)
    tails[11:12, :] = row_sum(g_act_two * wide)
    tails[12:13, :] = row_sum(g_act_two)

    for j in range(3):
        total = None
        for i in range(4):
            piece = w_qkv[:, i, :, 256 * j : 256 * j + 256].reshape(PART, 256)
            piece = jnp.where(lanes_of(256) < PART, piece, 0.0)
            piece = jnp.concatenate([piece, jnp.zeros((PART, 512), F32)], axis=1)
            piece = turned(piece, PART * i)
            total = piece if total is None else total + piece
        packed[j] = total
    for index, ref in enumerate(grad_refs):
        q = place_of(index)
        for i in range(3):
            for j in range(3):
                slab[24 * i + 8 * j : 24 * i + 8 * j + 8, :] = packed[
                    j, pl.ds(pl.multiple_of(24 * q + 8 * i, 8), 8), :
                ]

        @pl.when(q >= 3)
        def _():
            slab[80:152, :] = w_up[pl.ds(pl.multiple_of(72 * q - 192, 8), 72), :]

        @pl.when(q == 2)
        def _():
            slab[80:104, :] = w_up[0:24, :]
            slab[104:168, :] = w_out[128:192, :]

        @pl.when((q < 2) & (plane < 3))
        def _():
            slab[80:144, :] = w_out[pl.ds(pl.multiple_of(64 * q, 8), 64), :]

        @pl.when((q < 2) & (plane == 3))
        def _():
            slab[80:176, :] = w_out[pl.ds(pl.multiple_of(96 * q, 8), 96), :]

        @pl.when(q < 5)
        def _():
            slab[176:248, :] = w_up[pl.ds(pl.multiple_of(384 + 72 * q, 8), 72), :]

        @pl.when(q == 5)
        def _():
            slab[176:200, :] = w_up[744:768, :]
            slab[200:248, :] = w_down[0:48, :]

        @pl.when(q > 5)
        def _():
            slab[176:248, :] = w_down[pl.ds(pl.multiple_of(72 * q - 384, 8), 72), :]

        slab[256:328, :] = w_down[pl.ds(pl.multiple_of(192 + 72 * q, 8), 72), :]
        slab[328:344, :] = tails[...]
        ref[...] = slab[...].astype(BF)


def local_call(kernel, outs, scratch, limit, kept_out, where, *operands):
    vmem = pl.BlockSpec(memory_space=pltpu.VMEM)
    operands = [pltpu.with_memory_space_constraint(x, pltpu.VMEM) for x in operands]
    out_specs = jax.tree.map(lambda _: vmem, outs)
    if kept_out:
        outs = jax.tree.map(lambda x: pltpu.VMEM(x.shape, x.dtype), outs)
    return pl.pallas_call(
        kernel,
        out_shape=outs,
        in_specs=[pl.BlockSpec(memory_space=pltpu.SMEM)] + [vmem] * len(operands),
        out_specs=out_specs,
        scratch_shapes=scratch,
        compiler_params=pltpu.CompilerParams(vmem_limit_bytes=limit << 20),
    )(where, *operands)


def sliced_step(planes, places, *args):
    return sliced_body(planes, places, *args)


def sliced_body(planes, places, block_input, out_grad, seg_ids, params, first_moment, second_moment):
    count = planes * places * 2
    spread = TAIL // count
    dp, core = lax.axis_index("dp"), lax.axis_index("fsdp")
    plane, spot = dp // places, dp % places
    where_owner = jnp.stack([plane, 2 * spot + core]).astype(jnp.int32)
    where_spot = jnp.stack([plane, spot, core]).astype(jnp.int32)
    across = [
        [(i, (i // places ^ r) * places + i % places) for i in range(planes * places)]
        for r in range(planes)
    ]
    within = [
        [(i, i // places * places + (i % places ^ r)) for i in range(planes * places)]
        for r in range(places)
    ]

    def to_plane(value, r):
        return lax.ppermute(value, "dp", across[r]) if r else value

    def to_spot(value, r):
        return lax.ppermute(value, "dp", within[r]) if r else value

    def to_core(value):
        return lax.ppermute(value, "fsdp", [(0, 1), (1, 0)])

    micro, row_count, _ = block_input.shape
    tokens = micro * row_count
    flat_x = block_input.reshape(tokens, D)
    mean = jnp.mean(flat_x, axis=-1, keepdims=True)
    centred = flat_x - mean
    inv_std = lax.rsqrt(jnp.mean(centred * centred, axis=-1, keepdims=True) + NORM_EPS)
    normed = centred * inv_std
    valid = (seg_ids >= 0).astype(F32).reshape(tokens, 1)
    grad_y = out_grad.reshape(tokens, D) * valid
    seg_rows = jnp.pad(seg_ids.reshape(1, tokens).astype(BF), ((0, 15), (0, D - tokens)))
    sent_acts = jnp.concatenate([normed.astype(BF), seg_rows])
    acts = [to_plane(sent_acts, r) for r in range(3)]
    acts.append(to_plane(acts[2], 1))
    cots = [to_plane(grad_y.astype(BF), r) for r in range(3)]
    cots.append(to_plane(cots[2], 1))

    rows, tail = rows_from_flat(params, spread, count)
    tail = jnp.pad(tail, ((0, 3), (0, 0)))
    spot_shape = jax.ShapeDtypeStruct((SPOT, D), BF)
    slab_shape = jax.ShapeDtypeStruct((SLAB, D), BF)
    sort_scratch = [
        pltpu.VMEM((planes, SPOT, D), F32),
        pltpu.VMEM((D, D), BF),
        pltpu.VMEM(rows.shape, BF),
    ]
    spots = local_call(
        pack_kernel, [spot_shape] * planes, sort_scratch, 12, True,
        where_owner, rows, tail,
    )
    spots = [to_plane(spots[r], r) for r in range(planes)]
    slab = local_call(slab_kernel, slab_shape, [], 8, True, where_owner, *spots)
    slabs = [to_spot(slab, r) for r in range(places)]
    slabs = slabs + [to_core(s) for s in slabs]

    total = planes * tokens
    outs = local_call(
        layer_kernel,
        [slab_shape] * 8 + [jax.ShapeDtypeStruct((2 * tokens, D), BF)] * planes,
        [
            pltpu.VMEM((D, D), F32),
            pltpu.VMEM((D, D), F32),
            pltpu.VMEM((256, D), F32),
            pltpu.VMEM((3, PART, D), F32),
            pltpu.VMEM((24, 4, 8, D), F32),
            pltpu.VMEM((16, D), F32),
            pltpu.VMEM((D, D), BF),
            pltpu.VMEM((D, D), BF),
            pltpu.VMEM((256, D), BF),
            pltpu.VMEM((D, D), BF),
            pltpu.VMEM((total, D), BF),
            pltpu.VMEM((total, D), BF),
            pltpu.VMEM((total, D), F32),
            pltpu.VMEM((total, 256), BF),
            pltpu.VMEM((total, D), F32),
            pltpu.VMEM((total, 256), BF),
            pltpu.VMEM((total, D), F32),
            pltpu.VMEM((SLAB, D), F32),
        ],
        44, True, where_spot, *acts, *cots, *slabs,
    )
    grads, backs = outs[:8], outs[8:]
    paired = [
        (grads[r].astype(F32) + to_core(grads[4 + r]).astype(F32)).astype(BF) for r in range(places)
    ]
    arrived = [to_spot(paired[r], r) for r in range(places)]
    passed = to_plane(backs[3], 1)
    backs = [
        backs[0],
        to_plane(backs[1], 1),
        to_plane((backs[2].astype(F32) + passed.astype(F32)).astype(BF), 2),
    ]
    spots = local_call(
        split_kernel, [spot_shape] * planes, [pltpu.VMEM((SLAB, D), F32)], 12, True, where_owner, *arrived
    )
    spots = [to_plane(spots[r], r) for r in range(planes)]
    grad_rows, grad_tail = local_call(
        unpack_kernel,
        [
            jax.ShapeDtypeStruct(rows.shape, F32),
            jax.ShapeDtypeStruct((16, D), F32),
        ],
        sort_scratch, 12, True,
        where_owner, *spots,
    )
    back = sum(b.astype(F32) for b in backs)
    result = flat_x + back[:tokens]
    scaled = back[tokens:]
    input_grad = grad_y + inv_std * (
        scaled
        - jnp.mean(scaled, axis=-1, keepdims=True)
        - normed * jnp.mean(scaled * normed, axis=-1, keepdims=True)
    )
    owned = flat_from_rows(grad_rows, grad_tail[:13], spread, count)
    new_params, new_first, new_second = adam_update(params, owned, first_moment, second_moment)
    return (
        result.reshape(block_input.shape),
        input_grad.reshape(block_input.shape),
        owned,
        new_params,
        new_first,
        new_second,
    )


def solution(mesh):
    vector, tokens = P(AXES), P(None, AXES, None)
    dp, cores = mesh.shape["dp"], mesh.shape["fsdp"]
    if dp == PLANES * PLANES and cores == 2:
        step = functools.partial(sliced_step, PLANES, dp // PLANES)
    else:
        step = functools.partial(body, dp * cores)
    return jax.shard_map(
        step,
        mesh=mesh,
        in_specs=(tokens, tokens, P(None, AXES), vector, vector, vector),
        out_specs=(tokens, tokens, vector, vector, vector, vector),
        check_vma=False,
    )
```

```python
import functools
import math

import jax
import jax.numpy as jnp
from jax import lax
from jax.experimental import pallas as pl
from jax.experimental.pallas import tpu as pltpu
from jax.sharding import PartitionSpec as P


D = 768
FF = 3072
HEADS = 12
HEAD_DIM = 64
ROT = 16
STEP = 3


NORM_EPS = 1e-05
BETA_ONE = 0.9
BETA_TWO = 0.95
LEARN_RATE = 0.05
WEIGHT_DECAY = 0.1
ADAM_EPS = 1e-08


def layout_shapes():
    return [
        (D, 3 * D),
        (D, D),
        (D, FF),
        (FF, D),
        (3 * D,),
        (D,),
        (FF,),
        (D,),
        (D,),
        (D,),
        (D,),
        (D,),
    ]


def unpack_flat(flat_vec):
    pieces_out = []
    offset = 0
    for item_shape in layout_shapes():
        length = math.prod(item_shape)
        pieces_out.append(flat_vec[offset : offset + length].reshape(item_shape))
        offset += length
    return pieces_out


def product(form, left, right):
    return jnp.einsum(form, left, right, preferred_element_type=jnp.float32)


def block_tables(seg_rows):
    row_count = seg_rows.shape[1]
    row_idx = jnp.arange(row_count)
    same_seq = seg_rows[:, :, None] == seg_rows[:, None, :]
    earlier = row_idx[None, :] < row_idx[:, None]
    diagonal = row_idx[None, :] == row_idx[:, None]
    causal = row_idx[None, :] <= row_idx[:, None]
    allowed = same_seq & causal[None] & ((seg_rows[:, :, None] >= 0) | diagonal[None])
    position = jnp.sum(jnp.where(same_seq & earlier[None], 1, 0), axis=2).astype(jnp.float32)
    inv_freq = 10000.0 ** (-(jnp.arange(ROT // 2, dtype=jnp.float32) * 2.0) / ROT)
    angles = position[:, :, None] * inv_freq[None, None, :]
    return (allowed, jnp.cos(angles)[:, :, None, :], jnp.sin(angles)[:, :, None, :])


def rotate(vecs, cos_t, sin_t):
    half_rot = ROT // 2
    first = vecs[..., :half_rot]
    second = vecs[..., half_rot:ROT]
    return jnp.concatenate(
        [first * cos_t - second * sin_t, second * cos_t + first * sin_t, vecs[..., ROT:]], axis=-1
    )


def unrotate(vecs, cos_t, sin_t):
    half_rot = ROT // 2
    first = vecs[..., :half_rot]
    second = vecs[..., half_rot:ROT]
    return jnp.concatenate(
        [first * cos_t + second * sin_t, second * cos_t - first * sin_t, vecs[..., ROT:]], axis=-1
    )


def layer_norm(flat_x, gain, shift):
    row_mean = jnp.mean(flat_x, axis=-1, keepdims=True)
    centred = flat_x - row_mean
    row_var = jnp.mean(centred * centred, axis=-1, keepdims=True)
    inv_std = lax.rsqrt(row_var + NORM_EPS)
    normed = centred * inv_std
    return (
        normed,
        inv_std,
        (normed * gain.astype(jnp.float32) + shift.astype(jnp.float32)).astype(jnp.bfloat16),
    )


def norm_back(grad_act, normed, inv_std, gain):
    grad_gain = jnp.sum(grad_act * normed, axis=0)
    grad_shift = jnp.sum(grad_act, axis=0)
    scaled = grad_act * gain.astype(jnp.float32)
    grad_in = inv_std * (
        scaled
        - jnp.mean(scaled, axis=-1, keepdims=True)
        - normed * jnp.mean(scaled * normed, axis=-1, keepdims=True)
    )
    return (grad_gain, grad_shift, grad_in)


def softmax_rows(query_bf, key_bf, allowed, log_total):
    scores = product("gqhd,gkhd->ghqk", query_bf, key_bf) * HEAD_DIM ** (-0.5)
    mask_b = allowed[:, None]
    masked = jnp.where(mask_b, scores, -jnp.inf)
    if log_total is None:
        top_score = jnp.max(masked, axis=-1, keepdims=True)
        expo = jnp.where(mask_b, jnp.exp(masked - top_score), 0.0)
        log_total = top_score + jnp.log(jnp.sum(expo, axis=-1, keepdims=True))
    prob_rows = jnp.where(mask_b, jnp.exp(masked - log_total), 0.0)
    return (prob_rows, log_total)


def forward(x_rows, seg_rows, weights):
    (
        w_qkv,
        w_out,
        w_up,
        w_down,
        b_qkv,
        b_out,
        b_up,
        b_down,
        gain_one,
        shift_one,
        gain_two,
        shift_two,
    ) = weights
    group_count, row_count = seg_rows.shape
    allowed, cos_t, sin_t = block_tables(seg_rows)
    flat_x = x_rows.reshape(group_count * row_count, D)
    normed_one, inv_one, act_one = layer_norm(flat_x, gain_one, shift_one)
    normed_two, inv_two, act_two = layer_norm(flat_x, gain_two, shift_two)
    qkv_rows = jnp.dot(act_one, w_qkv, preferred_element_type=jnp.float32) + b_qkv.astype(
        jnp.float32
    )
    qkv_rows = qkv_rows.reshape(group_count, row_count, 3, HEADS, HEAD_DIM)
    query_bf = rotate(qkv_rows[:, :, 0], cos_t, sin_t).astype(jnp.bfloat16)
    key_bf = rotate(qkv_rows[:, :, 1], cos_t, sin_t).astype(jnp.bfloat16)
    value_bf = qkv_rows[:, :, 2].astype(jnp.bfloat16)
    prob_rows, log_total = softmax_rows(query_bf, key_bf, allowed, None)
    prob_bf = prob_rows.astype(jnp.bfloat16)
    attn_bf = (
        product("ghqk,gkhd->gqhd", prob_bf, value_bf)
        .astype(jnp.bfloat16)
        .reshape(group_count * row_count, D)
    )
    attn_out = jnp.dot(attn_bf, w_out, preferred_element_type=jnp.float32) + b_out.astype(
        jnp.float32
    )
    up_rows = jnp.dot(act_two, w_up, preferred_element_type=jnp.float32) + b_up.astype(jnp.float32)
    hidden_bf = jax.nn.gelu(up_rows, approximate=False).astype(jnp.bfloat16)
    mlp_out = jnp.dot(hidden_bf, w_down, preferred_element_type=jnp.float32) + b_down.astype(
        jnp.float32
    )
    result = flat_x + attn_out + mlp_out
    kept_state = (
        normed_one,
        inv_one,
        act_one,
        normed_two,
        inv_two,
        act_two,
        query_bf,
        key_bf,
        value_bf,
        log_total,
        attn_bf,
        up_rows,
        hidden_bf,
        allowed,
        cos_t,
        sin_t,
        seg_rows,
    )
    return (result.reshape(group_count, row_count, D), kept_state)


def backward(kept_state, grad_rows, weights):
    (w_qkv, w_out, w_up, w_down, _, _, _, _, gain_one, _, gain_two, _) = weights
    (
        normed_one,
        inv_one,
        act_one,
        normed_two,
        inv_two,
        act_two,
        query_bf,
        key_bf,
        value_bf,
        log_total,
        attn_bf,
        up_rows,
        hidden_bf,
        allowed,
        cos_t,
        sin_t,
        seg_rows,
    ) = kept_state
    group_count, row_count = seg_rows.shape
    valid = (seg_rows >= 0).astype(jnp.float32).reshape(group_count * row_count, 1)
    grad_y = grad_rows.reshape(group_count * row_count, D) * valid
    grad_y_bf = grad_y.astype(jnp.bfloat16)
    grad_bias = jnp.sum(grad_y, axis=0)
    grad_w_down = jnp.dot(hidden_bf.T, grad_y_bf, preferred_element_type=jnp.float32)
    grad_w_out = jnp.dot(attn_bf.T, grad_y_bf, preferred_element_type=jnp.float32)
    grad_hidden = jnp.dot(grad_y_bf, w_down.T, preferred_element_type=jnp.float32)
    cdf_part = 0.5 * (1.0 + jax.scipy.special.erf(up_rows * 0.7071067811865476))
    pdf_part = jnp.exp(-0.5 * up_rows * up_rows) * 0.3989422804014327
    grad_up = grad_hidden * (cdf_part + up_rows * pdf_part)
    grad_b_up = jnp.sum(grad_up, axis=0)
    grad_up_bf = grad_up.astype(jnp.bfloat16)
    grad_w_up = jnp.dot(act_two.T, grad_up_bf, preferred_element_type=jnp.float32)
    grad_act_two = jnp.dot(grad_up_bf, w_up.T, preferred_element_type=jnp.float32)
    grad_attn = jnp.dot(grad_y_bf, w_out.T, preferred_element_type=jnp.float32).astype(jnp.bfloat16)
    grad_attn = grad_attn.reshape(group_count, row_count, HEADS, HEAD_DIM)
    prob_rows, _ = softmax_rows(query_bf, key_bf, allowed, log_total)
    prob_bf = prob_rows.astype(jnp.bfloat16)
    grad_value = product("ghqk,gqhd->gkhd", prob_bf, grad_attn)
    grad_prob = product("gqhd,gkhd->ghqk", grad_attn, value_bf)
    delta_rows = jnp.sum(prob_rows * grad_prob, axis=-1, keepdims=True)
    grad_score_bf = (prob_rows * (grad_prob - delta_rows) * HEAD_DIM ** (-0.5)).astype(jnp.bfloat16)
    grad_query = unrotate(product("ghqk,gkhd->gqhd", grad_score_bf, key_bf), cos_t, sin_t)
    grad_key = unrotate(product("ghqk,gqhd->gkhd", grad_score_bf, query_bf), cos_t, sin_t)
    grad_qkv = jnp.stack([grad_query, grad_key, grad_value], axis=2).reshape(
        group_count * row_count, 3 * D
    )
    grad_b_qkv = jnp.sum(grad_qkv, axis=0)
    grad_qkv_bf = grad_qkv.astype(jnp.bfloat16)
    grad_w_qkv = jnp.dot(act_one.T, grad_qkv_bf, preferred_element_type=jnp.float32)
    grad_act_one = jnp.dot(grad_qkv_bf, w_qkv.T, preferred_element_type=jnp.float32)
    grad_gain_one, grad_shift_one, back_one = norm_back(grad_act_one, normed_one, inv_one, gain_one)
    grad_gain_two, grad_shift_two, back_two = norm_back(grad_act_two, normed_two, inv_two, gain_two)
    input_grad = (grad_y + back_one + back_two).reshape(group_count, row_count, D)
    grads = (
        grad_w_qkv,
        grad_w_out,
        grad_w_up,
        grad_w_down,
        grad_b_qkv,
        grad_bias,
        grad_b_up,
        grad_bias,
        grad_gain_one,
        grad_shift_one,
        grad_gain_two,
        grad_shift_two,
    )
    return (input_grad, grads)


def adam_update(params, grads, first_moment, second_moment):
    new_first = BETA_ONE * first_moment + (1.0 - BETA_ONE) * grads
    new_second = BETA_TWO * second_moment + (1.0 - BETA_TWO) * grads * grads
    first_hat = new_first / (1.0 - BETA_ONE**STEP)
    second_hat = new_second / (1.0 - BETA_TWO**STEP)
    new_params = params - LEARN_RATE * (
        first_hat / (jnp.sqrt(second_hat) + ADAM_EPS) + WEIGHT_DECAY * params
    )
    return (new_params, new_first, new_second)


AXES = ("dp", "fsdp")
TAIL = 13 * D


def rows_from_flat(flat, spread, count):
    me = lax.axis_index(AXES)
    tail = flat[flat.shape[0] - TAIL :]
    before = lax.ppermute(tail, AXES, [(i, (i + 1) % count) for i in range(count)])
    joined = jnp.concatenate([before, flat])
    rows = lax.dynamic_slice(joined, (TAIL - spread * me,), (flat.shape[0] - spread,))
    return rows.reshape(-1, D), tail.reshape(-1, D)


def flat_from_rows(rows, tail, spread, count):
    me = lax.axis_index(AXES)
    head = rows.reshape(-1)[:TAIL]
    after = lax.ppermute(head, AXES, [(i, (i - 1) % count) for i in range(count)])
    after = jnp.where(me == count - 1, tail.reshape(-1), after)
    joined = jnp.concatenate([rows.reshape(-1), after])
    return lax.dynamic_slice(joined, (spread * me,), (rows.size + spread,))


def body(count, block_input, out_grad, seg_ids, params, first_moment, second_moment):
    spread = TAIL // count
    row_count = (params.shape[0] - spread) // D
    rows, tail = rows_from_flat(params.astype(jnp.bfloat16), spread, count)
    sent = jnp.concatenate([rows, jnp.pad(tail, ((0, 3), (0, 0)))])
    whole = lax.all_gather(sent, AXES, axis=0, tiled=False)
    matrices = whole[:, :row_count].reshape(-1)
    weights = unpack_flat(jnp.concatenate([matrices, whole[count - 1, row_count : row_count + 13].reshape(-1)]))
    result, kept_state = forward(block_input, seg_ids, weights)
    back_x, grads = backward(kept_state, out_grad, weights)
    big = jnp.concatenate([g.astype(jnp.bfloat16).reshape(-1, D) for g in grads[:4]])
    small = jnp.concatenate([g.astype(jnp.bfloat16).reshape(-1, D) for g in grads[4:]])
    small = jnp.pad(small, ((0, 3), (0, 0)))
    spots = jnp.where(jnp.arange(count)[:, None, None] == count - 1, small[None], jnp.zeros((), jnp.bfloat16))
    out = jnp.concatenate([big.reshape(count, row_count, D), spots], axis=1)
    owned = lax.psum_scatter(out, AXES, scatter_dimension=0, tiled=False).astype(jnp.float32)
    owned_grads = flat_from_rows(owned[:row_count], owned[row_count : row_count + 13], spread, count)
    new_params, new_first, new_second = adam_update(params, owned_grads, first_moment, second_moment)
    return (result, back_x, owned_grads, new_params, new_first, new_second)


BF = jnp.bfloat16
F32 = jnp.float32
PLANES = 4
PART = D // PLANES
SPOT = 96
SLAB = 352
EARLY = 80
STARTS = (0, 80, 176, 256)


def dot_nn(a, b):
    return lax.dot_general(a, b, (((1,), (0,)), ((), ())), preferred_element_type=F32)


def dot_nt(a, b):
    return lax.dot_general(a, b, (((1,), (1,)), ((), ())), preferred_element_type=F32)


def dot_tn(a, b):
    return lax.dot_general(a, b, (((0,), (0,)), ((), ())), preferred_element_type=F32)


def lanes_of(width):
    return lax.broadcasted_iota(jnp.int32, (1, width), 1)


def group_mask(index, width=D, size=PART):
    lane = lanes_of(width)
    return (lane >= index * size) & (lane < (index + 1) * size)


def turned(value, shift):
    shift = shift % value.shape[-1]
    return value if shift == 0 else pltpu.roll(value, shift, value.ndim - 1)


def spread_groups(parts, first):
    total = None
    for group, part in enumerate(parts):
        moved = turned(part, PART * (group - first))
        total = moved if total is None else jnp.where(group_mask(group), moved, total)
    if len(parts) < PLANES:
        total = jnp.where(lanes_of(D) < PART * len(parts), total, 0.0)
    return total


def count_of(value, *limits):
    return sum(jnp.where(value >= limit, 1, 0) for limit in limits)


def pick_matrix(kinds, size):
    row = lax.broadcasted_iota(jnp.int32, (SPOT, SPOT), 0)
    col = lax.broadcasted_iota(jnp.int32, (SPOT, SPOT), 1)
    kind = count_of(row, *range(size, SPOT, size))
    return jnp.where(col == kinds * (row - size * kind) + kind, 1.0, 0.0).astype(BF)


def order_columns(perm_ref, by_head):
    place = lax.broadcasted_iota(jnp.int32, (8, D), 1)
    part = count_of(place, PART, 2 * PART, 3 * PART)
    inner = place - PART * part
    if by_head:
        kind = count_of(inner, HEAD_DIM, 2 * HEAD_DIM)
        early = part + jnp.where(kind == 0, 0, jnp.where(kind == 1, 5, 9))
        late = jnp.where(kind == 0, 3, jnp.where(kind == 1, 4, 8))
        source = HEAD_DIM * (jnp.where(part < 3, early, late) - kind) + inner
    else:
        run = count_of(inner, *range(24, PART, 24))
        source = (SPOT - 24) * run + 24 * part + inner
    row = lax.broadcasted_iota(jnp.int32, (D, D), 0)
    perm_ref[...] = jnp.where(row == source[0:1], 1.0, 0.0).astype(BF)


def pack_kernel(where_ref, rows_ref, tail_ref, *refs):
    out_refs, (spot, perm, mixed) = refs[:PLANES], refs[PLANES:]
    plane, place = where_ref[0], where_ref[1]
    device = 8 * plane + place
    with_heads = device < 8
    with_hidden = (device >= 10) & (device < 22)
    spot[...] = jnp.zeros_like(spot)
    pl.when(with_heads)(lambda: order_columns(perm, True))
    pl.when(with_hidden)(lambda: order_columns(perm, False))

    @pl.when(with_heads | with_hidden)
    def _():
        mixed[...] = dot_nn(rows_ref[...].astype(BF), perm[...]).astype(BF)

    @pl.when(with_heads)
    def _():
        sort = pick_matrix(3, 32)
        for i in range(3):
            picked = dot_nn(sort, mixed[SPOT * i : SPOT * i + SPOT, :])
            for j in range(3):
                parts = [picked[32 * j + 8 * g : 32 * j + 8 * g + 8] for g in range(4)]
                for s in range(PLANES):
                    spot[s, 24 * i + 8 * j : 24 * i + 8 * j + 8, :] = spread_groups(parts, s)

    for i in range(3):
        block = 3 * device + i

        @pl.when((block >= 32) & (block < 64))
        def _():
            picked = dot_nn(pick_matrix(4, 24), mixed[SPOT * i : SPOT * i + SPOT, :])
            parts = [picked[24 * j : 24 * j + 24] for j in range(4)]
            start = 24 * i
            if i == 2:
                start = pl.multiple_of(jnp.where(block == 32, 0, 48), 8)
            for s in range(PLANES):
                spot[s, pl.ds(start, 24), :] = spread_groups(parts, s)

        @pl.when(block >= 64)
        def _():
            for s in range(PLANES):
                spot[s, 24 * i : 24 * i + 24, :] = rows_ref[
                    SPOT * i + 24 * s : SPOT * i + 24 * s + 24, :
                ]

    @pl.when(device == 8)
    def _():
        for s in range(3):
            spot[s, 0:64, :] = rows_ref[64 * s : 64 * s + 64, :]
        spot[3, 0:96, :] = rows_ref[192:288, :]

    @pl.when(device == 9)
    def _():
        for s in range(3):
            spot[s, 0:64, :] = rows_ref[32 + 64 * s : 96 + 64 * s, :]
        spot[3, 0:32, :] = rows_ref[0:32, :]
        spot[3, 32:96, :] = rows_ref[224:288, :]

    @pl.when(device == 10)
    def _():
        for s in range(3):
            spot[s, 24:88, :] = rows_ref[64 * s : 64 * s + 64, :]

    @pl.when(device == 31)
    def _():
        upper = tail_ref[0:8, :].astype(BF)
        order_columns(perm, True)
        by_head = dot_nn(upper, perm[...])
        order_columns(perm, False)
        by_hidden = dot_nn(upper, perm[...])
        for s in range(PLANES):
            spot[s, 80:81, :] = spread_groups([by_hidden[4 + j : 5 + j] for j in range(4)], s)
            spot[s, 81:82, :] = spread_groups([by_head[j : j + 1] for j in range(3)], s)
            spot[s, 82:83, :] = tail_ref[3:4, :]
            spot[s, 88:96, :] = tail_ref[8:16, :]

    for r in range(PLANES):
        out_refs[r][...] = spot[plane ^ r].astype(BF)


def unpack_kernel(where_ref, *refs):
    in_refs, (rows_ref, tail_ref, spot, perm, mixed) = refs[:PLANES], refs[PLANES:]
    plane, place = where_ref[0], where_ref[1]
    device = 8 * plane + place
    with_heads = device < 8
    with_hidden = (device >= 10) & (device < 22)
    for r in range(PLANES):
        spot[plane ^ r] = in_refs[r][...].astype(F32)
    pl.when(with_heads)(lambda: order_columns(perm, True))

    @pl.when(with_heads)
    def _():
        sort = pick_matrix(3, 32)
        for i in range(3):
            sorted_ = []
            for j in range(3):
                base = 24 * i + 8 * j
                parts = [spot[s, base : base + 8, :] for s in range(PLANES)]
                sorted_.extend(spread_groups(parts, g) for g in range(4))
            block_rows = jnp.concatenate(sorted_, axis=0).astype(BF)
            mixed[SPOT * i : SPOT * i + SPOT, :] = dot_tn(sort, block_rows).astype(BF)

    @pl.when(with_hidden)
    def _():
        order_columns(perm, False)
        mixed[...] = jnp.zeros_like(mixed)

    for i in range(3):
        block = 3 * device + i

        @pl.when((block >= 32) & (block < 64))
        def _():
            start = 24 * i
            if i == 2:
                start = pl.multiple_of(jnp.where(block == 32, 0, 48), 8)
            parts = [spot[s, pl.ds(start, 24), :] for s in range(PLANES)]
            block_rows = jnp.concatenate([spread_groups(parts, j) for j in range(4)], axis=0)
            mixed[SPOT * i : SPOT * i + SPOT, :] = dot_tn(
                pick_matrix(4, 24), block_rows.astype(BF)
            ).astype(BF)

    @pl.when(with_heads | with_hidden)
    def _():
        rows_ref[...] = dot_nt(mixed[...], perm[...])

    for i in range(3):

        @pl.when(3 * device + i >= 64)
        def _():
            for s in range(PLANES):
                rows_ref[SPOT * i + 24 * s : SPOT * i + 24 * s + 24, :] = spot[
                    s, 24 * i : 24 * i + 24, :
                ]

    @pl.when(device == 8)
    def _():
        for s in range(3):
            rows_ref[64 * s : 64 * s + 64, :] = spot[s, 0:64, :]
        rows_ref[192:288, :] = spot[3, 0:96, :]

    @pl.when(device == 9)
    def _():
        for s in range(3):
            rows_ref[32 + 64 * s : 96 + 64 * s, :] = spot[s, 0:64, :]
        rows_ref[0:32, :] = spot[3, 0:32, :]
        rows_ref[224:288, :] = spot[3, 32:96, :]

    @pl.when(device == 10)
    def _():
        for s in range(3):
            rows_ref[64 * s : 64 * s + 64, :] = spot[s, 24:88, :]

    tail_ref[...] = jnp.zeros_like(tail_ref)

    @pl.when(device == 31)
    def _():
        order_columns(perm, False)
        whole = [spot[s, 80:81, :] for s in range(PLANES)]
        for j in range(4):
            row = jnp.broadcast_to(spread_groups(whole, j), (8, D)).astype(BF)
            tail_ref[4 + j : 5 + j, :] = dot_nt(row, perm[...])[0:1]
        order_columns(perm, True)
        whole = [spot[s, 81:82, :] for s in range(PLANES)]
        for j in range(3):
            row = jnp.broadcast_to(spread_groups(whole, j), (8, D)).astype(BF)
            tail_ref[j : j + 1, :] = dot_nt(row, perm[...])[0:1]
        tail_ref[3:4, :] = sum(spot[s, 82:83, :] for s in range(PLANES))
        tail_ref[8:16, :] = sum(spot[s, 88:96, :] for s in range(PLANES))


def slab_start(plane):
    start = jnp.where(plane == 1, STARTS[1], jnp.where(plane == 2, STARTS[2], STARTS[3]))
    return pl.multiple_of(jnp.where(plane == 0, 0, start), 16)


def slab_kernel(where_ref, *refs):
    in_refs, (first, second) = refs[:PLANES], refs[PLANES:]
    for r, ref in enumerate(in_refs):
        source = where_ref[0] ^ r

        @pl.when(source == 0)
        def _():
            first[0:80, :] = ref[0:80, :]

        @pl.when(source == 1)
        def _():
            first[80:176, :] = ref[...]

        @pl.when(source == 2)
        def _():
            second[0:80, :] = ref[0:80, :]

        @pl.when(source == 3)
        def _():
            second[80:160, :] = ref[0:80, :]
            first[176:192, :] = ref[80:96, :]


def split_kernel(where_ref, *refs):
    early, late, out_refs, total = refs[:4], refs[4:8], refs[8:12], refs[12]

    def sum_of(parts):
        a, b, c, d = (part[...].astype(F32) for part in parts)
        return (a + b) + (c + d)

    total[0:EARLY, :] = sum_of(early)
    total[EARLY:SLAB, :] = sum_of(late)
    for r in range(PLANES):
        out_refs[r][...] = total[pl.ds(slab_start(where_ref[0] ^ r), SPOT), :].astype(BF)


def place_of(index, spot, core):
    return 2 * (spot ^ (index % 4)) + (core if index < 4 else 1 - core)


def row_sum(x):
    return jnp.sum(x, axis=0, keepdims=True)


def attention_kernel(where_ref, *refs):
    act_refs, cot_refs, slab_refs, grad_refs = refs[:4], refs[4:8], refs[8:16], refs[16:24]
    (y_ref, dn_ref, g_out_ref, up_low, tails, g_tails, normed, grad_y,
     w_out, packed, w_qkv, bf_out, bf_qkv, qkv, attn, g_qkv, g_attn) = refs[24:]
    plane, spot, core = where_ref[0], where_ref[1], where_ref[2]
    lane = lanes_of(D)

    w_out[...] = jnp.zeros_like(w_out)
    for index, ref in enumerate(slab_refs):
        q = place_of(index, spot, core)
        for i in range(3):
            for j in range(3):
                packed[j, pl.ds(pl.multiple_of(24 * q + 8 * i, 8), 8), :] = ref[0:80, :][
                    24 * i + 8 * j : 24 * i + 8 * j + 8
                ].astype(F32)
        one = ref[80:176, :].astype(F32)

        @pl.when(q >= 3)
        def _():
            up_low[pl.ds(pl.multiple_of(72 * q - 192, 8), 72), :] = one[0:72]

        @pl.when(q == 2)
        def _():
            up_low[0:24, :] = one[0:24]

            @pl.when(plane < 3)
            def _():
                w_out[128:192, :] = one[24:88]

        @pl.when((q < 2) & (plane < 3))
        def _():
            w_out[pl.ds(pl.multiple_of(64 * q, 8), 64), :] = one[0:64]

        @pl.when((q < 2) & (plane == 3))
        def _():
            w_out[pl.ds(pl.multiple_of(96 * q, 8), 96), :] = one[0:96]

        @pl.when(q == 7)
        def _():
            tails[...] = ref[176:192, :].astype(F32)

    for j in range(3):
        for i in range(4):
            moved = turned(packed[j], -PART * i)[:, 0:256]
            moved = jnp.where(lanes_of(256) < PART, moved, 0.0)
            w_qkv[:, i, :, 256 * j : 256 * j + 256] = moved.reshape(24, 8, 256)
    bf_out[...] = w_out[...].astype(BF)
    bf_qkv[...] = w_qkv[...].reshape(D, D).astype(BF)

    for r in range(4):
        normed[128 * r : 128 * r + 128, :] = act_refs[r][0:128, :]
        grad_y[128 * r : 128 * r + 128, :] = cot_refs[r][...]
    flat_bias = tails[1:2, :]
    bias_qkv = jnp.zeros((1, D), F32)
    for j in range(3):
        keep = (lane >= 256 * j) & (lane < 256 * j + PART)
        bias_qkv = jnp.where(keep, turned(flat_bias, 64 * j), bias_qkv)
    bias_y = jnp.where(plane == 0, tails[2:3, :] + tails[8:9, :], 0.0)
    gain_one, shift_one = tails[9:10, :], tails[10:11, :]
    wide = normed[...].astype(F32)
    act_one = (wide * gain_one + shift_one).astype(BF)
    qkv[...] = dot_nn(act_one, bf_qkv[...]) + bias_qkv
    g_attn[...] = dot_nt(grad_y[...], bf_out[...]).astype(BF)

    rows = lax.broadcasted_iota(jnp.int32, (128, 128), 0)
    cols = lax.broadcasted_iota(jnp.int32, (128, 128), 1)
    same_block = (rows < 64) == (cols < 64)
    eye = rows == cols
    in_head = lanes_of(128) % 64
    freq = jnp.exp((in_head % 8).astype(F32) * (-2.0 * math.log(10000.0) / ROT))
    low_half = lanes_of(128) < 64
    for r in range(4):
        span = slice(128 * r, 128 * r + 128)
        seg_row = jnp.broadcast_to(act_refs[r][128:144, 0:128].astype(F32)[0:1], (128, 128))
        seg_col = jnp.sum(jnp.where(eye, seg_row, 0.0), axis=1, keepdims=True)
        same = (seg_col == seg_row) & same_block
        allowed = same & (cols <= rows) & ((seg_col >= 0.0) | eye)
        position = jnp.sum(jnp.where(same & (cols < rows), 1.0, 0.0), axis=1, keepdims=True)
        angle = position * freq
        cos_t = jnp.where(in_head < ROT, jnp.cos(angle), 1.0)
        sine = jnp.sin(angle)
        sin_a = jnp.where(in_head < 8, sine, 0.0)
        sin_b = jnp.where((in_head >= 8) & (in_head < ROT), sine, 0.0)

        def rotated(x):
            return x * cos_t - turned(x, -8) * sin_a + turned(x, 8) * sin_b

        def unrotated(x):
            return x * cos_t + turned(x, -8) * sin_a - turned(x, 8) * sin_b

        for tile in range(2):
            at = [256 * j + 128 * tile for j in range(3)]
            query = rotated(qkv[span, at[0] : at[0] + 128]).astype(BF)
            key = rotated(qkv[span, at[1] : at[1] + 128]).astype(BF)
            value = qkv[span, at[2] : at[2] + 128].astype(BF)
            g_out = g_attn[span, 128 * tile : 128 * tile + 128]
            parts = []
            for half in range(2 - tile):
                mask = low_half if half == 0 else jnp.logical_not(low_half)
                key_h = jnp.where(mask, key, jnp.zeros_like(key))
                value_h = jnp.where(mask, value, jnp.zeros_like(value))
                scores = dot_nt(query, key_h) * HEAD_DIM ** (-0.5)
                masked = jnp.where(allowed, scores, -1e30)
                top = jnp.max(masked, axis=1, keepdims=True)
                expo = jnp.where(allowed, jnp.exp(masked - top), 0.0)
                prob = expo * (1.0 / jnp.sum(expo, axis=1, keepdims=True))
                prob_bf = prob.astype(BF)
                g_prob = dot_nt(g_out, value_h)
                delta = jnp.sum(prob * g_prob, axis=1, keepdims=True)
                g_score = (prob * (g_prob - delta) * HEAD_DIM ** (-0.5)).astype(BF)
                parts.append(
                    (
                        dot_nn(prob_bf, value),
                        dot_tn(prob_bf, g_out),
                        dot_nn(g_score, key),
                        dot_tn(g_score, query),
                    )
                )
            if tile == 0:
                o, gv, gq, gk = [jnp.where(low_half, a, b) for a, b in zip(*parts)]
            else:
                o, gv, gq, gk = [jnp.where(low_half, a, 0.0) for a in parts[0]]
            attn[span, 128 * tile : 128 * tile + 128] = o.astype(BF)
            g_qkv[span, at[0] : at[0] + 128] = unrotated(gq)
            g_qkv[span, at[1] : at[1] + 128] = unrotated(gk)
            g_qkv[span, at[2] : at[2] + 128] = gv
    y_ref[...] = dot_nn(attn[...], bf_out[...]) + bias_y
    g_out_ref[...] = dot_tn(attn[...], grad_y[...])
    g_bias_qkv = jnp.sum(g_qkv[...], axis=0, keepdims=True)
    g_qkv_bf = g_qkv[...].astype(BF)
    w_qkv[...] = dot_tn(act_one, g_qkv_bf).reshape(24, 4, 8, D)
    g_act_one = dot_nt(g_qkv_bf, bf_qkv[...])
    dn_ref[...] = g_act_one * gain_one
    flat_bias = jnp.zeros((1, D), F32)
    for j in range(3):
        keep = (lane >= PART * j) & (lane < PART * (j + 1))
        flat_bias = jnp.where(keep, turned(g_bias_qkv, -64 * j), flat_bias)
    g_bias_y = row_sum(grad_y[0:128, :].astype(F32))
    g_tails[...] = jnp.zeros_like(g_tails)
    g_tails[1:2, :] = flat_bias
    g_tails[2:3, :] = g_bias_y
    g_tails[8:9, :] = g_bias_y
    g_tails[9:10, :] = row_sum(g_act_one * wide)
    g_tails[10:11, :] = row_sum(g_act_one)
    for j in range(3):
        total = None
        for i in range(4):
            piece = w_qkv[:, i, :, 256 * j : 256 * j + 256].reshape(PART, 256)
            piece = jnp.where(lanes_of(256) < PART, piece, 0.0)
            piece = jnp.concatenate([piece, jnp.zeros((PART, 512), F32)], axis=1)
            piece = turned(piece, PART * i)
            total = piece if total is None else total + piece
        packed[j] = total
    for index, ref in enumerate(grad_refs):
        q = place_of(index, spot, core)
        pieces = [
            packed[j, pl.ds(pl.multiple_of(24 * q + 8 * i, 8), 8), :]
            for i in range(3)
            for j in range(3)
        ]
        pieces.append(jnp.zeros((8, D), F32))
        ref[...] = jnp.concatenate(pieces, axis=0).astype(BF)


def feed_forward_kernel(where_ref, *refs):
    (y_ref, dn_ref, g_out_ref, up_low, tails, g_tails, normed, grad_y) = refs[:8]
    slab_refs, grad_refs, back_refs = refs[8:16], refs[16:24], refs[24:28]
    w_up, w_down, bf_up, bf_down, up, slab = refs[28:]
    plane, spot, core = where_ref[0], where_ref[1], where_ref[2]
    w_up[0:384, :] = up_low[...]
    for index, ref in enumerate(slab_refs):
        q = place_of(index, spot, core)
        two = ref[0:80, :].astype(F32)
        three = ref[80:160, :].astype(F32)

        @pl.when(q < 5)
        def _():
            w_up[pl.ds(pl.multiple_of(384 + 72 * q, 8), 72), :] = two[0:72]

        @pl.when(q == 5)
        def _():
            w_up[744:768, :] = two[0:24]
            w_down[0:48, :] = two[24:72]

        @pl.when(q > 5)
        def _():
            w_down[pl.ds(pl.multiple_of(72 * q - 384, 8), 72), :] = two[0:72]

        w_down[pl.ds(pl.multiple_of(192 + 72 * q, 8), 72), :] = three[0:72]

    bf_up[...] = w_up[...].astype(BF)
    bf_down[...] = w_down[...].astype(BF)
    bias_up = tails[0:1, :]
    gain_two, shift_two = tails[11:12, :], tails[12:13, :]
    wide = normed[...].astype(F32)
    act_two = (wide * gain_two + shift_two).astype(BF)
    up[...] = dot_nn(act_two, bf_up[...]) + bias_up
    cdf = 0.5 * (1.0 + lax.erf(up[...] * 0.7071067811865476))
    hidden = (up[...] * cdf).astype(BF)
    y = y_ref[...] + dot_nn(hidden, bf_down[...])
    for r in range(4):
        back_refs[r][0:128, :] = y[128 * r : 128 * r + 128].astype(BF)
    w_down[...] = dot_tn(hidden, grad_y[...])
    pdf = jnp.exp(-0.5 * up[...] * up[...]) * 0.3989422804014327
    g_up = dot_nt(grad_y[...], bf_down[...]) * (cdf + up[...] * pdf)
    g_bias_up = row_sum(g_up)
    g_up_bf = g_up.astype(BF)
    w_up[...] = dot_tn(act_two, g_up_bf)
    g_act_two = dot_nt(g_up_bf, bf_up[...])
    dn = dn_ref[...] + g_act_two * gain_two
    for r in range(4):
        back_refs[r][128:256, :] = dn[128 * r : 128 * r + 128].astype(BF)
    slab[256:272, :] = g_tails[...]
    slab[256:257, :] = g_bias_up
    slab[267:268, :] = row_sum(g_act_two * wide)
    slab[268:269, :] = row_sum(g_act_two)
    for index, ref in enumerate(grad_refs):
        q = place_of(index, spot, core)

        @pl.when(q >= 3)
        def _():
            slab[0:72, :] = w_up[pl.ds(pl.multiple_of(72 * q - 192, 8), 72), :]

        @pl.when(q == 2)
        def _():
            slab[0:24, :] = w_up[0:24, :]
            slab[24:88, :] = g_out_ref[128:192, :]

        @pl.when((q < 2) & (plane < 3))
        def _():
            slab[0:64, :] = g_out_ref[pl.ds(pl.multiple_of(64 * q, 8), 64), :]

        @pl.when((q < 2) & (plane == 3))
        def _():
            slab[0:96, :] = g_out_ref[pl.ds(pl.multiple_of(96 * q, 8), 96), :]

        @pl.when(q < 5)
        def _():
            slab[96:168, :] = w_up[pl.ds(pl.multiple_of(384 + 72 * q, 8), 72), :]

        @pl.when(q == 5)
        def _():
            slab[96:120, :] = w_up[744:768, :]
            slab[120:168, :] = w_down[0:48, :]

        @pl.when(q > 5)
        def _():
            slab[96:168, :] = w_down[pl.ds(pl.multiple_of(72 * q - 384, 8), 72), :]

        slab[176:248, :] = w_down[pl.ds(pl.multiple_of(192 + 72 * q, 8), 72), :]
        ref[...] = slab[...].astype(BF)


def local_call(kernel, outs, scratch, limit, kept_out, where, *operands):
    vmem = pl.BlockSpec(memory_space=pltpu.VMEM)
    operands = [pltpu.with_memory_space_constraint(x, pltpu.VMEM) for x in operands]
    out_specs = jax.tree.map(lambda _: vmem, outs)
    if kept_out:
        outs = jax.tree.map(lambda x: pltpu.VMEM(x.shape, x.dtype), outs)
    return pl.pallas_call(
        kernel,
        out_shape=outs,
        in_specs=[pl.BlockSpec(memory_space=pltpu.SMEM)] + [vmem] * len(operands),
        out_specs=out_specs,
        scratch_shapes=scratch,
        compiler_params=pltpu.CompilerParams(vmem_limit_bytes=limit << 20),
    )(where, *operands)


def sliced_step(planes, places, *args):
    return sliced_body(planes, places, *args)


def sliced_body(planes, places, block_input, out_grad, seg_ids, params, first_moment, second_moment):
    count = planes * places * 2
    spread = TAIL // count
    dp, core = lax.axis_index("dp"), lax.axis_index("fsdp")
    plane, spot = dp // places, dp % places
    where_owner = jnp.stack([plane, 2 * spot + core]).astype(jnp.int32)
    where_spot = jnp.stack([plane, spot, core]).astype(jnp.int32)
    across = [
        [(i, (i // places ^ r) * places + i % places) for i in range(planes * places)]
        for r in range(planes)
    ]
    within = [
        [(i, i // places * places + (i % places ^ r)) for i in range(planes * places)]
        for r in range(places)
    ]

    def to_plane(value, r):
        return lax.ppermute(value, "dp", across[r]) if r else value

    def to_spot(value, r):
        return lax.ppermute(value, "dp", within[r]) if r else value

    def to_core(value):
        return lax.ppermute(value, "fsdp", [(0, 1), (1, 0)])

    micro, row_count, _ = block_input.shape
    tokens = micro * row_count
    flat_x = block_input.reshape(tokens, D)
    mean = jnp.mean(flat_x, axis=-1, keepdims=True)
    centred = flat_x - mean
    inv_std = lax.rsqrt(jnp.mean(centred * centred, axis=-1, keepdims=True) + NORM_EPS)
    normed = centred * inv_std
    valid = (seg_ids >= 0).astype(F32).reshape(tokens, 1)
    grad_y = out_grad.reshape(tokens, D) * valid
    seg_rows = jnp.pad(seg_ids.reshape(1, tokens).astype(BF), ((0, 15), (0, D - tokens)))
    sent_acts = jnp.concatenate([normed.astype(BF), seg_rows])
    acts = [to_plane(sent_acts, r) for r in range(3)]
    acts.append(to_plane(acts[2], 1))
    cots = [to_plane(grad_y.astype(BF), r) for r in range(3)]
    cots.append(to_plane(cots[2], 1))

    rows, tail = rows_from_flat(params, spread, count)
    tail = jnp.pad(tail, ((0, 3), (0, 0)))
    spot_shape = jax.ShapeDtypeStruct((SPOT, D), BF)

    def shaped(rows, kind=BF):
        return jax.ShapeDtypeStruct((rows, D), kind)

    sort_scratch = [
        pltpu.VMEM((planes, SPOT, D), F32),
        pltpu.VMEM((D, D), BF),
        pltpu.VMEM(rows.shape, BF),
    ]
    spots = local_call(
        pack_kernel, [spot_shape] * planes, sort_scratch, 8, True,
        where_owner, rows, tail,
    )
    spots = [to_plane(spots[r], r) for r in range(planes)]
    first, second = local_call(
        slab_kernel, [shaped(192), shaped(160)], [], 8, True, where_owner, *spots
    )
    firsts = [to_spot(first, r) for r in range(places)]
    seconds = [to_spot(second, r) for r in range(places)]
    firsts = firsts + [to_core(x) for x in firsts]
    total = planes * tokens
    outs = local_call(
        attention_kernel,
        [shaped(EARLY)] * 8
        + [
            shaped(total, F32),
            shaped(total, F32),
            shaped(256, F32),
            shaped(384, F32),
            shaped(16, F32),
            shaped(16, F32),
            shaped(total),
            shaped(total),
        ],
        [
            pltpu.VMEM((256, D), F32),
            pltpu.VMEM((3, PART, D), F32),
            pltpu.VMEM((24, 4, 8, D), F32),
            pltpu.VMEM((256, D), BF),
            pltpu.VMEM((D, D), BF),
            pltpu.VMEM((total, D), F32),
            pltpu.VMEM((total, 256), BF),
            pltpu.VMEM((total, D), F32),
            pltpu.VMEM((total, 256), BF),
        ],
        28, True, where_spot, *acts, *cots, *firsts,
    )
    early, kept = outs[:8], outs[8:]

    def summed(parts):
        paired = [
            (parts[r].astype(F32) + to_core(parts[4 + r]).astype(F32)).astype(BF)
            for r in range(places)
        ]
        return [to_spot(paired[r], r) for r in range(places)]

    early = summed(early)
    seconds = seconds + [to_core(x) for x in seconds]
    outs = local_call(
        feed_forward_kernel,
        [shaped(SLAB - EARLY)] * 8 + [shaped(2 * tokens)] * planes,
        [
            pltpu.VMEM((D, D), F32),
            pltpu.VMEM((D, D), F32),
            pltpu.VMEM((D, D), BF),
            pltpu.VMEM((D, D), BF),
            pltpu.VMEM((total, D), F32),
            pltpu.VMEM((SLAB - EARLY, D), F32),
        ],
        28, True, where_spot, *kept, *seconds,
    )
    late, backs = summed(outs[:8]), outs[8:]
    passed = to_plane(backs[3], 1)
    backs = [
        backs[0],
        to_plane(backs[1], 1),
        to_plane((backs[2].astype(F32) + passed.astype(F32)).astype(BF), 2),
    ]
    spots = local_call(
        split_kernel, [spot_shape] * planes, [pltpu.VMEM((SLAB, D), F32)], 12, True, where_owner, *early, *late
    )
    spots = [to_plane(spots[r], r) for r in range(planes)]
    grad_rows, grad_tail = local_call(
        unpack_kernel,
        [
            jax.ShapeDtypeStruct(rows.shape, F32),
            jax.ShapeDtypeStruct((16, D), F32),
        ],
        sort_scratch, 12, True,
        where_owner, *spots,
    )
    back = sum(b.astype(F32) for b in backs)
    result = flat_x + back[:tokens]
    scaled = back[tokens:]
    input_grad = grad_y + inv_std * (
        scaled
        - jnp.mean(scaled, axis=-1, keepdims=True)
        - normed * jnp.mean(scaled * normed, axis=-1, keepdims=True)
    )
    owned = flat_from_rows(grad_rows, grad_tail[:13], spread, count)
    new_params, new_first, new_second = adam_update(params, owned, first_moment, second_moment)
    return (
        result.reshape(block_input.shape),
        input_grad.reshape(block_input.shape),
        owned,
        new_params,
        new_first,
        new_second,
    )


def solution(mesh):
    vector, tokens = P(AXES), P(None, AXES, None)
    dp, cores = mesh.shape["dp"], mesh.shape["fsdp"]
    if dp == PLANES * PLANES and cores == 2:
        step = functools.partial(sliced_step, PLANES, dp // PLANES)
    else:
        step = functools.partial(body, dp * cores)
    return jax.shard_map(
        step,
        mesh=mesh,
        in_specs=(tokens, tokens, P(None, AXES), vector, vector, vector),
        out_specs=(tokens, tokens, vector, vector, vector, vector),
        check_vma=False,
    )
```

```python
import functools
import math

import jax
import jax.numpy as jnp
from jax import lax
from jax.experimental import pallas as pl
from jax.experimental.pallas import tpu as pltpu
from jax.sharding import PartitionSpec as P


D = 768
FF = 3072
HEADS = 12
HEAD_DIM = 64
ROT = 16
STEP = 3


NORM_EPS = 1e-05
BETA_ONE = 0.9
BETA_TWO = 0.95
LEARN_RATE = 0.05
WEIGHT_DECAY = 0.1
ADAM_EPS = 1e-08


def layout_shapes():
    return [
        (D, 3 * D),
        (D, D),
        (D, FF),
        (FF, D),
        (3 * D,),
        (D,),
        (FF,),
        (D,),
        (D,),
        (D,),
        (D,),
        (D,),
    ]


def unpack_flat(flat_vec):
    pieces_out = []
    offset = 0
    for item_shape in layout_shapes():
        length = math.prod(item_shape)
        pieces_out.append(flat_vec[offset : offset + length].reshape(item_shape))
        offset += length
    return pieces_out


def product(form, left, right):
    return jnp.einsum(form, left, right, preferred_element_type=jnp.float32)


def block_tables(seg_rows):
    row_count = seg_rows.shape[1]
    row_idx = jnp.arange(row_count)
    same_seq = seg_rows[:, :, None] == seg_rows[:, None, :]
    earlier = row_idx[None, :] < row_idx[:, None]
    diagonal = row_idx[None, :] == row_idx[:, None]
    causal = row_idx[None, :] <= row_idx[:, None]
    allowed = same_seq & causal[None] & ((seg_rows[:, :, None] >= 0) | diagonal[None])
    position = jnp.sum(jnp.where(same_seq & earlier[None], 1, 0), axis=2).astype(jnp.float32)
    inv_freq = 10000.0 ** (-(jnp.arange(ROT // 2, dtype=jnp.float32) * 2.0) / ROT)
    angles = position[:, :, None] * inv_freq[None, None, :]
    return (allowed, jnp.cos(angles)[:, :, None, :], jnp.sin(angles)[:, :, None, :])


def rotate(vecs, cos_t, sin_t):
    half_rot = ROT // 2
    first = vecs[..., :half_rot]
    second = vecs[..., half_rot:ROT]
    return jnp.concatenate(
        [first * cos_t - second * sin_t, second * cos_t + first * sin_t, vecs[..., ROT:]], axis=-1
    )


def unrotate(vecs, cos_t, sin_t):
    half_rot = ROT // 2
    first = vecs[..., :half_rot]
    second = vecs[..., half_rot:ROT]
    return jnp.concatenate(
        [first * cos_t + second * sin_t, second * cos_t - first * sin_t, vecs[..., ROT:]], axis=-1
    )


def layer_norm(flat_x, gain, shift):
    row_mean = jnp.mean(flat_x, axis=-1, keepdims=True)
    centred = flat_x - row_mean
    row_var = jnp.mean(centred * centred, axis=-1, keepdims=True)
    inv_std = lax.rsqrt(row_var + NORM_EPS)
    normed = centred * inv_std
    return (
        normed,
        inv_std,
        (normed * gain.astype(jnp.float32) + shift.astype(jnp.float32)).astype(jnp.bfloat16),
    )


def norm_back(grad_act, normed, inv_std, gain):
    grad_gain = jnp.sum(grad_act * normed, axis=0)
    grad_shift = jnp.sum(grad_act, axis=0)
    scaled = grad_act * gain.astype(jnp.float32)
    grad_in = inv_std * (
        scaled
        - jnp.mean(scaled, axis=-1, keepdims=True)
        - normed * jnp.mean(scaled * normed, axis=-1, keepdims=True)
    )
    return (grad_gain, grad_shift, grad_in)


def softmax_rows(query_bf, key_bf, allowed, log_total):
    scores = product("gqhd,gkhd->ghqk", query_bf, key_bf) * HEAD_DIM ** (-0.5)
    mask_b = allowed[:, None]
    masked = jnp.where(mask_b, scores, -jnp.inf)
    if log_total is None:
        top_score = jnp.max(masked, axis=-1, keepdims=True)
        expo = jnp.where(mask_b, jnp.exp(masked - top_score), 0.0)
        log_total = top_score + jnp.log(jnp.sum(expo, axis=-1, keepdims=True))
    prob_rows = jnp.where(mask_b, jnp.exp(masked - log_total), 0.0)
    return (prob_rows, log_total)


def forward(x_rows, seg_rows, weights):
    (
        w_qkv,
        w_out,
        w_up,
        w_down,
        b_qkv,
        b_out,
        b_up,
        b_down,
        gain_one,
        shift_one,
        gain_two,
        shift_two,
    ) = weights
    group_count, row_count = seg_rows.shape
    allowed, cos_t, sin_t = block_tables(seg_rows)
    flat_x = x_rows.reshape(group_count * row_count, D)
    normed_one, inv_one, act_one = layer_norm(flat_x, gain_one, shift_one)
    normed_two, inv_two, act_two = layer_norm(flat_x, gain_two, shift_two)
    qkv_rows = jnp.dot(act_one, w_qkv, preferred_element_type=jnp.float32) + b_qkv.astype(
        jnp.float32
    )
    qkv_rows = qkv_rows.reshape(group_count, row_count, 3, HEADS, HEAD_DIM)
    query_bf = rotate(qkv_rows[:, :, 0], cos_t, sin_t).astype(jnp.bfloat16)
    key_bf = rotate(qkv_rows[:, :, 1], cos_t, sin_t).astype(jnp.bfloat16)
    value_bf = qkv_rows[:, :, 2].astype(jnp.bfloat16)
    prob_rows, log_total = softmax_rows(query_bf, key_bf, allowed, None)
    prob_bf = prob_rows.astype(jnp.bfloat16)
    attn_bf = (
        product("ghqk,gkhd->gqhd", prob_bf, value_bf)
        .astype(jnp.bfloat16)
        .reshape(group_count * row_count, D)
    )
    attn_out = jnp.dot(attn_bf, w_out, preferred_element_type=jnp.float32) + b_out.astype(
        jnp.float32
    )
    up_rows = jnp.dot(act_two, w_up, preferred_element_type=jnp.float32) + b_up.astype(jnp.float32)
    hidden_bf = jax.nn.gelu(up_rows, approximate=False).astype(jnp.bfloat16)
    mlp_out = jnp.dot(hidden_bf, w_down, preferred_element_type=jnp.float32) + b_down.astype(
        jnp.float32
    )
    result = flat_x + attn_out + mlp_out
    kept_state = (
        normed_one,
        inv_one,
        act_one,
        normed_two,
        inv_two,
        act_two,
        query_bf,
        key_bf,
        value_bf,
        log_total,
        attn_bf,
        up_rows,
        hidden_bf,
        allowed,
        cos_t,
        sin_t,
        seg_rows,
    )
    return (result.reshape(group_count, row_count, D), kept_state)


def backward(kept_state, grad_rows, weights):
    (w_qkv, w_out, w_up, w_down, _, _, _, _, gain_one, _, gain_two, _) = weights
    (
        normed_one,
        inv_one,
        act_one,
        normed_two,
        inv_two,
        act_two,
        query_bf,
        key_bf,
        value_bf,
        log_total,
        attn_bf,
        up_rows,
        hidden_bf,
        allowed,
        cos_t,
        sin_t,
        seg_rows,
    ) = kept_state
    group_count, row_count = seg_rows.shape
    valid = (seg_rows >= 0).astype(jnp.float32).reshape(group_count * row_count, 1)
    grad_y = grad_rows.reshape(group_count * row_count, D) * valid
    grad_y_bf = grad_y.astype(jnp.bfloat16)
    grad_bias = jnp.sum(grad_y, axis=0)
    grad_w_down = jnp.dot(hidden_bf.T, grad_y_bf, preferred_element_type=jnp.float32)
    grad_w_out = jnp.dot(attn_bf.T, grad_y_bf, preferred_element_type=jnp.float32)
    grad_hidden = jnp.dot(grad_y_bf, w_down.T, preferred_element_type=jnp.float32)
    cdf_part = 0.5 * (1.0 + jax.scipy.special.erf(up_rows * 0.7071067811865476))
    pdf_part = jnp.exp(-0.5 * up_rows * up_rows) * 0.3989422804014327
    grad_up = grad_hidden * (cdf_part + up_rows * pdf_part)
    grad_b_up = jnp.sum(grad_up, axis=0)
    grad_up_bf = grad_up.astype(jnp.bfloat16)
    grad_w_up = jnp.dot(act_two.T, grad_up_bf, preferred_element_type=jnp.float32)
    grad_act_two = jnp.dot(grad_up_bf, w_up.T, preferred_element_type=jnp.float32)
    grad_attn = jnp.dot(grad_y_bf, w_out.T, preferred_element_type=jnp.float32).astype(jnp.bfloat16)
    grad_attn = grad_attn.reshape(group_count, row_count, HEADS, HEAD_DIM)
    prob_rows, _ = softmax_rows(query_bf, key_bf, allowed, log_total)
    prob_bf = prob_rows.astype(jnp.bfloat16)
    grad_value = product("ghqk,gqhd->gkhd", prob_bf, grad_attn)
    grad_prob = product("gqhd,gkhd->ghqk", grad_attn, value_bf)
    delta_rows = jnp.sum(prob_rows * grad_prob, axis=-1, keepdims=True)
    grad_score_bf = (prob_rows * (grad_prob - delta_rows) * HEAD_DIM ** (-0.5)).astype(jnp.bfloat16)
    grad_query = unrotate(product("ghqk,gkhd->gqhd", grad_score_bf, key_bf), cos_t, sin_t)
    grad_key = unrotate(product("ghqk,gqhd->gkhd", grad_score_bf, query_bf), cos_t, sin_t)
    grad_qkv = jnp.stack([grad_query, grad_key, grad_value], axis=2).reshape(
        group_count * row_count, 3 * D
    )
    grad_b_qkv = jnp.sum(grad_qkv, axis=0)
    grad_qkv_bf = grad_qkv.astype(jnp.bfloat16)
    grad_w_qkv = jnp.dot(act_one.T, grad_qkv_bf, preferred_element_type=jnp.float32)
    grad_act_one = jnp.dot(grad_qkv_bf, w_qkv.T, preferred_element_type=jnp.float32)
    grad_gain_one, grad_shift_one, back_one = norm_back(grad_act_one, normed_one, inv_one, gain_one)
    grad_gain_two, grad_shift_two, back_two = norm_back(grad_act_two, normed_two, inv_two, gain_two)
    input_grad = (grad_y + back_one + back_two).reshape(group_count, row_count, D)
    grads = (
        grad_w_qkv,
        grad_w_out,
        grad_w_up,
        grad_w_down,
        grad_b_qkv,
        grad_bias,
        grad_b_up,
        grad_bias,
        grad_gain_one,
        grad_shift_one,
        grad_gain_two,
        grad_shift_two,
    )
    return (input_grad, grads)


def adam_update(params, grads, first_moment, second_moment):
    new_first = BETA_ONE * first_moment + (1.0 - BETA_ONE) * grads
    new_second = BETA_TWO * second_moment + (1.0 - BETA_TWO) * grads * grads
    first_hat = new_first / (1.0 - BETA_ONE**STEP)
    second_hat = new_second / (1.0 - BETA_TWO**STEP)
    new_params = params - LEARN_RATE * (
        first_hat / (jnp.sqrt(second_hat) + ADAM_EPS) + WEIGHT_DECAY * params
    )
    return (new_params, new_first, new_second)


AXES = ("dp", "fsdp")
TAIL = 13 * D


def rows_from_flat(flat, spread, count):
    me = lax.axis_index(AXES)
    tail = flat[flat.shape[0] - TAIL :]
    before = lax.ppermute(tail, AXES, [(i, (i + 1) % count) for i in range(count)])
    joined = jnp.concatenate([before, flat])
    rows = lax.dynamic_slice(joined, (TAIL - spread * me,), (flat.shape[0] - spread,))
    return rows.reshape(-1, D), tail.reshape(-1, D)


def flat_from_rows(rows, tail, spread, count):
    me = lax.axis_index(AXES)
    head = rows.reshape(-1)[:TAIL]
    after = lax.ppermute(head, AXES, [(i, (i - 1) % count) for i in range(count)])
    after = jnp.where(me == count - 1, tail.reshape(-1), after)
    joined = jnp.concatenate([rows.reshape(-1), after])
    return lax.dynamic_slice(joined, (spread * me,), (rows.size + spread,))


def body(count, block_input, out_grad, seg_ids, params, first_moment, second_moment):
    spread = TAIL // count
    row_count = (params.shape[0] - spread) // D
    rows, tail = rows_from_flat(params.astype(jnp.bfloat16), spread, count)
    sent = jnp.concatenate([rows, jnp.pad(tail, ((0, 3), (0, 0)))])
    whole = lax.all_gather(sent, AXES, axis=0, tiled=False)
    matrices = whole[:, :row_count].reshape(-1)
    weights = unpack_flat(jnp.concatenate([matrices, whole[count - 1, row_count : row_count + 13].reshape(-1)]))
    result, kept_state = forward(block_input, seg_ids, weights)
    back_x, grads = backward(kept_state, out_grad, weights)
    big = jnp.concatenate([g.astype(jnp.bfloat16).reshape(-1, D) for g in grads[:4]])
    small = jnp.concatenate([g.astype(jnp.bfloat16).reshape(-1, D) for g in grads[4:]])
    small = jnp.pad(small, ((0, 3), (0, 0)))
    spots = jnp.where(jnp.arange(count)[:, None, None] == count - 1, small[None], jnp.zeros((), jnp.bfloat16))
    out = jnp.concatenate([big.reshape(count, row_count, D), spots], axis=1)
    owned = lax.psum_scatter(out, AXES, scatter_dimension=0, tiled=False).astype(jnp.float32)
    owned_grads = flat_from_rows(owned[:row_count], owned[row_count : row_count + 13], spread, count)
    new_params, new_first, new_second = adam_update(params, owned_grads, first_moment, second_moment)
    return (result, back_x, owned_grads, new_params, new_first, new_second)


BF = jnp.bfloat16
F32 = jnp.float32
PLANES = 4
PART = D // PLANES
SPOT = 96
SLAB = 352
EARLY = 80
STARTS = (0, 80, 176, 256)


def dot_nn(a, b):
    return lax.dot_general(a, b, (((1,), (0,)), ((), ())), preferred_element_type=F32)


def dot_nt(a, b):
    return lax.dot_general(a, b, (((1,), (1,)), ((), ())), preferred_element_type=F32)


def dot_tn(a, b):
    return lax.dot_general(a, b, (((0,), (0,)), ((), ())), preferred_element_type=F32)


def lanes_of(width):
    return lax.broadcasted_iota(jnp.int32, (1, width), 1)


def group_mask(index, width=D, size=PART):
    lane = lanes_of(width)
    return (lane >= index * size) & (lane < (index + 1) * size)


def turned(value, shift):
    shift = shift % value.shape[-1]
    return value if shift == 0 else pltpu.roll(value, shift, value.ndim - 1)


def spread_groups(parts, first):
    total = None
    for group, part in enumerate(parts):
        moved = turned(part, PART * (group - first))
        total = moved if total is None else jnp.where(group_mask(group), moved, total)
    if len(parts) < PLANES:
        total = jnp.where(lanes_of(D) < PART * len(parts), total, 0.0)
    return total


def count_of(value, *limits):
    return sum(jnp.where(value >= limit, 1, 0) for limit in limits)


def pick_matrix(kinds, size):
    row = lax.broadcasted_iota(jnp.int32, (SPOT, SPOT), 0)
    col = lax.broadcasted_iota(jnp.int32, (SPOT, SPOT), 1)
    kind = count_of(row, *range(size, SPOT, size))
    return jnp.where(col == kinds * (row - size * kind) + kind, 1.0, 0.0).astype(BF)


def order_columns(perm_ref, by_head):
    place = lax.broadcasted_iota(jnp.int32, (8, D), 1)
    part = count_of(place, PART, 2 * PART, 3 * PART)
    inner = place - PART * part
    if by_head:
        kind = count_of(inner, HEAD_DIM, 2 * HEAD_DIM)
        early = part + jnp.where(kind == 0, 0, jnp.where(kind == 1, 5, 9))
        late = jnp.where(kind == 0, 3, jnp.where(kind == 1, 4, 8))
        source = HEAD_DIM * (jnp.where(part < 3, early, late) - kind) + inner
    else:
        run = count_of(inner, *range(24, PART, 24))
        source = (SPOT - 24) * run + 24 * part + inner
    row = lax.broadcasted_iota(jnp.int32, (D, D), 0)
    perm_ref[...] = jnp.where(row == source[0:1], 1.0, 0.0).astype(BF)


def pack_kernel(where_ref, lines_ref, tail_ref, *refs):
    out_refs, (spot, perm, mixed, rows_ref) = refs[:PLANES], refs[PLANES:]
    for j in range(D // 128):
        rows_ref[:, 128 * j : 128 * j + 128] = lines_ref[
            pl.ds(j, rows_ref.shape[0], stride=D // 128), :
        ]
    plane, place = where_ref[0], where_ref[1]
    device = 8 * plane + place
    with_heads = device < 8
    with_hidden = (device >= 10) & (device < 22)
    spot[...] = jnp.zeros_like(spot)
    pl.when(with_heads)(lambda: order_columns(perm, True))
    pl.when(with_hidden)(lambda: order_columns(perm, False))

    @pl.when(with_heads | with_hidden)
    def _():
        mixed[...] = dot_nn(rows_ref[...].astype(BF), perm[...]).astype(BF)

    @pl.when(with_heads)
    def _():
        sort = pick_matrix(3, 32)
        for i in range(3):
            picked = dot_nn(sort, mixed[SPOT * i : SPOT * i + SPOT, :])
            for j in range(3):
                parts = [picked[32 * j + 8 * g : 32 * j + 8 * g + 8] for g in range(4)]
                for s in range(PLANES):
                    spot[s, 24 * i + 8 * j : 24 * i + 8 * j + 8, :] = spread_groups(parts, s)

    for i in range(3):
        block = 3 * device + i

        @pl.when((block >= 32) & (block < 64))
        def _():
            picked = dot_nn(pick_matrix(4, 24), mixed[SPOT * i : SPOT * i + SPOT, :])
            parts = [picked[24 * j : 24 * j + 24] for j in range(4)]
            start = 24 * i
            if i == 2:
                start = pl.multiple_of(jnp.where(block == 32, 0, 48), 8)
            for s in range(PLANES):
                spot[s, pl.ds(start, 24), :] = spread_groups(parts, s)

        @pl.when(block >= 64)
        def _():
            for s in range(PLANES):
                spot[s, 24 * i : 24 * i + 24, :] = rows_ref[
                    SPOT * i + 24 * s : SPOT * i + 24 * s + 24, :
                ]

    @pl.when(device == 8)
    def _():
        for s in range(3):
            spot[s, 0:64, :] = rows_ref[64 * s : 64 * s + 64, :]
        spot[3, 0:96, :] = rows_ref[192:288, :]

    @pl.when(device == 9)
    def _():
        for s in range(3):
            spot[s, 0:64, :] = rows_ref[32 + 64 * s : 96 + 64 * s, :]
        spot[3, 0:32, :] = rows_ref[0:32, :]
        spot[3, 32:96, :] = rows_ref[224:288, :]

    @pl.when(device == 10)
    def _():
        for s in range(3):
            spot[s, 24:88, :] = rows_ref[64 * s : 64 * s + 64, :]

    @pl.when(device == 31)
    def _():
        upper = tail_ref[0:8, :].astype(BF)
        order_columns(perm, True)
        by_head = dot_nn(upper, perm[...])
        order_columns(perm, False)
        by_hidden = dot_nn(upper, perm[...])
        for s in range(PLANES):
            spot[s, 80:81, :] = spread_groups([by_hidden[4 + j : 5 + j] for j in range(4)], s)
            spot[s, 81:82, :] = spread_groups([by_head[j : j + 1] for j in range(3)], s)
            spot[s, 82:83, :] = tail_ref[3:4, :]
            spot[s, 88:96, :] = tail_ref[8:16, :]

    for r in range(PLANES):
        out_refs[r][...] = spot[plane ^ r].astype(BF)


def unpack_kernel(where_ref, *refs):
    in_refs, (lines_ref, tail_ref, spot, perm, mixed, rows_ref) = refs[:PLANES], refs[PLANES:]
    plane, place = where_ref[0], where_ref[1]
    device = 8 * plane + place
    with_heads = device < 8
    with_hidden = (device >= 10) & (device < 22)
    for r in range(PLANES):
        spot[plane ^ r] = in_refs[r][...].astype(F32)
    pl.when(with_heads)(lambda: order_columns(perm, True))

    @pl.when(with_heads)
    def _():
        sort = pick_matrix(3, 32)
        for i in range(3):
            sorted_ = []
            for j in range(3):
                base = 24 * i + 8 * j
                parts = [spot[s, base : base + 8, :] for s in range(PLANES)]
                sorted_.extend(spread_groups(parts, g) for g in range(4))
            block_rows = jnp.concatenate(sorted_, axis=0).astype(BF)
            mixed[SPOT * i : SPOT * i + SPOT, :] = dot_tn(sort, block_rows).astype(BF)

    @pl.when(with_hidden)
    def _():
        order_columns(perm, False)
        mixed[...] = jnp.zeros_like(mixed)

    for i in range(3):
        block = 3 * device + i

        @pl.when((block >= 32) & (block < 64))
        def _():
            start = 24 * i
            if i == 2:
                start = pl.multiple_of(jnp.where(block == 32, 0, 48), 8)
            parts = [spot[s, pl.ds(start, 24), :] for s in range(PLANES)]
            block_rows = jnp.concatenate([spread_groups(parts, j) for j in range(4)], axis=0)
            mixed[SPOT * i : SPOT * i + SPOT, :] = dot_tn(
                pick_matrix(4, 24), block_rows.astype(BF)
            ).astype(BF)

    @pl.when(with_heads | with_hidden)
    def _():
        rows_ref[...] = dot_nt(mixed[...], perm[...])

    for i in range(3):

        @pl.when(3 * device + i >= 64)
        def _():
            for s in range(PLANES):
                rows_ref[SPOT * i + 24 * s : SPOT * i + 24 * s + 24, :] = spot[
                    s, 24 * i : 24 * i + 24, :
                ]

    @pl.when(device == 8)
    def _():
        for s in range(3):
            rows_ref[64 * s : 64 * s + 64, :] = spot[s, 0:64, :]
        rows_ref[192:288, :] = spot[3, 0:96, :]

    @pl.when(device == 9)
    def _():
        for s in range(3):
            rows_ref[32 + 64 * s : 96 + 64 * s, :] = spot[s, 0:64, :]
        rows_ref[0:32, :] = spot[3, 0:32, :]
        rows_ref[224:288, :] = spot[3, 32:96, :]

    @pl.when(device == 10)
    def _():
        for s in range(3):
            rows_ref[64 * s : 64 * s + 64, :] = spot[s, 24:88, :]

    for j in range(D // 128):
        lines_ref[pl.ds(j, rows_ref.shape[0], stride=D // 128), :] = rows_ref[
            :, 128 * j : 128 * j + 128
        ]
    tail_ref[...] = jnp.zeros_like(tail_ref)

    @pl.when(device == 31)
    def _():
        order_columns(perm, False)
        whole = [spot[s, 80:81, :] for s in range(PLANES)]
        for j in range(4):
            row = jnp.broadcast_to(spread_groups(whole, j), (8, D)).astype(BF)
            tail_ref[4 + j : 5 + j, :] = dot_nt(row, perm[...])[0:1]
        order_columns(perm, True)
        whole = [spot[s, 81:82, :] for s in range(PLANES)]
        for j in range(3):
            row = jnp.broadcast_to(spread_groups(whole, j), (8, D)).astype(BF)
            tail_ref[j : j + 1, :] = dot_nt(row, perm[...])[0:1]
        tail_ref[3:4, :] = sum(spot[s, 82:83, :] for s in range(PLANES))
        tail_ref[8:16, :] = sum(spot[s, 88:96, :] for s in range(PLANES))


def slab_start(plane):
    start = jnp.where(plane == 1, STARTS[1], jnp.where(plane == 2, STARTS[2], STARTS[3]))
    return pl.multiple_of(jnp.where(plane == 0, 0, start), 16)


def slab_kernel(where_ref, *refs):
    in_refs, (first, second) = refs[:PLANES], refs[PLANES:]
    for r, ref in enumerate(in_refs):
        source = where_ref[0] ^ r

        @pl.when(source == 0)
        def _():
            first[0:80, :] = ref[0:80, :]

        @pl.when(source == 1)
        def _():
            first[80:176, :] = ref[...]

        @pl.when(source == 2)
        def _():
            second[0:80, :] = ref[0:80, :]

        @pl.when(source == 3)
        def _():
            second[80:160, :] = ref[0:80, :]
            first[176:192, :] = ref[80:96, :]


def split_kernel(where_ref, *refs):
    early, late, out_refs, total = refs[:4], refs[4:8], refs[8:12], refs[12]

    def sum_of(parts):
        a, b, c, d = (part[...].astype(F32) for part in parts)
        return (a + b) + (c + d)

    total[0:EARLY, :] = sum_of(early)
    total[EARLY:SLAB, :] = sum_of(late)
    for r in range(PLANES):
        out_refs[r][...] = total[pl.ds(slab_start(where_ref[0] ^ r), SPOT), :].astype(BF)


def norm_kernel(seg_ref, x_ref, g_ref, act_ref, cot_ref, normed_ref, g_y_ref, inv_ref, segs):
    micro, row_count = seg_ref.shape
    segs[...] = jnp.zeros_like(segs)
    segs[0:micro, 0:row_count] = seg_ref[...].astype(F32)
    x = x_ref[...]
    centred = x - jnp.mean(x, axis=1, keepdims=True)
    inv = lax.rsqrt(jnp.mean(centred * centred, axis=1, keepdims=True) + NORM_EPS)
    normed = centred * inv
    normed_ref[...] = normed
    inv_ref[...] = jnp.broadcast_to(inv, inv_ref.shape)
    tokens = micro * row_count
    act_ref[0:tokens, :] = normed.astype(BF)
    act_ref[tokens:, :] = jnp.zeros((16, D), BF)
    act_ref[tokens:, 0:128] = segs[...].astype(BF)
    rows = lax.broadcasted_iota(jnp.int32, (row_count, 128), 0)
    cols = lax.broadcasted_iota(jnp.int32, (row_count, 128), 1)
    for m in range(micro):
        own = jnp.where(rows == cols, jnp.broadcast_to(segs[m : m + 1, :], rows.shape), 0.0)
        valid = jnp.sum(own, axis=1, keepdims=True) >= 0.0
        span = slice(row_count * m, row_count * (m + 1))
        g_y = jnp.where(valid, g_ref[span, :], 0.0)
        g_y_ref[span, :] = g_y
        cot_ref[span, :] = g_y.astype(BF)


def place_of(index, spot, core):
    return 2 * (spot ^ (index % 4)) + (core if index < 4 else 1 - core)


def row_sum(x):
    return jnp.sum(x, axis=0, keepdims=True)


def attention_kernel(where_ref, *refs):
    act_refs, cot_refs, slab_refs, grad_refs = refs[:4], refs[4:8], refs[8:16], refs[16:24]
    (y_ref, dn_ref, g_out_ref, up_low, tails, g_tails, normed, grad_y,
     w_out, packed, w_qkv, bf_out, bf_qkv, qkv, attn, g_qkv, g_attn) = refs[24:]
    plane, spot, core = where_ref[0], where_ref[1], where_ref[2]
    lane = lanes_of(D)

    w_out[...] = jnp.zeros_like(w_out)
    for index, ref in enumerate(slab_refs):
        q = place_of(index, spot, core)
        for i in range(3):
            for j in range(3):
                packed[j, pl.ds(pl.multiple_of(24 * q + 8 * i, 8), 8), :] = ref[0:80, :][
                    24 * i + 8 * j : 24 * i + 8 * j + 8
                ].astype(F32)
        one = ref[80:176, :].astype(F32)

        @pl.when(q >= 3)
        def _():
            up_low[pl.ds(pl.multiple_of(72 * q - 192, 8), 72), :] = one[0:72]

        @pl.when(q == 2)
        def _():
            up_low[0:24, :] = one[0:24]

            @pl.when(plane < 3)
            def _():
                w_out[128:192, :] = one[24:88]

        @pl.when((q < 2) & (plane < 3))
        def _():
            w_out[pl.ds(pl.multiple_of(64 * q, 8), 64), :] = one[0:64]

        @pl.when((q < 2) & (plane == 3))
        def _():
            w_out[pl.ds(pl.multiple_of(96 * q, 8), 96), :] = one[0:96]

        @pl.when(q == 7)
        def _():
            tails[...] = ref[176:192, :].astype(F32)

    for j in range(3):
        for i in range(4):
            moved = turned(packed[j], -PART * i)[:, 0:256]
            moved = jnp.where(lanes_of(256) < PART, moved, 0.0)
            w_qkv[:, i, :, 256 * j : 256 * j + 256] = moved.reshape(24, 8, 256)
    bf_out[...] = w_out[...].astype(BF)
    bf_qkv[...] = w_qkv[...].reshape(D, D).astype(BF)

    for r in range(4):
        normed[128 * r : 128 * r + 128, :] = act_refs[r][0:128, :]
        grad_y[128 * r : 128 * r + 128, :] = cot_refs[r][...]
    flat_bias = tails[1:2, :]
    bias_qkv = jnp.zeros((1, D), F32)
    for j in range(3):
        keep = (lane >= 256 * j) & (lane < 256 * j + PART)
        bias_qkv = jnp.where(keep, turned(flat_bias, 64 * j), bias_qkv)
    bias_y = jnp.where(plane == 0, tails[2:3, :] + tails[8:9, :], 0.0)
    gain_one, shift_one = tails[9:10, :], tails[10:11, :]
    wide = normed[...].astype(F32)
    act_one = (wide * gain_one + shift_one).astype(BF)
    qkv[...] = dot_nn(act_one, bf_qkv[...]) + bias_qkv
    g_attn[...] = dot_nt(grad_y[...], bf_out[...]).astype(BF)

    rows = lax.broadcasted_iota(jnp.int32, (128, 128), 0)
    cols = lax.broadcasted_iota(jnp.int32, (128, 128), 1)
    same_block = (rows < 64) == (cols < 64)
    eye = rows == cols
    in_head = lanes_of(128) % 64
    freq = jnp.exp((in_head % 8).astype(F32) * (-2.0 * math.log(10000.0) / ROT))
    low_half = lanes_of(128) < 64
    for r in range(4):
        span = slice(128 * r, 128 * r + 128)
        ids = act_refs[r][128:144, 0:128].astype(F32)
        ids = jnp.where(low_half, ids[0:1], turned(ids[1:2], 64))
        seg_row = jnp.broadcast_to(ids, (128, 128))
        seg_col = jnp.sum(jnp.where(eye, seg_row, 0.0), axis=1, keepdims=True)
        same = (seg_col == seg_row) & same_block
        allowed = same & (cols <= rows) & ((seg_col >= 0.0) | eye)
        position = jnp.sum(jnp.where(same & (cols < rows), 1.0, 0.0), axis=1, keepdims=True)
        angle = position * freq
        cos_t = jnp.where(in_head < ROT, jnp.cos(angle), 1.0)
        sine = jnp.sin(angle)
        sin_a = jnp.where(in_head < 8, sine, 0.0)
        sin_b = jnp.where((in_head >= 8) & (in_head < ROT), sine, 0.0)

        def rotated(x):
            return x * cos_t - turned(x, -8) * sin_a + turned(x, 8) * sin_b

        def unrotated(x):
            return x * cos_t + turned(x, -8) * sin_a - turned(x, 8) * sin_b

        for tile in range(2):
            at = [256 * j + 128 * tile for j in range(3)]
            query = rotated(qkv[span, at[0] : at[0] + 128]).astype(BF)
            key = rotated(qkv[span, at[1] : at[1] + 128]).astype(BF)
            value = qkv[span, at[2] : at[2] + 128].astype(BF)
            g_out = g_attn[span, 128 * tile : 128 * tile + 128]
            parts = []
            for half in range(2 - tile):
                mask = low_half if half == 0 else jnp.logical_not(low_half)
                key_h = jnp.where(mask, key, jnp.zeros_like(key))
                value_h = jnp.where(mask, value, jnp.zeros_like(value))
                scores = dot_nt(query, key_h) * HEAD_DIM ** (-0.5)
                masked = jnp.where(allowed, scores, -1e30)
                top = jnp.max(masked, axis=1, keepdims=True)
                expo = jnp.where(allowed, jnp.exp(masked - top), 0.0)
                prob = expo * (1.0 / jnp.sum(expo, axis=1, keepdims=True))
                prob_bf = prob.astype(BF)
                g_prob = dot_nt(g_out, value_h)
                delta = jnp.sum(prob * g_prob, axis=1, keepdims=True)
                g_score = (prob * (g_prob - delta) * HEAD_DIM ** (-0.5)).astype(BF)
                parts.append(
                    (
                        dot_nn(prob_bf, value),
                        dot_tn(prob_bf, g_out),
                        dot_nn(g_score, key),
                        dot_tn(g_score, query),
                    )
                )
            if tile == 0:
                o, gv, gq, gk = [jnp.where(low_half, a, b) for a, b in zip(*parts)]
            else:
                o, gv, gq, gk = [jnp.where(low_half, a, 0.0) for a in parts[0]]
            attn[span, 128 * tile : 128 * tile + 128] = o.astype(BF)
            g_qkv[span, at[0] : at[0] + 128] = unrotated(gq)
            g_qkv[span, at[1] : at[1] + 128] = unrotated(gk)
            g_qkv[span, at[2] : at[2] + 128] = gv
    y_ref[...] = dot_nn(attn[...], bf_out[...]) + bias_y
    g_out_ref[...] = dot_tn(attn[...], grad_y[...])
    g_bias_qkv = jnp.sum(g_qkv[...], axis=0, keepdims=True)
    g_qkv_bf = g_qkv[...].astype(BF)
    w_qkv[...] = dot_tn(act_one, g_qkv_bf).reshape(24, 4, 8, D)
    g_act_one = dot_nt(g_qkv_bf, bf_qkv[...])
    dn_ref[...] = g_act_one * gain_one
    flat_bias = jnp.zeros((1, D), F32)
    for j in range(3):
        keep = (lane >= PART * j) & (lane < PART * (j + 1))
        flat_bias = jnp.where(keep, turned(g_bias_qkv, -64 * j), flat_bias)
    g_bias_y = row_sum(grad_y[0:128, :].astype(F32))
    g_tails[...] = jnp.zeros_like(g_tails)
    g_tails[1:2, :] = flat_bias
    g_tails[2:3, :] = g_bias_y
    g_tails[8:9, :] = g_bias_y
    g_tails[9:10, :] = row_sum(g_act_one * wide)
    g_tails[10:11, :] = row_sum(g_act_one)
    for j in range(3):
        total = None
        for i in range(4):
            piece = w_qkv[:, i, :, 256 * j : 256 * j + 256].reshape(PART, 256)
            piece = jnp.where(lanes_of(256) < PART, piece, 0.0)
            piece = jnp.concatenate([piece, jnp.zeros((PART, 512), F32)], axis=1)
            piece = turned(piece, PART * i)
            total = piece if total is None else total + piece
        packed[j] = total
    for index, ref in enumerate(grad_refs):
        q = place_of(index, spot, core)
        pieces = [
            packed[j, pl.ds(pl.multiple_of(24 * q + 8 * i, 8), 8), :]
            for i in range(3)
            for j in range(3)
        ]
        pieces.append(jnp.zeros((8, D), F32))
        ref[...] = jnp.concatenate(pieces, axis=0).astype(BF)


def feed_forward_kernel(where_ref, *refs):
    (y_ref, dn_ref, g_out_ref, up_low, tails, g_tails, normed, grad_y) = refs[:8]
    slab_refs, grad_refs, back_refs = refs[8:16], refs[16:24], refs[24:28]
    w_up, w_down, bf_up, bf_down, up, slab = refs[28:]
    plane, spot, core = where_ref[0], where_ref[1], where_ref[2]
    w_up[0:384, :] = up_low[...]
    for index, ref in enumerate(slab_refs):
        q = place_of(index, spot, core)
        two = ref[0:80, :].astype(F32)
        three = ref[80:160, :].astype(F32)

        @pl.when(q < 5)
        def _():
            w_up[pl.ds(pl.multiple_of(384 + 72 * q, 8), 72), :] = two[0:72]

        @pl.when(q == 5)
        def _():
            w_up[744:768, :] = two[0:24]
            w_down[0:48, :] = two[24:72]

        @pl.when(q > 5)
        def _():
            w_down[pl.ds(pl.multiple_of(72 * q - 384, 8), 72), :] = two[0:72]

        w_down[pl.ds(pl.multiple_of(192 + 72 * q, 8), 72), :] = three[0:72]

    bf_up[...] = w_up[...].astype(BF)
    bf_down[...] = w_down[...].astype(BF)
    bias_up = tails[0:1, :]
    gain_two, shift_two = tails[11:12, :], tails[12:13, :]
    wide = normed[...].astype(F32)
    act_two = (wide * gain_two + shift_two).astype(BF)
    up[...] = dot_nn(act_two, bf_up[...]) + bias_up
    cdf = 0.5 * (1.0 + lax.erf(up[...] * 0.7071067811865476))
    hidden = (up[...] * cdf).astype(BF)
    y = y_ref[...] + dot_nn(hidden, bf_down[...])
    for r in range(4):
        back_refs[r][0:128, :] = y[128 * r : 128 * r + 128].astype(BF)
    w_down[...] = dot_tn(hidden, grad_y[...])
    pdf = jnp.exp(-0.5 * up[...] * up[...]) * 0.3989422804014327
    g_up = dot_nt(grad_y[...], bf_down[...]) * (cdf + up[...] * pdf)
    g_bias_up = row_sum(g_up)
    g_up_bf = g_up.astype(BF)
    w_up[...] = dot_tn(act_two, g_up_bf)
    g_act_two = dot_nt(g_up_bf, bf_up[...])
    dn = dn_ref[...] + g_act_two * gain_two
    for r in range(4):
        back_refs[r][128:256, :] = dn[128 * r : 128 * r + 128].astype(BF)
    slab[256:272, :] = g_tails[...]
    slab[256:257, :] = g_bias_up
    slab[267:268, :] = row_sum(g_act_two * wide)
    slab[268:269, :] = row_sum(g_act_two)
    for index, ref in enumerate(grad_refs):
        q = place_of(index, spot, core)

        @pl.when(q >= 3)
        def _():
            slab[0:72, :] = w_up[pl.ds(pl.multiple_of(72 * q - 192, 8), 72), :]

        @pl.when(q == 2)
        def _():
            slab[0:24, :] = w_up[0:24, :]
            slab[24:88, :] = g_out_ref[128:192, :]

        @pl.when((q < 2) & (plane < 3))
        def _():
            slab[0:64, :] = g_out_ref[pl.ds(pl.multiple_of(64 * q, 8), 64), :]

        @pl.when((q < 2) & (plane == 3))
        def _():
            slab[0:96, :] = g_out_ref[pl.ds(pl.multiple_of(96 * q, 8), 96), :]

        @pl.when(q < 5)
        def _():
            slab[96:168, :] = w_up[pl.ds(pl.multiple_of(384 + 72 * q, 8), 72), :]

        @pl.when(q == 5)
        def _():
            slab[96:120, :] = w_up[744:768, :]
            slab[120:168, :] = w_down[0:48, :]

        @pl.when(q > 5)
        def _():
            slab[96:168, :] = w_down[pl.ds(pl.multiple_of(72 * q - 384, 8), 72), :]

        slab[176:248, :] = w_down[pl.ds(pl.multiple_of(192 + 72 * q, 8), 72), :]
        ref[...] = slab[...].astype(BF)


def local_call(kernel, outs, scratch, limit, kept_out, where, *operands):
    vmem = pl.BlockSpec(memory_space=pltpu.VMEM)
    operands = [pltpu.with_memory_space_constraint(x, pltpu.VMEM) for x in operands]
    out_specs = jax.tree.map(lambda _: vmem, outs)
    if kept_out:
        outs = jax.tree.map(lambda x: pltpu.VMEM(x.shape, x.dtype), outs)
    return pl.pallas_call(
        kernel,
        out_shape=outs,
        in_specs=[pl.BlockSpec(memory_space=pltpu.SMEM)] + [vmem] * len(operands),
        out_specs=out_specs,
        scratch_shapes=scratch,
        compiler_params=pltpu.CompilerParams(vmem_limit_bytes=limit << 20),
    )(where, *operands)


def sliced_step(planes, places, *args):
    return sliced_body(planes, places, *args)


def sliced_body(planes, places, block_input, out_grad, seg_ids, params, first_moment, second_moment):
    count = planes * places * 2
    spread = TAIL // count
    dp, core = lax.axis_index("dp"), lax.axis_index("fsdp")
    plane, spot = dp // places, dp % places
    where_owner = jnp.stack([plane, 2 * spot + core]).astype(jnp.int32)
    where_spot = jnp.stack([plane, spot, core]).astype(jnp.int32)
    across = [
        [(i, (i // places ^ r) * places + i % places) for i in range(planes * places)]
        for r in range(planes)
    ]
    within = [
        [(i, i // places * places + (i % places ^ r)) for i in range(planes * places)]
        for r in range(places)
    ]

    def to_plane(value, r):
        return lax.ppermute(value, "dp", across[r]) if r else value

    def to_spot(value, r):
        return lax.ppermute(value, "dp", within[r]) if r else value

    def to_core(value):
        return lax.ppermute(value, "fsdp", [(0, 1), (1, 0)])

    micro, row_count, _ = block_input.shape
    tokens = micro * row_count
    flat_x = block_input.reshape(tokens, D)
    vmem = pl.BlockSpec(memory_space=pltpu.VMEM)
    sent_acts, sent_cots, normed, grad_y, inv_std = pl.pallas_call(
        norm_kernel,
        out_shape=[
            pltpu.VMEM((tokens + 16, D), BF),
            pltpu.VMEM((tokens, D), BF),
            jax.ShapeDtypeStruct((tokens, D), F32),
            jax.ShapeDtypeStruct((tokens, D), F32),
            jax.ShapeDtypeStruct((tokens, 128), F32),
        ],
        in_specs=[vmem] * 3,
        out_specs=[vmem] * 5,
        scratch_shapes=[pltpu.VMEM((16, 128), F32)],
        compiler_params=pltpu.CompilerParams(vmem_limit_bytes=8 << 20),
        name="norm",
    )(
        *(
            pltpu.with_memory_space_constraint(x, pltpu.HBM)
            for x in (seg_ids, flat_x, out_grad.reshape(tokens, D))
        )
    )
    inv_std = inv_std[:, 0:1]
    acts = [to_plane(sent_acts, r) for r in range(3)]
    acts.append(to_plane(acts[2], 1))
    cots = [to_plane(sent_cots, r) for r in range(3)]
    cots.append(to_plane(cots[2], 1))

    rows, tail = rows_from_flat(params, spread, count)
    tail = jnp.pad(tail, ((0, 3), (0, 0)))
    spot_shape = jax.ShapeDtypeStruct((SPOT, D), BF)

    def shaped(rows, kind=BF):
        return jax.ShapeDtypeStruct((rows, D), kind)

    sort_scratch = [
        pltpu.VMEM((planes, SPOT, D), F32),
        pltpu.VMEM((D, D), BF),
        pltpu.VMEM(rows.shape, BF),
        pltpu.VMEM(rows.shape, F32),
    ]
    spots = local_call(
        pack_kernel, [spot_shape] * planes, sort_scratch, 10, True,
        where_owner, rows.reshape(-1, 128), tail,
    )
    spots = [to_plane(spots[r], r) for r in range(planes)]
    first, second = local_call(
        slab_kernel, [shaped(192), shaped(160)], [], 8, True, where_owner, *spots
    )
    firsts = [to_spot(first, r) for r in range(places)]
    seconds = [to_spot(second, r) for r in range(places)]
    firsts = firsts + [to_core(x) for x in firsts]
    total = planes * tokens
    outs = local_call(
        attention_kernel,
        [shaped(EARLY)] * 8
        + [
            shaped(total, F32),
            shaped(total, F32),
            shaped(256, F32),
            shaped(384, F32),
            shaped(16, F32),
            shaped(16, F32),
            shaped(total),
            shaped(total),
        ],
        [
            pltpu.VMEM((256, D), F32),
            pltpu.VMEM((3, PART, D), F32),
            pltpu.VMEM((24, 4, 8, D), F32),
            pltpu.VMEM((256, D), BF),
            pltpu.VMEM((D, D), BF),
            pltpu.VMEM((total, D), F32),
            pltpu.VMEM((total, 256), BF),
            pltpu.VMEM((total, D), F32),
            pltpu.VMEM((total, 256), BF),
        ],
        28, True, where_spot, *acts, *cots, *firsts,
    )
    early, kept = outs[:8], outs[8:]

    def summed(parts):
        paired = [
            (parts[r].astype(F32) + to_core(parts[4 + r]).astype(F32)).astype(BF)
            for r in range(places)
        ]
        return [to_spot(paired[r], r) for r in range(places)]

    early = summed(early)
    seconds = seconds + [to_core(x) for x in seconds]
    outs = local_call(
        feed_forward_kernel,
        [shaped(SLAB - EARLY)] * 8 + [shaped(2 * tokens)] * planes,
        [
            pltpu.VMEM((D, D), F32),
            pltpu.VMEM((D, D), F32),
            pltpu.VMEM((D, D), BF),
            pltpu.VMEM((D, D), BF),
            pltpu.VMEM((total, D), F32),
            pltpu.VMEM((SLAB - EARLY, D), F32),
        ],
        28, True, where_spot, *kept, *seconds,
    )
    late, backs = summed(outs[:8]), outs[8:]
    passed = to_plane(backs[3], 1)
    backs = [
        backs[0],
        to_plane(backs[1], 1),
        to_plane((backs[2].astype(F32) + passed.astype(F32)).astype(BF), 2),
    ]
    spots = local_call(
        split_kernel, [spot_shape] * planes, [pltpu.VMEM((SLAB, D), F32)], 12, True, where_owner, *early, *late
    )
    spots = [to_plane(spots[r], r) for r in range(planes)]
    grad_rows, grad_tail = local_call(
        unpack_kernel,
        [
            jax.ShapeDtypeStruct((rows.size // 128, 128), F32),
            jax.ShapeDtypeStruct((16, D), F32),
        ],
        sort_scratch, 12, True,
        where_owner, *spots,
    )
    back = sum(b.astype(F32) for b in backs)
    result = flat_x + back[:tokens]
    scaled = back[tokens:]
    input_grad = grad_y + inv_std * (
        scaled
        - jnp.mean(scaled, axis=-1, keepdims=True)
        - normed * jnp.mean(scaled * normed, axis=-1, keepdims=True)
    )
    owned = flat_from_rows(grad_rows, grad_tail[:13], spread, count)
    new_params, new_first, new_second = adam_update(params, owned, first_moment, second_moment)
    return (
        result.reshape(block_input.shape),
        input_grad.reshape(block_input.shape),
        owned,
        new_params,
        new_first,
        new_second,
    )


def solution(mesh):
    vector, tokens = P(AXES), P(None, AXES, None)
    dp, cores = mesh.shape["dp"], mesh.shape["fsdp"]
    if dp == PLANES * PLANES and cores == 2:
        step = functools.partial(sliced_step, PLANES, dp // PLANES)
    else:
        step = functools.partial(body, dp * cores)
    return jax.shard_map(
        step,
        mesh=mesh,
        in_specs=(tokens, tokens, P(None, AXES), vector, vector, vector),
        out_specs=(tokens, tokens, vector, vector, vector, vector),
        check_vma=False,
    )
```
